256 devices in a mesh: gx: 32 (over x, z), gy: 8 (over y, core).
Axes of the slice: x: 4, y: 4, z: 8, core: 2. Of those that a mesh axis runs over, the one named last changes fastest.
Arguments:
- depth: float32 [4096, 4096], P('gx', 'gy'), may hold values from 0.3 to 1.2
- momentum_x: float32 [4096, 4096], P('gx', 'gy'), may hold values from -3 to 3
- momentum_y: float32 [4096, 4096], P('gx', 'gy'), may hold values from -3 to 3
- bed: float32 [4096, 4096], P('gx', 'gy'), may hold values from -1 to 1
- wet: int32 [4096, 4096], P('gx', 'gy'), may hold values 0 or 1
Outputs:
- new_depth: float32 [4096, 4096], P('gx', 'gy')
- velocity_x: float32 [4096, 4096], P('gx', 'gy')
- velocity_y: float32 [4096, 4096], P('gx', 'gy')
The draws below stay inside these ranges and needn't reach their ends.
All inputs are finite; a program needn't handle non-finite values. No bound on the sum of `wet` on one device may be relied on, other than what follows from the above.
Results may differ from the reference program's by a relative error of at most 0.0013.
Values sent between devices are 32-bit elements; how exact they have to be, the bound alone decides.
A program may use at most 64 MiB of HBM per device.

```python
import jax
import jax.numpy as jnp
from jax import lax

CY = 512
NX = 4096
NY = 4096
N_GY = 8


def set_ends(values, rng, smallest, top_value):
    dims = values.shape
    place = [jax.random.randint(jax.random.fold_in(rng, axis), (), 0, dims[axis]) for axis in range(len(dims))]
    values = values.at[tuple(place)].set(smallest)
    longest = dims.index(max(dims))
    place[longest] = (place[longest] + 1) % dims[longest]
    return values.at[tuple(place)].set(top_value)


def shard_levels(key, extent, pieces, smallest, largest):
    level, own = 1.0, jax.random.fold_in(key, 6)
    for dim, parts in pieces:
        heights = jnp.exp(jax.random.uniform(jax.random.fold_in(own, dim), (parts,), jnp.float32, smallest / len(pieces), largest / len(pieces)))
        level = level * jnp.repeat(heights, extent[dim] // parts).reshape([-1 if axis == dim else 1 for axis in range(len(extent))])
    return level


def noise(key, dims, scale, bound, pieces=(), kind=jnp.bfloat16):
    drawn = scale * jax.random.normal(key, dims, jnp.float32)
    if pieces:
        drawn = drawn * shard_levels(key, dims, pieces, -0.22, 0.18)
    return jnp.clip(drawn, -bound, bound).astype(kind)


def setup_inputs(seed: int = 0) -> dict:
    arg_keys = jax.random.split(jax.random.key(seed), 6)
    return {
        "depth": jnp.clip(0.3 + 0.90000004 * jax.random.uniform(arg_keys[0], (NX, NY), jnp.float32) ** shard_levels(arg_keys[0], (NX, NY), ((0, 32), (1, 8)), -0.2, 0.2), 0.3, 1.2),
        "momentum_x": noise(arg_keys[1], (NX, NY), 0.5, 3.0, ((0, 32), (1, 8)), jnp.float32),
        "momentum_y": noise(arg_keys[2], (NX, NY), 0.5, 3.0, ((0, 32), (1, 8)), jnp.float32),
        "bed": jnp.clip(jax.random.uniform(arg_keys[3], (NX, NY), jnp.float32, -1.0, 1.0) * shard_levels(arg_keys[3], (NX, NY), ((0, 32), (1, 8)), -0.4, 0.0), -1.0, 1.0),
        "wet": set_ends((jax.random.randint(arg_keys[4], (NX, NY), 0, 8) < 7).astype(jnp.int32), jax.random.fold_in(arg_keys[4], 1), 0, 1),
    }


gravity = 9.81
ratio_x = 0.05
ratio_y = 0.05

def minmod(left, right):
    return 0.5 * (jnp.sign(left) + jnp.sign(right)) * jnp.minimum(jnp.abs(left), jnp.abs(right))

def window(values, start, stop, line_axis):
    return lax.slice_in_dim(values, start, stop, axis=line_axis)

def physical(height, normal, across):
    speed_n = normal / height
    fluxes = (normal, normal * speed_n + 0.5 * gravity * height * height, across * speed_n)
    return (fluxes, jnp.abs(speed_n) + jnp.sqrt(gravity * height))

def face_terms(depth, normal, across, wet_cells, line_axis):
    length = depth.shape[line_axis]
    states = (depth, normal, across)
    slopes = [minmod(window(field, 1, length - 1, line_axis) - window(field, 0, length - 2, line_axis), window(field, 2, length, line_axis) - window(field, 1, length - 1, line_axis)) for field in states]
    lefts = [window(field, 1, length - 2, line_axis) + 0.5 * window(slope, 0, length - 3, line_axis) for field, slope in zip(states, slopes)]
    rights = [window(field, 2, length - 1, line_axis) - 0.5 * window(slope, 1, length - 2, line_axis) for field, slope in zip(states, slopes)]
    opened = window(wet_cells, 1, length - 2, line_axis) * window(wet_cells, 2, length - 1, line_axis)
    safe_left = jnp.where(opened > 0.5, lefts[0], 1.0)
    safe_right = jnp.where(opened > 0.5, rights[0], 1.0)
    flux_left, speed_left = physical(safe_left, lefts[1], lefts[2])
    flux_right, speed_right = physical(safe_right, rights[1], rights[2])
    fastest = jnp.maximum(speed_left, speed_right)
    result = []
    for flux_a, flux_b, state_a, state_b in zip(flux_left, flux_right, lefts, rights):
        face = opened * (0.5 * (flux_a + flux_b) - 0.5 * fastest * (state_b - state_a))
        count = face.shape[line_axis]
        result.append(window(face, 1, count, line_axis) - window(face, 0, count - 1, line_axis))
    return result

def predict(padded):
    along_x = padded[:, :, 2:-2]
    along_y = padded[:, 2:-2, :]
    center = padded[:, 2:-2, 2:-2]
    depth, flow_x, flow_y, wet_cells = (center[0], center[1], center[2], center[4])
    mass_x, normal_x, shear_x = face_terms(along_x[0], along_x[1], along_x[2], along_x[4], 0)
    mass_y, normal_y, shear_y = face_terms(along_y[0], along_y[2], along_y[1], along_y[4], 1)
    bed_x = 0.5 * (along_x[3, 3:-1] - along_x[3, 1:-3])
    bed_y = 0.5 * (along_y[3, :, 3:-1] - along_y[3, :, 1:-3])
    new_depth = depth - wet_cells * (ratio_x * mass_x + ratio_y * mass_y)
    push_x = wet_cells * (flow_x - ratio_x * normal_x - ratio_y * shear_y - ratio_x * gravity * depth * bed_x)
    push_y = wet_cells * (flow_y - ratio_x * shear_x - ratio_y * normal_y - ratio_y * gravity * depth * bed_y)
    return (new_depth, push_x, push_y)

def thomas(coefficient, right):

    def forward(carry, row):
        prev_upper, prev_right = carry
        coef_row, right_row = row
        denom = 1.0 + 2.0 * coef_row + coef_row * prev_upper
        upper_new = -coef_row / denom
        right_new = (right_row + coef_row * prev_right) / denom
        return ((upper_new, right_new), (upper_new, right_new))
    zeros = jnp.zeros(right.shape[1:], jnp.float32)
    carry_end, (uppers, rights) = lax.scan(forward, (zeros, zeros), (coefficient, right))

    def backward(after_value, row):
        upper_row, right_row = row
        value = right_row - upper_row * after_value
        return (value, value)
    last_value, solved = lax.scan(backward, zeros, (uppers, rights), reverse=True)
    return solved

def reference(depth, momentum_x, momentum_y, bed, wet):
    stacked = jnp.stack([depth, momentum_x, momentum_y, bed, wet.astype(jnp.float32)])
    padded = jnp.pad(stacked, ((0, 0), (2, 2), (2, 2)))

    def one_block(index):
        block = lax.dynamic_slice_in_dim(padded, index * CY, CY + 4, axis=2)
        return jnp.stack(predict(block))
    blocks = lax.map(one_block, jnp.arange(N_GY, dtype=jnp.int32))
    fields = jnp.transpose(blocks, (1, 2, 0, 3)).reshape(3, NX, NY)
    scale_x = (NX / 4.0) ** 2 / 3.0
    scale_y = (NY / 4.0) ** 2 / 3.0
    coef_x = scale_x * depth * depth
    coef_y = scale_y * depth * depth
    flux_u = thomas(coef_x, fields[1])
    flux_v = thomas(coef_y.T, fields[2].T).T
    return (fields[0], flux_u / depth, flux_v / depth)
```

```python
import functools

import jax
import jax.numpy as jnp
from jax import lax
from jax.experimental import pallas as pl
from jax.experimental.pallas import tpu as pltpu
from jax.sharding import PartitionSpec as P

MESH = pl.DeviceIdType.MESH
GRAVITY = 9.81
ROOT_G = GRAVITY**0.5
RATIO = 0.05
LANES = 128
TILES = 4
STEPS = 16
TOP = 8
f32 = jnp.float32


def minmod(a, c):
    return jnp.maximum(jnp.minimum(a, c), 0.0) + jnp.minimum(jnp.maximum(a, c), 0.0)


def face_flux(lefts, rights, opened):
    hl, pl_, ql = lefts
    hr, pr, qr = rights
    sl = jnp.where(opened, hl, 1.0)
    sr = jnp.where(opened, hr, 1.0)
    il = lax.rsqrt(sl)
    ir = lax.rsqrt(sr)
    ul = pl_ * (il * il)
    ur = pr * (ir * ir)
    fast = jnp.maximum(
        jnp.abs(ul) + (ROOT_G * sl) * il, jnp.abs(ur) + (ROOT_G * sr) * ir
    )
    factor = jnp.where(opened, 0.5 * RATIO, 0.0)
    mass = (pl_ + pr) - fast * (hr - hl)
    normal = (pl_ * ul + pr * ur) + (0.5 * GRAVITY) * (sl * sl + sr * sr) - fast * (pr - pl_)
    across = (ql * ul + qr * ur) - fast * (qr - ql)
    return factor * mass, factor * normal, factor * across


def lane_up(tiles, lane):
    n = len(tiles)
    rolled = [pltpu.roll(t, LANES - 1, 1) for t in tiles]
    return [jnp.where(lane == LANES - 1, rolled[(i + 1) % n], rolled[i]) for i in range(n)]


def lane_down(tiles, lane):
    n = len(tiles)
    rolled = [pltpu.roll(t, 1, 1) for t in tiles]
    return [jnp.where(lane == 0, rolled[(i - 1) % n], rolled[i]) for i in range(n)]


def matmul2(m, a):
    m11, m12, m21, m22 = m
    a11, a12, a21, a22 = a
    return (
        m11 * a11 + m12 * a21,
        m11 * a12 + m12 * a22,
        m21 * a11 + m22 * a21,
        m21 * a12 + m22 * a22,
    )


def apply2(m, v):
    return (m[0] * v[0] + m[1] * v[1], m[2] * v[0] + m[3] * v[1])


def shifted(values, k, sub, first):
    return tuple(
        jnp.where(sub >= k, pltpu.roll(v, k, 0), f) for v, f in zip(values, first)
    )


IDENT = (1.0, 0.0, 0.0, 1.0)


def scan_matrices(m, sub):
    windows = []
    for k in (1, 2, 4):
        windows.append(m)
        m = matmul2(m, shifted(m, k, sub, IDENT))
    return windows, m, shifted(m, 1, sub, IDENT)


def scan_vectors(windows, v, sub):
    for k, m in zip((1, 2, 4), windows):
        moved = apply2(m, shifted(v, k, sub, (0.0, 0.0)))
        v = (v[0] + moved[0], v[1] + moved[1])
    return v, shifted(v, 1, sub, (0.0, 0.0))


def kernel(
    sizes, spring,
    h_in, p_in, q_in, b_in, m_in,
    corr_out, u_out, v_out,
    fields, wetc, csx, ctr, ax, bx, cx, ay, by, cy, win_x, win_y, pre_x, pre_y,
    faces, qs, qt, vt, os_n, os_u, os_v, pack, got, hc,
    coef_z, coef_x, coef_y, rhs_z, rhs_x, rhs_y, row_y,
    load_sem, halo_send, halo_recv, far_send, far_recv, out_sem,
):
    nx, nz, ny = sizes
    gx = lax.axis_index("gx")
    gy = lax.axis_index("gy")
    xi = lax.div(gx, nz)
    zi = lax.rem(gx, nz)
    ngx = nx * nz

    x_up = (lax.rem(gx + 1, ngx), gy)
    x_dn = (lax.rem(gx + ngx - 1, ngx), gy)
    y_up = (gx, lax.rem(gy + 1, ny))
    y_dn = (gx, lax.rem(gy + ny - 1, ny))
    z_mates = [(xi * nz + lax.rem(zi + k, nz), gy) for k in range(1, nz)]
    x_mates = [(lax.rem(xi + k, nx) * nz + zi, gy) for k in range(1, nx)]
    y_mates = [(gx, lax.rem(gy + k, ny)) for k in range(1, ny)]

    barrier = pltpu.get_barrier_semaphore()
    peers = [x_up, x_dn] + z_mates + x_mates + y_mates
    for peer in peers:
        pl.semaphore_signal(barrier, inc=1, device_id=peer, device_id_type=MESH)

    loads = []
    for i, src in enumerate((h_in, p_in, q_in, b_in, m_in)):
        for l in range(TILES):
            where = pl.ds(l * LANES, LANES)
            dst = fields.at[i, l, pl.ds(TOP, 128), :] if i < 4 else wetc.at[l, pl.ds(TOP, 128), :]
            copy = pltpu.make_async_copy(src.at[:, where], dst, load_sem.at[i * TILES + l])
            copy.start()
            loads.append(copy)

    sub = lax.broadcasted_iota(jnp.int32, (8, LANES), 0)
    lane = lax.broadcasted_iota(jnp.int32, (8, LANES), 1)
    zero = jnp.where(lane + sub < 0, 1.0, 0.0)
    one = jnp.where(lane + sub < 0, 0.0, 1.0)

    def strided(ref, l, start):
        return ref[l, pl.ds(start, 8, stride=STEPS), :]

    def block(t):
        return pl.ds(pl.multiple_of(8 * t, 8), 8)

    for copy in loads[:TILES]:
        copy.wait()

    def start_pieces():
        return tuple((one, zero, zero, one) for _ in range(TILES))

    def coef_step_x(t, carry):
        out = []
        for l in range(TILES):
            ua, ga, ub, gb = carry[l]
            h = fields[0, l, pl.ds(TOP + t, 8, stride=STEPS), :]
            c = spring / (h * h)
            csx[l, block(t), :] = c
            ua = ua + ga
            ub = ub + gb
            ax[l, block(t), :] = ua
            bx[l, block(t), :] = ub
            out.append((ua, ga + c * ua, ub, gb + c * ub))
        return tuple(out)

    ends = lax.fori_loop(0, STEPS, coef_step_x, start_pieces(), unroll=2)
    for l in range(TILES):
        ua, ga, ub, gb = ends[l]
        windows, total, before = scan_matrices((ua, ub, ga, gb), sub)
        for k in range(3):
            for e in range(4):
                win_x[l, 4 * k + e] = windows[k][e]
        for e in range(4):
            pre_x[l, e] = before[e]
        f = 1.0 / total[3]
        coef_x_row = (f, total[1] * f, total[2] * f)
        for e in range(3):
            coef_z[zi, 4 * e + l : 4 * e + l + 1, :] = coef_x_row[e][7:8, :]
            win_x[l, 12 + e] = coef_x_row[e]

    for l in range(TILES):
        ctr[l] = csx[l].T

    def coef_step_y(t, carry):
        out = []
        for l in range(TILES):
            ua, ga, ub, gb = carry[l]
            c = ctr[l, pl.ds(t, 8, stride=STEPS), :]
            ua = ua + ga
            ub = ub + gb
            ay[l, block(t), :] = ua
            by[l, block(t), :] = ub
            out.append((ua, ga + c * ua, ub, gb + c * ub))
        return tuple(out)

    ends = lax.fori_loop(0, STEPS, coef_step_y, start_pieces(), unroll=2)
    total_y = None
    for l in range(TILES):
        ua, ga, ub, gb = ends[l]
        windows, total, before = scan_matrices((ua, ub, ga, gb), sub)
        for k in range(3):
            for e in range(4):
                win_y[l, 4 * k + e] = windows[k][e]
        for e in range(4):
            pre_y[l, e] = before[e]
            win_y[l, 12 + e] = total[e]
        total_y = total if total_y is None else matmul2(total, total_y)
    f = 1.0 / total_y[3]
    coef_y_row = (f, total_y[1] * f, total_y[2] * f)
    for e in range(3):
        coef_y[gy, e : e + 1, :] = coef_y_row[e][7:8, :]
        row_y[e] = coef_y_row[e]

    for copy in loads[TILES:]:
        copy.wait()

    full_lane = lax.broadcasted_iota(jnp.int32, (128, LANES), 1)
    packed = jnp.zeros((128, LANES), f32)
    own = pl.ds(TOP, 128)
    wet_first = wetc[0, own, :].astype(f32)
    wet_last = wetc[TILES - 1, own, :].astype(f32)
    for i in range(3):
        low = fields[i, 0, own, :]
        high = fields[i, TILES - 1, own, :]
        if i:
            low = pltpu.roll(low, 2 * i, 1)
            high = pltpu.roll(high, LANES - 2 * i, 1)
        packed = jnp.where((full_lane >> 1) == i, low, packed)
        packed = jnp.where((full_lane >> 1) == 63 - i, high, packed)
    packed = jnp.where(full_lane == 6, pltpu.roll(fields[3, 0, own, :], 6, 1), packed)
    packed = jnp.where(full_lane == 7, pltpu.roll(wet_first, 7, 1), packed)
    packed = jnp.where(
        full_lane == 121, pltpu.roll(fields[3, TILES - 1, own, :], LANES - 6, 1), packed
    )
    packed = jnp.where(full_lane == 120, pltpu.roll(wet_last, LANES - 7, 1), packed)
    turned = packed.T
    pack[0] = turned[0:8, :]
    pack[1] = turned[120:128, :]

    pl.semaphore_wait(barrier, len(peers))

    def remote(src, dst, send, recv, device):
        copy = pltpu.make_async_remote_copy(
            src_ref=src, dst_ref=dst, send_sem=send, recv_sem=recv,
            device_id=device, device_id_type=MESH,
        )
        copy.start()
        return copy

    halos_x = [
        remote(fields.at[:, :, pl.ds(TOP, 2), :], fields.at[:, :, pl.ds(TOP + 128, 2), :],
               halo_send.at[0], halo_recv.at[0], x_dn),
        remote(fields.at[:, :, pl.ds(TOP + 126, 2), :], fields.at[:, :, pl.ds(TOP - 2, 2), :],
               halo_send.at[1], halo_recv.at[1], x_up),
        remote(wetc.at[:, pl.ds(TOP, 2), :], wetc.at[:, pl.ds(TOP + 128, 2), :],
               halo_send.at[2], halo_recv.at[2], x_dn),
        remote(wetc.at[:, pl.ds(TOP + 126, 2), :], wetc.at[:, pl.ds(TOP - 2, 2), :],
               halo_send.at[3], halo_recv.at[3], x_up),
    ]
    halos_y = [
        remote(pack.at[0], got.at[0], halo_send.at[4], halo_recv.at[4], y_dn),
        remote(pack.at[1], got.at[1], halo_send.at[5], halo_recv.at[5], y_up),
    ]

    def gather(buf, slot, mates, base):
        return [
            remote(buf.at[slot], buf.at[slot], far_send.at[base + i], far_recv.at[base + i], mate)
            for i, mate in enumerate(mates)
        ]

    sent = list(halos_x) + list(halos_y)
    base_y = nz - 1
    base_x = base_y + ny - 1
    half = base_x + nx - 1
    coef_z_copies = gather(coef_z, zi, z_mates, 0)
    coef_y_copies = gather(coef_y, gy, y_mates, base_y)
    sent += coef_z_copies + coef_y_copies

    def x_faces(t):
        for l in range(TILES):
            lefts, rights = [], []
            for i in range(3):
                w = [fields[i, l, pl.ds(TOP + t + d, 8, stride=STEPS), :] for d in (-2, -1, 0, 1)]
                d0 = 0.5 * (w[1] - w[0])
                d1 = 0.5 * (w[2] - w[1])
                d2 = 0.5 * (w[3] - w[2])
                lefts.append(w[1] + minmod(d0, d1))
                rights.append(w[2] - minmod(d1, d2))
            m0 = wetc[l, pl.ds(TOP + t - 1, 8, stride=STEPS), :]
            m1 = wetc[l, pl.ds(TOP + t, 8, stride=STEPS), :]
            flux = face_flux(lefts, rights, (m0 * m1) > 0)
            for i in range(3):
                faces[i, l, block(t), :] = flux[i]

    def interior(t, carry):
        x_faces(t)
        return carry

    lax.fori_loop(2, STEPS - 1, interior, 0)

    for copy in halos_x:
        copy.wait_recv()

    @pl.when(gx == 0)
    def _():
        fields[:, :, TOP - 2 : TOP, :] = jnp.zeros((4, TILES, 2, LANES), f32)
        wetc[:, TOP - 2 : TOP, :] = jnp.zeros((TILES, 2, LANES), jnp.int32)

    @pl.when(gx == ngx - 1)
    def _():
        fields[:, :, TOP + 128 : TOP + 130, :] = jnp.zeros((4, TILES, 2, LANES), f32)
        wetc[:, TOP + 128 : TOP + 130, :] = jnp.zeros((TILES, 2, LANES), jnp.int32)

    def rim(k, carry):
        x_faces(jnp.where(k < 2, k, k + (STEPS - 3)))
        return carry

    lax.fori_loop(0, 4, rim, 0)

    for copy in coef_z_copies:
        copy.wait_recv()

    def port(buf, k):
        return buf[k, 0:4, :], buf[k, 4:8, :], buf[k, 8:12, :]

    group_steps = []
    f, tau, mu = port(coef_z, 0)
    for k in range(1, nz):
        fk, tk, mk = port(coef_z, k)
        inv = 1.0 / (1.0 + tau * mk)
        a = fk * inv
        d = f * inv
        group_steps.append((a, a * tau, d, d * mk))
        f, tau, mu = f * a, tk + fk * (a * tau), mu + f * (d * mk)
    coef_x[xi, 0:4, :] = f
    coef_x[xi, 4:8, :] = tau
    coef_x[xi, 8:12, :] = mu
    coef_x_copies = gather(coef_x, xi, x_mates, base_x)
    sent += coef_x_copies

    for copy in halos_y:
        copy.wait_recv()
    above = jnp.where(gy < ny - 1, got[0], 0.0)
    below = jnp.where(gy > 0, got[1], 0.0)
    hc[...] = jnp.concatenate([above, jnp.zeros((112, LANES), f32), below], axis=0).T

    def y_pass(t, carry):
        edge = hc[pl.ds(t, 8, stride=STEPS), :]

        def rim_tile(up, down):
            return jnp.where(lane < 64, pltpu.roll(edge, LANES - up, 1), pltpu.roll(edge, down, 1))

        rims = [edge, rim_tile(2, 2), rim_tile(4, 4)]
        bed_rim = rim_tile(6, 6)
        wet_rim = rim_tile(7, 7)
        start = pl.ds(TOP + t, 8, stride=STEPS)
        values = [[fields[i, l, start, :] for l in range(TILES)] + [rims[i]] for i in range(3)]
        wet_own = [wetc[l, start, :].astype(f32) for l in range(TILES)]
        wet_all = wet_own + [jnp.where((lane == 0) | (lane == LANES - 1), wet_rim, 0.0)]
        wet_next = lane_up(wet_all, lane)
        opened = [(a * b) > 0.5 for a, b in zip(wet_all, wet_next)]
        lefts, rights = [], []
        for i in (0, 2, 1):
            w = values[i]
            ahead = lane_up(w, lane)
            diff = [0.5 * (a - b) for a, b in zip(ahead, w)]
            before = lane_down(diff, lane)
            slope = [minmod(a, b) for a, b in zip(before, diff)]
            lefts.append([a + s for a, s in zip(w, slope)])
            rights.append(lane_up([a - s for a, s in zip(w, slope)], lane))
        flux = [
            face_flux([x[l] for x in lefts], [x[l] for x in rights], opened[l])
            for l in range(TILES + 1)
        ]
        grads = []
        for i in range(3):
            line = [flux[l][i] for l in range(TILES + 1)]
            past = lane_down(line, lane)
            grads.append([a - b for a, b in zip(line, past)][:TILES])
        bed = [fields[3, l, start, :] for l in range(TILES)] + [bed_rim]
        bed_next = lane_up(bed, lane)
        bed_past = lane_down(bed, lane)
        out = []
        for l in range(TILES):
            uc, gc = carry[l]
            h, p, q = (values[i][l] for i in range(3))
            m = wet_own[l]
            fx = [faces[i, l, block(t + 1), :] - faces[i, l, block(t), :] for i in range(3)]
            push = (0.5 * RATIO * GRAVITY) * h
            bed_up = fields[3, l, pl.ds(TOP + t + 1, 8, stride=STEPS), :]
            bed_dn = fields[3, l, pl.ds(TOP + t - 1, 8, stride=STEPS), :]
            os_n[l, pl.ds(t, 8, stride=STEPS), :] = m * (fx[0] + grads[0][l])
            px = m * (p - fx[1] - grads[2][l] - push * (bed_up - bed_dn))
            qs[l, block(t), :] = m * (
                q - fx[2] - grads[1][l] - push * (bed_next[l] - bed_past[l])
            )
            uc = uc + gc
            cx[l, block(t), :] = uc
            out.append((uc, gc + csx[l, block(t), :] * (uc - px)))
        return tuple(out)

    rest = tuple((zero, zero) for _ in range(TILES))
    ends = lax.fori_loop(0, STEPS, y_pass, rest)

    before_x = []
    for l in range(TILES):
        windows = [[win_x[l, 4 * k + e] for e in range(4)] for k in range(3)]
        total, before = scan_vectors(windows, ends[l], sub)
        before_x.append(before)
        f, tau = win_x[l, 12], win_x[l, 13]
        rhs_z[zi, l : l + 1, :] = (total[0] - tau * total[1])[7:8, :]
        rhs_z[zi, 4 + l : 5 + l, :] = (-(f * total[1]))[7:8, :]
    rhs_z_copies = gather(rhs_z, zi, z_mates, half)
    sent += rhs_z_copies

    outs = [
        pltpu.make_async_copy(os_n.at[l], corr_out.at[:, pl.ds(l * LANES, LANES)], out_sem.at[l])
        for l in range(TILES)
    ]
    for copy in outs:
        copy.start()

    for l in range(TILES):
        qt[l] = qs[l].T

    def rhs_step_y(t, carry):
        out = []
        for l in range(TILES):
            uc, gc = carry[l]
            where = pl.ds(t, 8, stride=STEPS)
            uc = uc + gc
            cy[l, block(t), :] = uc
            out.append((uc, gc + ctr[l, where, :] * (uc - qt[l, where, :])))
        return tuple(out)

    ends = lax.fori_loop(0, STEPS, rhs_step_y, rest, unroll=2)
    before_y, totals_y = [], []
    sum_y = None
    for l in range(TILES):
        windows = [[win_y[l, 4 * k + e] for e in range(4)] for k in range(3)]
        total, before = scan_vectors(windows, ends[l], sub)
        before_y.append(before)
        totals_y.append(total)
        if sum_y is None:
            sum_y = total
        else:
            moved = apply2([win_y[l, 12 + e] for e in range(4)], sum_y)
            sum_y = (total[0] + moved[0], total[1] + moved[1])
    rhs_y[gy, 0:1, :] = (sum_y[0] - row_y[1] * sum_y[1])[7:8, :]
    rhs_y[gy, 1:2, :] = (-(row_y[0] * sum_y[1]))[7:8, :]
    rhs_y_copies = gather(rhs_y, gy, y_mates, half + base_y)
    sent += rhs_y_copies

    def left_chain(ports, mine, rho):
        steps = []
        for k in range(len(ports)):
            fk, tk, mk = ports[k]
            inv = 1.0 / (1.0 + rho * mk)
            a = fk * inv
            steps.append((a, a * rho))
            rho = jnp.where(k < mine, tk + fk * (a * rho), rho)
        return rho, steps

    def right_chain(ports, mine, back):
        steps = [None] * len(ports)
        for k in reversed(range(len(ports))):
            fk, tk, mk = ports[k]
            inv = 1.0 / (1.0 + tk * back)
            a = fk * inv
            steps[k] = (a, a * back)
            back = jnp.where(k >= mine, mk + fk * (a * back), back)
        return back, steps

    def left_values(steps, rhs, mine, w):
        for k in range(len(steps)):
            a, b = steps[k]
            w1, w2 = rhs[k]
            w = jnp.where(k < mine, w1 + a * w + b * w2, w)
        return w

    def right_values(steps, rhs, mine, w):
        for k in reversed(range(len(steps))):
            a, b = steps[k]
            w1, w2 = rhs[k]
            w = jnp.where(k >= mine, w2 + a * w - b * w1, w)
        return w

    def meet(rho, back, wl, wr):
        inv = 1.0 / (1.0 + rho * back)
        return (rho * wr + wl) * inv, (wr - back * wl) * inv

    for copy in coef_y_copies:
        copy.wait_recv()
    ports_y = [tuple(coef_y[k, e : e + 1, :] for e in range(3)) for k in range(ny)]
    row_zero = jnp.zeros((1, LANES), f32)
    rho_y, left_y = left_chain(ports_y, gy, row_zero)
    back_y, right_y = right_chain(ports_y, gy, row_zero + 1.0)

    for copy in coef_x_copies:
        copy.wait_recv()
    ports_x = [port(coef_x, k) for k in range(nx)]
    ports_z = [port(coef_z, k) for k in range(nz)]
    four_zero = jnp.zeros((4, LANES), f32)
    rho_x, left_x = left_chain(ports_x, xi, four_zero)
    back_x, right_x = right_chain(ports_x, xi + 1, four_zero + 1.0)
    rho_z, left_z = left_chain(ports_z, zi, rho_x)
    back_z, right_z = right_chain(ports_z, zi, back_x)

    for copy in rhs_z_copies:
        copy.wait_recv()
    rhs_in_z = [(rhs_z[k, 0:4, :], rhs_z[k, 4:8, :]) for k in range(nz)]
    w1, w2 = rhs_in_z[0]
    for k in range(1, nz):
        a, at, d, dm = group_steps[k - 1]
        k1, k2 = rhs_in_z[k]
        w1, w2 = k1 + a * w1 + at * k2, w2 + d * k2 - dm * w1
    rhs_x[xi, 0:4, :] = w1
    rhs_x[xi, 4:8, :] = w2
    rhs_x_copies = gather(rhs_x, xi, x_mates, half + base_x)
    sent += rhs_x_copies

    for copy in rhs_y_copies:
        copy.wait_recv()
    rhs_in_y = [(rhs_y[k, 0:1, :], rhs_y[k, 1:2, :]) for k in range(ny)]
    wl = left_values(left_y, rhs_in_y, gy, row_zero)
    wr = right_values(right_y, rhs_in_y, gy, row_zero)
    state = meet(rho_y, back_y, wl, wr)
    starts = []
    for l in range(TILES):
        before = [pre_y[l, e] for e in range(4)]
        wide = tuple(jnp.broadcast_to(s, (8, LANES)) for s in state)
        moved = apply2(before, wide)
        starts.append((moved[0] + before_y[l][0], moved[1] + before_y[l][1]))
        if l < TILES - 1:
            moved = apply2([win_y[l, 12 + e] for e in range(4)], wide)
            state = tuple((moved[e] + totals_y[l][e])[7:8, :] for e in range(2))

    def finish_y(t, carry):
        for l in range(TILES):
            at = block(t)
            vt[l, pl.ds(t, 8, stride=STEPS), :] = (
                ay[l, at, :] * starts[l][0] + by[l, at, :] * starts[l][1] + cy[l, at, :]
            )
        return carry

    lax.fori_loop(0, STEPS, finish_y, 0, unroll=2)
    for l in range(TILES):
        natural = vt[l].T
        for t in range(STEPS):
            os_v[l, pl.ds(t, 8, stride=STEPS), :] = natural[8 * t : 8 * t + 8, :]
        copy = pltpu.make_async_copy(
            os_v.at[l], v_out.at[:, pl.ds(l * LANES, LANES)], out_sem.at[TILES + l]
        )
        copy.start()
        outs.append(copy)

    for copy in rhs_x_copies:
        copy.wait_recv()
    rhs_in_x = [(rhs_x[k, 0:4, :], rhs_x[k, 4:8, :]) for k in range(nx)]
    wl = left_values(left_x, rhs_in_x, xi, four_zero)
    wr = right_values(right_x, rhs_in_x, xi + 1, four_zero)
    wl = left_values(left_z, rhs_in_z, zi, wl)
    wr = right_values(right_z, rhs_in_z, zi, wr)
    state = meet(rho_z, back_z, wl, wr)
    for l in range(TILES):
        before = [pre_x[l, e] for e in range(4)]
        wide = tuple(jnp.broadcast_to(s[l : l + 1, :], (8, LANES)) for s in state)
        moved = apply2(before, wide)
        u0, g0 = moved[0] + before_x[l][0], moved[1] + before_x[l][1]
        for t in range(STEPS):
            at = pl.ds(8 * t, 8)
            os_u[l, pl.ds(t, 8, stride=STEPS), :] = (
                ax[l, at, :] * u0 + bx[l, at, :] * g0 + cx[l, at, :]
            )
        copy = pltpu.make_async_copy(
            os_u.at[l], u_out.at[:, pl.ds(l * LANES, LANES)], out_sem.at[2 * TILES + l]
        )
        copy.start()
        outs.append(copy)

    for copy in sent:
        copy.wait_send()
    for copy in outs:
        copy.wait()


def predictor(sizes, spring, depth, momentum_x, momentum_y, bed, wet):
    nx, nz, ny = sizes
    rows, cols = depth.shape
    flat = jax.ShapeDtypeStruct((rows, cols), f32)
    hbm = pl.BlockSpec(memory_space=pl.ANY)
    tile = (TILES, 128, LANES)
    far = 2 * (nz + nx + ny - 3)
    corr, flux_u, flux_v = pl.pallas_call(
        functools.partial(kernel, sizes, spring),
        out_shape=(flat, flat, flat),
        in_specs=[hbm] * 5,
        out_specs=[hbm] * 3,
        scratch_shapes=[
            pltpu.VMEM((4, TILES, 144, LANES), f32),
            pltpu.VMEM((TILES, 144, LANES), jnp.int32),
            pltpu.VMEM(tile, f32),
            pltpu.VMEM(tile, f32),
            pltpu.VMEM(tile, f32),
            pltpu.VMEM(tile, f32),
            pltpu.VMEM(tile, f32),
            pltpu.VMEM(tile, f32),
            pltpu.VMEM(tile, f32),
            pltpu.VMEM(tile, f32),
            pltpu.VMEM((TILES, 16, 8, LANES), f32),
            pltpu.VMEM((TILES, 16, 8, LANES), f32),
            pltpu.VMEM((TILES, 4, 8, LANES), f32),
            pltpu.VMEM((TILES, 4, 8, LANES), f32),
            pltpu.VMEM((3, TILES, 136, LANES), f32),
            pltpu.VMEM(tile, f32),
            pltpu.VMEM(tile, f32),
            pltpu.VMEM(tile, f32),
            pltpu.VMEM(tile, f32),
            pltpu.VMEM(tile, f32),
            pltpu.VMEM(tile, f32),
            pltpu.VMEM((2, 8, LANES), f32),
            pltpu.VMEM((2, 8, LANES), f32),
            pltpu.VMEM((128, LANES), f32),
            pltpu.VMEM((nz, 16, LANES), f32),
            pltpu.VMEM((nx, 16, LANES), f32),
            pltpu.VMEM((ny, 8, LANES), f32),
            pltpu.VMEM((nz, 8, LANES), f32),
            pltpu.VMEM((nx, 8, LANES), f32),
            pltpu.VMEM((ny, 8, LANES), f32),
            pltpu.VMEM((3, 8, LANES), f32),
            pltpu.SemaphoreType.DMA((5 * TILES,)),
            pltpu.SemaphoreType.DMA((6,)),
            pltpu.SemaphoreType.DMA((6,)),
            pltpu.SemaphoreType.DMA((far,)),
            pltpu.SemaphoreType.DMA((far,)),
            pltpu.SemaphoreType.DMA((3 * TILES,)),
        ],
        compiler_params=pltpu.CompilerParams(
            collective_id=0, has_side_effects=True, vmem_limit_bytes=48 * 1024 * 1024
        ),
    )(depth, momentum_x, momentum_y, bed, wet)
    return (depth - corr, flux_u / depth, flux_v / depth)


def solution(mesh):
    ngx, ny = mesh.shape["gx"], mesh.shape["gy"]
    nz = 8 if ngx % 8 == 0 else max(1, ngx // 2)
    sizes = (ngx // nz, nz, ny)
    scale = (4096 / 4.0) ** 2 / 3.0
    place = P("gx", "gy")
    return jax.shard_map(
        functools.partial(predictor, sizes, 1.0 / scale),
        mesh=mesh,
        in_specs=(place,) * 5,
        out_specs=(place,) * 3,
        check_vma=False,
    )
```

```python
import functools

import jax
import jax.numpy as jnp
from jax import lax
from jax.experimental import pallas as pl
from jax.experimental.pallas import tpu as pltpu
from jax.sharding import PartitionSpec as P

MESH = pl.DeviceIdType.MESH
GRAVITY = 9.81
ROOT_G = GRAVITY**0.5
RATIO = 0.05
LANES = 128
TILES = 4
STEPS = 16
PITCH = 20
f32 = jnp.float32


def minmod(a, c):
    return jnp.maximum(jnp.minimum(a, c), 0.0) + jnp.minimum(jnp.maximum(a, c), 0.0)


def face_flux(lefts, rights, opened):
    hl, pl_, ql = lefts
    hr, pr, qr = rights
    sl = jnp.where(opened, hl, 1.0)
    sr = jnp.where(opened, hr, 1.0)
    il = lax.rsqrt(sl)
    ir = lax.rsqrt(sr)
    ul = pl_ * (il * il)
    ur = pr * (ir * ir)
    fast = jnp.maximum(
        jnp.abs(ul) + (ROOT_G * sl) * il, jnp.abs(ur) + (ROOT_G * sr) * ir
    )
    factor = jnp.where(opened, 0.5 * RATIO, 0.0)
    mass = (pl_ + pr) - fast * (hr - hl)
    normal = (pl_ * ul + pr * ur) + (0.5 * GRAVITY) * (sl * sl + sr * sr) - fast * (pr - pl_)
    across = (ql * ul + qr * ur) - fast * (qr - ql)
    return factor * mass, factor * normal, factor * across


def lane_up(tiles, lane):
    n = len(tiles)
    rolled = [pltpu.roll(t, LANES - 1, 1) for t in tiles]
    return [jnp.where(lane == LANES - 1, rolled[(i + 1) % n], rolled[i]) for i in range(n)]


def lane_down(tiles, lane):
    n = len(tiles)
    rolled = [pltpu.roll(t, 1, 1) for t in tiles]
    return [jnp.where(lane == 0, rolled[(i - 1) % n], rolled[i]) for i in range(n)]


def matmul2(m, a):
    m11, m12, m21, m22 = m
    a11, a12, a21, a22 = a
    return (
        m11 * a11 + m12 * a21,
        m11 * a12 + m12 * a22,
        m21 * a11 + m22 * a21,
        m21 * a12 + m22 * a22,
    )


def apply2(m, v):
    return (m[0] * v[0] + m[1] * v[1], m[2] * v[0] + m[3] * v[1])


def shifted(values, k, sub, first):
    return tuple(
        jnp.where(sub >= k, pltpu.roll(v, k, 0), f) for v, f in zip(values, first)
    )


IDENT = (1.0, 0.0, 0.0, 1.0)


def scan_matrices(m, sub):
    windows = []
    for k in (1, 2, 4):
        windows.append(m)
        m = matmul2(m, shifted(m, k, sub, IDENT))
    return windows, m, shifted(m, 1, sub, IDENT)


def scan_vectors(windows, v, sub):
    for k, m in zip((1, 2, 4), windows):
        moved = apply2(m, shifted(v, k, sub, (0.0, 0.0)))
        v = (v[0] + moved[0], v[1] + moved[1])
    return v, shifted(v, 1, sub, (0.0, 0.0))


def kernel(
    sizes, spring,
    h_in, p_in, q_in, b_in, m_in,
    corr_out, u_out, v_out,
    fields, wetc, csx, cty, ax, bx, cx, ay, by, cy, win_x, win_y, pre_x, pre_y,
    faces, qs, qt, vt, os_n, os_u, os_v, pack, got, hc,
    coef_z, coef_x, coef_y, rhs_z, rhs_x, rhs_y, row_y,
    load_sem, halo_send, halo_recv, far_send, far_recv, out_sem,
):
    nx, nz, ny = sizes
    gx = lax.axis_index("gx")
    gy = lax.axis_index("gy")
    xi = lax.div(gx, nz)
    zi = lax.rem(gx, nz)
    ngx = nx * nz

    x_up = (lax.rem(gx + 1, ngx), gy)
    x_dn = (lax.rem(gx + ngx - 1, ngx), gy)
    y_up = (gx, lax.rem(gy + 1, ny))
    y_dn = (gx, lax.rem(gy + ny - 1, ny))
    z_mates = [(xi * nz + lax.rem(zi + k, nz), gy) for k in range(1, nz)]
    x_mates = [(lax.rem(xi + k, nx) * nz + zi, gy) for k in range(1, nx)]
    y_mates = [(gx, lax.rem(gy + k, ny)) for k in range(1, ny)]

    barrier = pltpu.get_barrier_semaphore()
    peers = [x_up, x_dn] + z_mates + x_mates + y_mates
    for peer in peers:
        pl.semaphore_signal(barrier, inc=1, device_id=peer, device_id_type=MESH)

    loads = []
    for i, src in enumerate((h_in, p_in, q_in, b_in, m_in)):
        for s in range(8):
            rows = pl.ds(2, STEPS)
            dst = fields.at[i, rows, s, :] if i < 4 else wetc.at[rows, s, :]
            copy = pltpu.make_async_copy(src.at[s], dst, load_sem.at[8 * i + s])
            copy.start()
            loads.append(copy)

    sub = lax.broadcasted_iota(jnp.int32, (8, LANES), 0)
    lane = lax.broadcasted_iota(jnp.int32, (8, LANES), 1)
    zero = jnp.where(lane + sub < 0, 1.0, 0.0)
    one = jnp.where(lane + sub < 0, 0.0, 1.0)
    cols = [pl.ds(LANES * l, LANES) for l in range(TILES)]

    def block(t):
        return pl.ds(pl.multiple_of(8 * t, 8), 8)

    for copy in loads:
        copy.wait()

    full_lane = lax.broadcasted_iota(jnp.int32, (128, LANES), 1)

    def edge(i, l):
        if i < 4:
            return fields[i, 2 : 2 + STEPS, :, cols[l]].reshape(128, LANES)
        return wetc[2 : 2 + STEPS, :, cols[l]].reshape(128, LANES).astype(f32)

    packed = edge(0, 0)
    packed = jnp.where(full_lane >= 64, edge(0, TILES - 1), packed)
    for i, width in ((1, 2), (2, 4), (3, 6), (4, 7)):
        low = pltpu.roll(edge(i, 0), width, 1)
        high = pltpu.roll(edge(i, TILES - 1), LANES - width, 1)
        packed = jnp.where((full_lane >= width) & (full_lane < 64), low, packed)
        packed = jnp.where((full_lane >= 64) & (full_lane < LANES - width), high, packed)
    turned = packed.T
    pack[0] = turned[0:8, :]
    pack[1] = turned[120:128, :]

    pl.semaphore_wait(barrier, len(peers))

    def remote(src, dst, send, recv, device):
        copy = pltpu.make_async_remote_copy(
            src_ref=src, dst_ref=dst, send_sem=send, recv_sem=recv,
            device_id=device, device_id_type=MESH,
        )
        copy.start()
        return copy

    first, last = pl.ds(2, 2), pl.ds(STEPS, 2)
    past, ahead = pl.ds(0, 2), pl.ds(STEPS + 2, 2)
    halos_x = [
        remote(fields.at[:, first, 0, :], fields.at[:, ahead, 7, :],
               halo_send.at[0], halo_recv.at[0], x_dn),
        remote(fields.at[:, last, 7, :], fields.at[:, past, 0, :],
               halo_send.at[1], halo_recv.at[1], x_up),
        remote(wetc.at[first, 0, :], wetc.at[ahead, 7, :],
               halo_send.at[2], halo_recv.at[2], x_dn),
        remote(wetc.at[last, 7, :], wetc.at[past, 0, :],
               halo_send.at[3], halo_recv.at[3], x_up),
    ]
    halos_y = [
        remote(pack.at[0], got.at[0], halo_send.at[4], halo_recv.at[4], y_dn),
        remote(pack.at[1], got.at[1], halo_send.at[5], halo_recv.at[5], y_up),
    ]

    def gather(buf, slot, mates, base):
        return [
            remote(buf.at[slot], buf.at[slot], far_send.at[base + i], far_recv.at[base + i], mate)
            for i, mate in enumerate(mates)
        ]

    sent = list(halos_x) + list(halos_y)
    base_y = nz - 1
    base_x = base_y + ny - 1
    half = base_x + nx - 1

    def start_pieces():
        return tuple((one, zero, zero, one) for _ in range(TILES))

    def coef_step_x(t, carry):
        out = []
        for l in range(TILES):
            ua, ga, ub, gb = carry[l]
            h = fields[0, t + 2, :, cols[l]]
            c = spring / (h * h)
            csx[l, block(t), :] = c
            ua = ua + ga
            ub = ub + gb
            ax[l, block(t), :] = ua
            bx[l, block(t), :] = ub
            out.append((ua, ga + c * ua, ub, gb + c * ub))
        return tuple(out)

    ends = lax.fori_loop(0, STEPS, coef_step_x, start_pieces(), unroll=2)
    for l in range(TILES):
        ua, ga, ub, gb = ends[l]
        windows, total, before = scan_matrices((ua, ub, ga, gb), sub)
        for k in range(3):
            for e in range(4):
                win_x[l, 4 * k + e] = windows[k][e]
        for e in range(4):
            pre_x[l, e] = before[e]
        f = 1.0 / total[3]
        coef_x_row = (f, total[1] * f, total[2] * f)
        for e in range(3):
            coef_z[zi, 4 * e + l : 4 * e + l + 1, :] = coef_x_row[e][7:8, :]
            win_x[l, 12 + e] = coef_x_row[e]
    coef_z_copies = gather(coef_z, zi, z_mates, 0)

    def turn(dst, value):
        for s in range(8):
            dst[PITCH * s : PITCH * s + STEPS, :] = value[STEPS * s : STEPS * (s + 1), :]

    for l in range(TILES):
        turn(cty.at[l], csx[l].T)

    def coef_step_y(t, carry):
        out = []
        for l in range(TILES):
            ua, ga, ub, gb = carry[l]
            c = cty[l, pl.ds(t, 8, stride=PITCH), :]
            ua = ua + ga
            ub = ub + gb
            ay[l, block(t), :] = ua
            by[l, block(t), :] = ub
            out.append((ua, ga + c * ua, ub, gb + c * ub))
        return tuple(out)

    ends = lax.fori_loop(0, STEPS, coef_step_y, start_pieces(), unroll=2)
    total_y = None
    for l in range(TILES):
        ua, ga, ub, gb = ends[l]
        windows, total, before = scan_matrices((ua, ub, ga, gb), sub)
        for k in range(3):
            for e in range(4):
                win_y[l, 4 * k + e] = windows[k][e]
        for e in range(4):
            pre_y[l, e] = before[e]
            win_y[l, 12 + e] = total[e]
        total_y = total if total_y is None else matmul2(total, total_y)
    f = 1.0 / total_y[3]
    coef_y_row = (f, total_y[1] * f, total_y[2] * f)
    for e in range(3):
        coef_y[gy, e : e + 1, :] = coef_y_row[e][7:8, :]
        row_y[e] = coef_y_row[e]
    coef_y_copies = gather(coef_y, gy, y_mates, base_y)
    sent += coef_z_copies + coef_y_copies

    def x_faces(col, dst, start, count):
        w = [[fields[i, start + d, :, col] for d in range(4)] for i in range(3)]
        diff = [[0.5 * (w[i][d + 1] - w[i][d]) for d in range(3)] for i in range(3)]
        slope = [minmod(diff[i][0], diff[i][1]) for i in range(3)]
        for k in range(count):
            lefts, rights = [], []
            for i in range(3):
                after = minmod(diff[i][1], diff[i][2])
                lefts.append(w[i][1] + slope[i])
                rights.append(w[i][2] - after)
                slope[i] = after
                if k + 1 < count:
                    new = fields[i, start + k + 4, :, col]
                    w[i] = [None, w[i][2], w[i][3], new]
                    diff[i] = [None, diff[i][2], 0.5 * (new - w[i][2])]
            m0 = wetc[start + k + 1, :, col]
            m1 = wetc[start + k + 2, :, col]
            flux = face_flux(lefts, rights, (m0 * m1) > 0)
            for i in range(3):
                faces[i, start + k, :, col] = flux[i]

    def interior(l, carry):
        x_faces(pl.ds(pl.multiple_of(LANES * l, LANES), LANES), None, 2, STEPS - 3)
        return carry

    lax.fori_loop(0, TILES, interior, 0)

    for copy in halos_x:
        copy.wait_recv()

    def fill(ref, kind, both):
        for l in range(TILES):
            for t, source, rim, shift in (
                (0, STEPS, 0, 1), (1, STEPS + 1, 0, 1),
                (STEPS + 2, 2, 7, 7), (STEPS + 3, 3, 7, 7),
            ):
                if not both and t in (0, STEPS + 3):
                    continue
                gone = gx == 0 if rim == 0 else gx == ngx - 1
                border = jnp.where(gone, jnp.zeros((), kind), ref[t, :, cols[l]])
                ref[t, :, cols[l]] = jnp.where(
                    sub == rim, border, pltpu.roll(ref[source, :, cols[l]], shift, 0)
                )

    for i in range(4):
        fill(fields.at[i], f32, i < 3)
    fill(wetc, jnp.int32, False)

    def rim_faces(l, carry):
        col = pl.ds(pl.multiple_of(LANES * l, LANES), LANES)
        x_faces(col, None, 0, 2)
        x_faces(col, None, STEPS - 1, 2)
        return carry

    lax.fori_loop(0, TILES, rim_faces, 0)

    for copy in coef_z_copies:
        copy.wait_recv()

    def port(buf, k):
        return buf[k, 0:4, :], buf[k, 4:8, :], buf[k, 8:12, :]

    group_steps = []
    f, tau, mu = port(coef_z, 0)
    for k in range(1, nz):
        fk, tk, mk = port(coef_z, k)
        inv = 1.0 / (1.0 + tau * mk)
        a = fk * inv
        d = f * inv
        group_steps.append((a, a * tau, d, d * mk))
        f, tau, mu = f * a, tk + fk * (a * tau), mu + f * (d * mk)
    coef_x[xi, 0:4, :] = f
    coef_x[xi, 4:8, :] = tau
    coef_x[xi, 8:12, :] = mu
    coef_x_copies = gather(coef_x, xi, x_mates, base_x)
    sent += coef_x_copies

    for copy in halos_y:
        copy.wait_recv()
    above = jnp.where(gy < ny - 1, got[0], 0.0)
    below = jnp.where(gy > 0, got[1], 0.0)
    hc[...] = jnp.concatenate([above, jnp.zeros((112, LANES), f32), below], axis=0).T

    def y_pass(t, carry):
        rim = hc[block(t), :]

        def rim_tile(k):
            return jnp.where(lane < 64, pltpu.roll(rim, LANES - k, 1), pltpu.roll(rim, k, 1))

        rims = [rim, rim_tile(2), rim_tile(4)]
        bed_rim = rim_tile(6)
        wet_rim = rim_tile(7)
        values = [[fields[i, t + 2, :, c] for c in cols] + [rims[i]] for i in range(3)]
        wet_own = [wetc[t + 2, :, c].astype(f32) for c in cols]
        wet_all = wet_own + [jnp.where((lane == 0) | (lane == LANES - 1), wet_rim, 0.0)]
        wet_next = lane_up(wet_all, lane)
        opened = [(a * b) > 0.5 for a, b in zip(wet_all, wet_next)]
        lefts, rights = [], []
        for i in (0, 2, 1):
            w = values[i]
            after = lane_up(w, lane)
            diff = [0.5 * (a - b) for a, b in zip(after, w)]
            before = lane_down(diff, lane)
            slope = [minmod(a, b) for a, b in zip(before, diff)]
            lefts.append([a + s for a, s in zip(w, slope)])
            rights.append(lane_up([a - s for a, s in zip(w, slope)], lane))
        flux = [
            face_flux([x[l] for x in lefts], [x[l] for x in rights], opened[l])
            for l in range(TILES + 1)
        ]
        grads = []
        for i in range(3):
            line = [flux[l][i] for l in range(TILES + 1)]
            before = lane_down(line, lane)
            grads.append([a - b for a, b in zip(line, before)][:TILES])
        bed = [fields[3, t + 2, :, c] for c in cols] + [bed_rim]
        bed_next = lane_up(bed, lane)
        bed_past = lane_down(bed, lane)
        out = []
        for l in range(TILES):
            uc, gc = carry[l]
            h, p, q = (values[i][l] for i in range(3))
            m = wet_own[l]
            fx = [faces[i, t + 1, :, cols[l]] - faces[i, t, :, cols[l]] for i in range(3)]
            push = (0.5 * RATIO * GRAVITY) * h
            os_n[t, :, cols[l]] = m * (fx[0] + grads[0][l])
            rise = fields[3, t + 3, :, cols[l]] - fields[3, t + 1, :, cols[l]]
            px = m * (p - fx[1] - grads[2][l] - push * rise)
            qs[l, block(t), :] = m * (
                q - fx[2] - grads[1][l] - push * (bed_next[l] - bed_past[l])
            )
            uc = uc + gc
            cx[l, block(t), :] = uc
            out.append((uc, gc + csx[l, block(t), :] * (uc - px)))
        return tuple(out)

    rest = tuple((zero, zero) for _ in range(TILES))
    ends = lax.fori_loop(0, STEPS, y_pass, rest)

    before_x = []
    for l in range(TILES):
        windows = [[win_x[l, 4 * k + e] for e in range(4)] for k in range(3)]
        total, before = scan_vectors(windows, ends[l], sub)
        before_x.append(before)
        f, tau = win_x[l, 12], win_x[l, 13]
        rhs_z[zi, l : l + 1, :] = (total[0] - tau * total[1])[7:8, :]
        rhs_z[zi, 4 + l : 5 + l, :] = (-(f * total[1]))[7:8, :]
    rhs_z_copies = gather(rhs_z, zi, z_mates, half)
    sent += rhs_z_copies

    def store_out(staged, out, base):
        copies = [
            pltpu.make_async_copy(staged.at[:, s, :], out.at[s], out_sem.at[base + s])
            for s in range(8)
        ]
        for copy in copies:
            copy.start()
        return copies

    outs = store_out(os_n, corr_out, 0)

    for l in range(TILES):
        turn(qt.at[l], qs[l].T)

    def rhs_step_y(t, carry):
        out = []
        for l in range(TILES):
            uc, gc = carry[l]
            where = pl.ds(t, 8, stride=PITCH)
            uc = uc + gc
            cy[l, block(t), :] = uc
            out.append((uc, gc + cty[l, where, :] * (uc - qt[l, where, :])))
        return tuple(out)

    ends = lax.fori_loop(0, STEPS, rhs_step_y, rest, unroll=2)
    before_y, totals_y = [], []
    sum_y = None
    for l in range(TILES):
        windows = [[win_y[l, 4 * k + e] for e in range(4)] for k in range(3)]
        total, before = scan_vectors(windows, ends[l], sub)
        before_y.append(before)
        totals_y.append(total)
        if sum_y is None:
            sum_y = total
        else:
            moved = apply2([win_y[l, 12 + e] for e in range(4)], sum_y)
            sum_y = (total[0] + moved[0], total[1] + moved[1])
    rhs_y[gy, 0:1, :] = (sum_y[0] - row_y[1] * sum_y[1])[7:8, :]
    rhs_y[gy, 1:2, :] = (-(row_y[0] * sum_y[1]))[7:8, :]
    rhs_y_copies = gather(rhs_y, gy, y_mates, half + base_y)
    sent += rhs_y_copies

    def left_chain(ports, mine, rho):
        steps = []
        for k in range(len(ports)):
            fk, tk, mk = ports[k]
            inv = 1.0 / (1.0 + rho * mk)
            a = fk * inv
            steps.append((a, a * rho))
            rho = jnp.where(k < mine, tk + fk * (a * rho), rho)
        return rho, steps

    def right_chain(ports, mine, back):
        steps = [None] * len(ports)
        for k in reversed(range(len(ports))):
            fk, tk, mk = ports[k]
            inv = 1.0 / (1.0 + tk * back)
            a = fk * inv
            steps[k] = (a, a * back)
            back = jnp.where(k >= mine, mk + fk * (a * back), back)
        return back, steps

    def left_values(steps, rhs, mine, w):
        for k in range(len(steps)):
            a, b = steps[k]
            w1, w2 = rhs[k]
            w = jnp.where(k < mine, w1 + a * w + b * w2, w)
        return w

    def right_values(steps, rhs, mine, w):
        for k in reversed(range(len(steps))):
            a, b = steps[k]
            w1, w2 = rhs[k]
            w = jnp.where(k >= mine, w2 + a * w - b * w1, w)
        return w

    def meet(rho, back, wl, wr):
        inv = 1.0 / (1.0 + rho * back)
        return (rho * wr + wl) * inv, (wr - back * wl) * inv

    for copy in coef_y_copies:
        copy.wait_recv()
    ports_y = [tuple(coef_y[k, e : e + 1, :] for e in range(3)) for k in range(ny)]
    row_zero = jnp.zeros((1, LANES), f32)
    rho_y, left_y = left_chain(ports_y, gy, row_zero)
    back_y, right_y = right_chain(ports_y, gy, row_zero + 1.0)

    for copy in coef_x_copies:
        copy.wait_recv()
    ports_x = [port(coef_x, k) for k in range(nx)]
    ports_z = [port(coef_z, k) for k in range(nz)]
    four_zero = jnp.zeros((4, LANES), f32)
    rho_x, left_x = left_chain(ports_x, xi, four_zero)
    back_x, right_x = right_chain(ports_x, xi + 1, four_zero + 1.0)
    rho_z, left_z = left_chain(ports_z, zi, rho_x)
    back_z, right_z = right_chain(ports_z, zi, back_x)

    for copy in rhs_z_copies:
        copy.wait_recv()
    rhs_in_z = [(rhs_z[k, 0:4, :], rhs_z[k, 4:8, :]) for k in range(nz)]
    w1, w2 = rhs_in_z[0]
    for k in range(1, nz):
        a, at, d, dm = group_steps[k - 1]
        k1, k2 = rhs_in_z[k]
        w1, w2 = k1 + a * w1 + at * k2, w2 + d * k2 - dm * w1
    rhs_x[xi, 0:4, :] = w1
    rhs_x[xi, 4:8, :] = w2
    rhs_x_copies = gather(rhs_x, xi, x_mates, half + base_x)
    sent += rhs_x_copies

    for copy in rhs_y_copies:
        copy.wait_recv()
    rhs_in_y = [(rhs_y[k, 0:1, :], rhs_y[k, 1:2, :]) for k in range(ny)]
    wl = left_values(left_y, rhs_in_y, gy, row_zero)
    wr = right_values(right_y, rhs_in_y, gy, row_zero)
    state = meet(rho_y, back_y, wl, wr)
    starts = []
    for l in range(TILES):
        before = [pre_y[l, e] for e in range(4)]
        wide = tuple(jnp.broadcast_to(s, (8, LANES)) for s in state)
        moved = apply2(before, wide)
        starts.append((moved[0] + before_y[l][0], moved[1] + before_y[l][1]))
        if l < TILES - 1:
            moved = apply2([win_y[l, 12 + e] for e in range(4)], wide)
            state = tuple((moved[e] + totals_y[l][e])[7:8, :] for e in range(2))

    def finish_y(t, carry):
        for l in range(TILES):
            at = block(t)
            vt[l, pl.ds(t, 8, stride=PITCH), :] = (
                ay[l, at, :] * starts[l][0] + by[l, at, :] * starts[l][1] + cy[l, at, :]
            )
        return carry

    lax.fori_loop(0, STEPS, finish_y, 0, unroll=2)
    for l in range(TILES):
        line = [vt[l, PITCH * s : PITCH * s + STEPS, :] for s in range(8)]
        os_v[:, :, cols[l]] = jnp.concatenate(line, axis=0).T.reshape(STEPS, 8, LANES)
    outs += store_out(os_v, v_out, 8)

    for copy in rhs_x_copies:
        copy.wait_recv()
    rhs_in_x = [(rhs_x[k, 0:4, :], rhs_x[k, 4:8, :]) for k in range(nx)]
    wl = left_values(left_x, rhs_in_x, xi, four_zero)
    wr = right_values(right_x, rhs_in_x, xi + 1, four_zero)
    wl = left_values(left_z, rhs_in_z, zi, wl)
    wr = right_values(right_z, rhs_in_z, zi, wr)
    state = meet(rho_z, back_z, wl, wr)
    for l in range(TILES):
        before = [pre_x[l, e] for e in range(4)]
        wide = tuple(jnp.broadcast_to(s[l : l + 1, :], (8, LANES)) for s in state)
        moved = apply2(before, wide)
        u0, g0 = moved[0] + before_x[l][0], moved[1] + before_x[l][1]
        for t in range(STEPS):
            at = pl.ds(8 * t, 8)
            os_u[t, :, cols[l]] = ax[l, at, :] * u0 + bx[l, at, :] * g0 + cx[l, at, :]
    outs += store_out(os_u, u_out, 16)

    for copy in sent:
        copy.wait_send()
    for copy in outs:
        copy.wait()


def predictor(sizes, spring, depth, momentum_x, momentum_y, bed, wet):
    nx, nz, ny = sizes
    rows, cols = depth.shape
    shape = (8, STEPS, cols)
    flat = jax.ShapeDtypeStruct(shape, f32)
    hbm = pl.BlockSpec(memory_space=pl.ANY)
    tile = (TILES, 128, LANES)
    wide = (TILES, 8 * PITCH, LANES)
    far = 2 * (nz + nx + ny - 3)
    results = pl.pallas_call(
        functools.partial(kernel, sizes, spring),
        out_shape=(flat, flat, flat),
        in_specs=[hbm] * 5,
        out_specs=[hbm] * 3,
        scratch_shapes=[
            pltpu.VMEM((4, STEPS + 4, 8, cols), f32),
            pltpu.VMEM((STEPS + 4, 8, cols), jnp.int32),
            pltpu.VMEM(tile, f32),
            pltpu.VMEM(wide, f32),
            pltpu.VMEM(tile, f32),
            pltpu.VMEM(tile, f32),
            pltpu.VMEM(tile, f32),
            pltpu.VMEM(tile, f32),
            pltpu.VMEM(tile, f32),
            pltpu.VMEM(tile, f32),
            pltpu.VMEM((TILES, 16, 8, LANES), f32),
            pltpu.VMEM((TILES, 16, 8, LANES), f32),
            pltpu.VMEM((TILES, 4, 8, LANES), f32),
            pltpu.VMEM((TILES, 4, 8, LANES), f32),
            pltpu.VMEM((3, STEPS + 1, 8, cols), f32),
            pltpu.VMEM(tile, f32),
            pltpu.VMEM(wide, f32),
            pltpu.VMEM(wide, f32),
            pltpu.VMEM((STEPS, 8, cols), f32),
            pltpu.VMEM((STEPS, 8, cols), f32),
            pltpu.VMEM((STEPS, 8, cols), f32),
            pltpu.VMEM((2, 8, LANES), f32),
            pltpu.VMEM((2, 8, LANES), f32),
            pltpu.VMEM((128, LANES), f32),
            pltpu.VMEM((nz, 16, LANES), f32),
            pltpu.VMEM((nx, 16, LANES), f32),
            pltpu.VMEM((ny, 8, LANES), f32),
            pltpu.VMEM((nz, 8, LANES), f32),
            pltpu.VMEM((nx, 8, LANES), f32),
            pltpu.VMEM((ny, 8, LANES), f32),
            pltpu.VMEM((3, 8, LANES), f32),
            pltpu.SemaphoreType.DMA((40,)),
            pltpu.SemaphoreType.DMA((6,)),
            pltpu.SemaphoreType.DMA((6,)),
            pltpu.SemaphoreType.DMA((far,)),
            pltpu.SemaphoreType.DMA((far,)),
            pltpu.SemaphoreType.DMA((24,)),
        ],
        compiler_params=pltpu.CompilerParams(collective_id=0, has_side_effects=True),
    )(*(a.reshape(shape) for a in (depth, momentum_x, momentum_y, bed, wet)))
    corr, flux_u, flux_v = (a.reshape(rows, cols) for a in results)
    return (depth - corr, flux_u / depth, flux_v / depth)


def solution(mesh):
    ngx, ny = mesh.shape["gx"], mesh.shape["gy"]
    nz = 8 if ngx % 8 == 0 else max(1, ngx // 2)
    sizes = (ngx // nz, nz, ny)
    scale = (4096 / 4.0) ** 2 / 3.0
    place = P("gx", "gy")
    return jax.shard_map(
        functools.partial(predictor, sizes, 1.0 / scale),
        mesh=mesh,
        in_specs=(place,) * 5,
        out_specs=(place,) * 3,
        check_vma=False,
    )
```

```python
import functools

import jax
import jax.numpy as jnp
from jax import lax
from jax.experimental import pallas as pl
from jax.experimental.pallas import tpu as pltpu
from jax.sharding import PartitionSpec as P

MESH = pl.DeviceIdType.MESH
GRAVITY = 9.81
ROOT_G = GRAVITY**0.5
RATIO = 0.05
LANES = 128
TILES = 4
STEPS = 16
PITCH = 20
f32 = jnp.float32


def minmod(a, c):
    return jnp.maximum(jnp.minimum(a, c), 0.0) + jnp.minimum(jnp.maximum(a, c), 0.0)


def face_flux(lefts, rights, opened):
    hl, pl_, ql = lefts
    hr, pr, qr = rights
    sl = jnp.where(opened, hl, 1.0)
    sr = jnp.where(opened, hr, 1.0)
    il = lax.rsqrt(sl)
    ir = lax.rsqrt(sr)
    ul = pl_ * (il * il)
    ur = pr * (ir * ir)
    fast = jnp.maximum(
        jnp.abs(ul) + (ROOT_G * sl) * il, jnp.abs(ur) + (ROOT_G * sr) * ir
    )
    factor = jnp.where(opened, 0.5 * RATIO, 0.0)
    mass = (pl_ + pr) - fast * (hr - hl)
    normal = (pl_ * ul + pr * ur) + (0.5 * GRAVITY) * (sl * sl + sr * sr) - fast * (pr - pl_)
    across = (ql * ul + qr * ur) - fast * (qr - ql)
    return factor * mass, factor * normal, factor * across


def lane_up(tiles, lane):
    n = len(tiles)
    rolled = [pltpu.roll(t, LANES - 1, 1) for t in tiles]
    return [jnp.where(lane == LANES - 1, rolled[(i + 1) % n], rolled[i]) for i in range(n)]


def lane_down(tiles, lane):
    n = len(tiles)
    rolled = [pltpu.roll(t, 1, 1) for t in tiles]
    return [jnp.where(lane == 0, rolled[(i - 1) % n], rolled[i]) for i in range(n)]


def matmul2(m, a):
    m11, m12, m21, m22 = m
    a11, a12, a21, a22 = a
    return (
        m11 * a11 + m12 * a21,
        m11 * a12 + m12 * a22,
        m21 * a11 + m22 * a21,
        m21 * a12 + m22 * a22,
    )


def apply2(m, v):
    return (m[0] * v[0] + m[1] * v[1], m[2] * v[0] + m[3] * v[1])


def shifted(values, k, sub, first):
    return tuple(
        jnp.where(sub >= k, pltpu.roll(v, k, 0), f) for v, f in zip(values, first)
    )


IDENT = (1.0, 0.0, 0.0, 1.0)


def scan_matrices(m, sub):
    windows = []
    for k in (1, 2, 4):
        windows.append(m)
        m = matmul2(m, shifted(m, k, sub, IDENT))
    return windows, m, shifted(m, 1, sub, IDENT)


def scan_vectors(windows, v, sub):
    for k, m in zip((1, 2, 4), windows):
        moved = apply2(m, shifted(v, k, sub, (0.0, 0.0)))
        v = (v[0] + moved[0], v[1] + moved[1])
    return v, shifted(v, 1, sub, (0.0, 0.0))


def kernel(
    sizes, spring,
    h_in, p_in, q_in, b_in, m_in,
    corr_out, u_out, v_out,
    fields, wetc, csx, cty, ax, bx, cx, ay, by, cy, win_x, win_y, pre_x, pre_y,
    faces, qs, qt, vt, os_n, os_u, os_v, ys, edges, got, seq, fix, fixed,
    coef_z, coef_x, coef_y, rhs_z, rhs_x, rhs_y, row_y,
    load_sem, halo_send, halo_recv, far_send, far_recv, out_sem,
):
    nx, nz, ny = sizes
    gx = lax.axis_index("gx")
    gy = lax.axis_index("gy")
    xi = lax.div(gx, nz)
    zi = lax.rem(gx, nz)
    ngx = nx * nz

    x_up = (lax.rem(gx + 1, ngx), gy)
    x_dn = (lax.rem(gx + ngx - 1, ngx), gy)
    y_up = (gx, lax.rem(gy + 1, ny))
    y_dn = (gx, lax.rem(gy + ny - 1, ny))
    z_mates = [(xi * nz + lax.rem(zi + k, nz), gy) for k in range(1, nz)]
    x_mates = [(lax.rem(xi + k, nx) * nz + zi, gy) for k in range(1, nx)]
    y_mates = [(gx, lax.rem(gy + k, ny)) for k in range(1, ny)]

    barrier = pltpu.get_barrier_semaphore()
    peers = [x_up, x_dn] + z_mates + x_mates + y_mates
    for peer in peers:
        pl.semaphore_signal(barrier, inc=1, device_id=peer, device_id_type=MESH)

    loads = []
    for i, src in enumerate((h_in, p_in, q_in, b_in, m_in)):
        for s in range(8):
            rows = pl.ds(2, STEPS)
            dst = fields.at[i, rows, s, :] if i < 4 else wetc.at[rows, s, :]
            copy = pltpu.make_async_copy(src.at[s], dst, load_sem.at[8 * i + s])
            copy.start()
            loads.append(copy)

    sub = lax.broadcasted_iota(jnp.int32, (8, LANES), 0)
    lane = lax.broadcasted_iota(jnp.int32, (8, LANES), 1)
    zero = jnp.where(lane + sub < 0, 1.0, 0.0)
    one = jnp.where(lane + sub < 0, 0.0, 1.0)
    cols = [pl.ds(LANES * l, LANES) for l in range(TILES)]

    def block(t):
        return pl.ds(pl.multiple_of(8 * t, 8), 8)

    for copy in loads[:8]:
        copy.wait()

    def start_pieces():
        return tuple((one, zero, zero, one) for _ in range(TILES))

    def coef_step_x(t, carry):
        out = []
        for l in range(TILES):
            ua, ga, ub, gb = carry[l]
            h = fields[0, t + 2, :, cols[l]]
            c = spring / (h * h)
            csx[l, block(t), :] = c
            ua = ua + ga
            ub = ub + gb
            ax[l, block(t), :] = ua
            bx[l, block(t), :] = ub
            out.append((ua, ga + c * ua, ub, gb + c * ub))
        return tuple(out)

    ends = lax.fori_loop(0, STEPS, coef_step_x, start_pieces(), unroll=2)
    for l in range(TILES):
        ua, ga, ub, gb = ends[l]
        windows, total, before = scan_matrices((ua, ub, ga, gb), sub)
        for k in range(3):
            for e in range(4):
                win_x[l, 4 * k + e] = windows[k][e]
        for e in range(4):
            pre_x[l, e] = before[e]
        f = 1.0 / total[3]
        coef_x_row = (f, total[1] * f, total[2] * f)
        for e in range(3):
            coef_z[zi, 4 * e + l : 4 * e + l + 1, :] = coef_x_row[e][7:8, :]
            win_x[l, 12 + e] = coef_x_row[e]

    def turn(dst, value):
        for s in range(8):
            dst[PITCH * s : PITCH * s + STEPS, :] = value[STEPS * s : STEPS * (s + 1), :]

    for l in range(TILES):
        turn(cty.at[l], csx[l].T)

    def coef_step_y(t, carry):
        out = []
        for l in range(TILES):
            ua, ga, ub, gb = carry[l]
            c = cty[l, pl.ds(t, 8, stride=PITCH), :]
            ua = ua + ga
            ub = ub + gb
            ay[l, block(t), :] = ua
            by[l, block(t), :] = ub
            out.append((ua, ga + c * ua, ub, gb + c * ub))
        return tuple(out)

    ends = lax.fori_loop(0, STEPS, coef_step_y, start_pieces(), unroll=2)
    total_y = None
    for l in range(TILES):
        ua, ga, ub, gb = ends[l]
        windows, total, before = scan_matrices((ua, ub, ga, gb), sub)
        for k in range(3):
            for e in range(4):
                win_y[l, 4 * k + e] = windows[k][e]
        for e in range(4):
            pre_y[l, e] = before[e]
            win_y[l, 12 + e] = total[e]
        total_y = total if total_y is None else matmul2(total, total_y)
    f = 1.0 / total_y[3]
    coef_y_row = (f, total_y[1] * f, total_y[2] * f)
    for e in range(3):
        coef_y[gy, e : e + 1, :] = coef_y_row[e][7:8, :]
        row_y[e] = coef_y_row[e]

    seq[...] = jnp.zeros((5, 24, LANES), f32)
    fix[...] = jnp.zeros((3, 128, LANES), f32)

    for copy in loads[8:]:
        copy.wait()

    full_lane = lax.broadcasted_iota(jnp.int32, (128, LANES), 1)

    def edge(i, l):
        if i < 4:
            return fields[i, 2 : 2 + STEPS, :, cols[l]].reshape(128, LANES)
        return wetc[2 : 2 + STEPS, :, cols[l]].reshape(128, LANES).astype(f32)

    packed = jnp.where(full_lane < 64, edge(0, 0), edge(0, TILES - 1))
    for i in range(1, 5):
        width = 4 * i
        low = pltpu.roll(edge(i, 0), width, 1)
        high = pltpu.roll(edge(i, TILES - 1), LANES - width, 1)
        packed = jnp.where((full_lane >= width) & (full_lane < 64), low, packed)
        packed = jnp.where((full_lane >= 64) & (full_lane < LANES - width), high, packed)
    edges[...] = packed.T

    pl.semaphore_wait(barrier, len(peers))

    def remote(src, dst, send, recv, device):
        copy = pltpu.make_async_remote_copy(
            src_ref=src, dst_ref=dst, send_sem=send, recv_sem=recv,
            device_id=device, device_id_type=MESH,
        )
        copy.start()
        return copy

    first, last = pl.ds(2, 2), pl.ds(STEPS, 2)
    past, ahead = pl.ds(0, 2), pl.ds(STEPS + 2, 2)
    halos_x = [
        remote(fields.at[:, first, 0, :], fields.at[:, ahead, 7, :],
               halo_send.at[0], halo_recv.at[0], x_dn),
        remote(fields.at[:, last, 7, :], fields.at[:, past, 0, :],
               halo_send.at[1], halo_recv.at[1], x_up),
        remote(wetc.at[first, 0, :], wetc.at[ahead, 7, :],
               halo_send.at[2], halo_recv.at[2], x_dn),
        remote(wetc.at[last, 7, :], wetc.at[past, 0, :],
               halo_send.at[3], halo_recv.at[3], x_up),
    ]
    halos_y = [
        remote(edges.at[pl.ds(0, 24), :], got.at[0], halo_send.at[4], halo_recv.at[4], y_dn),
        remote(edges.at[pl.ds(104, 24), :], got.at[1], halo_send.at[5], halo_recv.at[5], y_up),
    ]

    def gather(buf, slot, mates, base):
        return [
            remote(buf.at[slot], buf.at[slot], far_send.at[base + i], far_recv.at[base + i], mate)
            for i, mate in enumerate(mates)
        ]

    sent = list(halos_x) + list(halos_y)
    base_y = nz - 1
    base_x = base_y + ny - 1
    half = base_x + nx - 1

    coef_z_copies = gather(coef_z, zi, z_mates, 0)
    coef_y_copies = gather(coef_y, gy, y_mates, base_y)
    sent += coef_z_copies + coef_y_copies

    def x_faces(col, dst, start, count):
        w = [[fields[i, start + d, :, col] for d in range(4)] for i in range(3)]
        diff = [[0.5 * (w[i][d + 1] - w[i][d]) for d in range(3)] for i in range(3)]
        slope = [minmod(diff[i][0], diff[i][1]) for i in range(3)]
        for k in range(count):
            lefts, rights = [], []
            for i in range(3):
                after = minmod(diff[i][1], diff[i][2])
                lefts.append(w[i][1] + slope[i])
                rights.append(w[i][2] - after)
                slope[i] = after
                if k + 1 < count:
                    new = fields[i, start + k + 4, :, col]
                    w[i] = [None, w[i][2], w[i][3], new]
                    diff[i] = [None, diff[i][2], 0.5 * (new - w[i][2])]
            m0 = wetc[start + k + 1, :, col]
            m1 = wetc[start + k + 2, :, col]
            flux = face_flux(lefts, rights, (m0 * m1) > 0)
            for i in range(3):
                faces[i, start + k, :, col] = flux[i]

    def interior(l, carry):
        x_faces(pl.ds(pl.multiple_of(LANES * l, LANES), LANES), None, 2, STEPS - 3)
        return carry

    lax.fori_loop(0, TILES, interior, 0)

    push_factor = 0.5 * RATIO * GRAVITY

    def y_inner(t, carry):
        values = [[fields[i, t + 2, :, c] for c in cols] for i in range(3)]
        wet = [wetc[t + 2, :, c].astype(f32) for c in cols]
        opened = [(a * b) > 0.5 for a, b in zip(wet, lane_up(wet, lane))]
        lefts, rights = [], []
        for i in (0, 2, 1):
            w = values[i]
            diff = [0.5 * (a - b) for a, b in zip(lane_up(w, lane), w)]
            slope = [minmod(a, b) for a, b in zip(lane_down(diff, lane), diff)]
            lefts.append([a + s for a, s in zip(w, slope)])
            rights.append(lane_up([a - s for a, s in zip(w, slope)], lane))
        flux = [
            face_flux([x[l] for x in lefts], [x[l] for x in rights], opened[l])
            for l in range(TILES)
        ]
        bed = [fields[3, t + 2, :, c] for c in cols]
        bed_next = lane_up(bed, lane)
        bed_past = lane_down(bed, lane)
        for k, i in ((0, 0), (1, 2), (2, 1)):
            line = [flux[l][i] for l in range(TILES)]
            for l, before in enumerate(lane_down(line, lane)):
                grad = line[l] - before
                if k == 2:
                    grad = grad + (push_factor * values[0][l]) * (bed_next[l] - bed_past[l])
                ys[k, t, :, cols[l]] = grad
        return carry

    lax.fori_loop(0, STEPS, y_inner, 0)

    for copy in halos_x:
        copy.wait_recv()

    def fill(ref, kind, both):
        for l in range(TILES):
            for t, source, rim, shift in (
                (0, STEPS, 0, 1), (1, STEPS + 1, 0, 1),
                (STEPS + 2, 2, 7, 7), (STEPS + 3, 3, 7, 7),
            ):
                if not both and t in (0, STEPS + 3):
                    continue
                gone = gx == 0 if rim == 0 else gx == ngx - 1
                border = jnp.where(gone, jnp.zeros((), kind), ref[t, :, cols[l]])
                ref[t, :, cols[l]] = jnp.where(
                    sub == rim, border, pltpu.roll(ref[source, :, cols[l]], shift, 0)
                )

    for i in range(4):
        fill(fields.at[i], f32, i < 3)
    fill(wetc, jnp.int32, False)

    def rim_faces(l, carry):
        col = pl.ds(pl.multiple_of(LANES * l, LANES), LANES)
        x_faces(col, None, 0, 2)
        x_faces(col, None, STEPS - 1, 2)
        return carry

    lax.fori_loop(0, TILES, rim_faces, 0)

    for copy in halos_y:
        copy.wait_recv()
    for i in range(5):
        low, high = 4 * i, LANES - 4 * i
        seq[i, 0:2, :] = jnp.where(gy > 0, got[1, 22 - low : 24 - low, :], 0.0)
        seq[i, 2:6, :] = edges[low : low + 4, :]
        seq[i, 8:12, :] = edges[high - 4 : high, :]
        seq[i, 12:14, :] = jnp.where(gy < ny - 1, got[0, low : low + 2, :], 0.0)

    def rows_of(i, d):
        return seq[i, d : d + 16, :]

    lefts, rights = [], []
    for i in (0, 2, 1):
        w = [rows_of(i, d) for d in range(4)]
        diff = [0.5 * (w[d + 1] - w[d]) for d in range(3)]
        lefts.append(w[1] + minmod(diff[0], diff[1]))
        rights.append(w[2] - minmod(diff[1], diff[2]))
    flux = face_flux(lefts, rights, (rows_of(4, 1) * rows_of(4, 2)) > 0.5)
    for k, i in ((0, 0), (1, 2), (2, 1)):
        grad = pltpu.roll(flux[i], 15, 0) - flux[i]
        if k == 2:
            grad = grad + (push_factor * rows_of(0, 2)) * (rows_of(3, 3) - rows_of(3, 1))
        fix[k, 0:2, :] = grad[0:2, :]
        fix[k, 126:128, :] = grad[8:10, :]
    for k in (1, 0, 2):
        fixed[k] = fix[k].T

    def y_grad(k, t, l):
        grad = ys[k, t, :, cols[l]]
        if l == 0:
            return jnp.where(lane < 2, fixed[k, block(t), :], grad)
        if l == TILES - 1:
            return jnp.where(lane >= LANES - 2, fixed[k, block(t), :], grad)
        return grad

    def push_x(t, carry):
        out = []
        for l in range(TILES):
            uc, gc = carry[l]
            c = cols[l]
            m = wetc[t + 2, :, c].astype(f32)
            flow = faces[1, t + 1, :, c] - faces[1, t, :, c]
            rise = fields[3, t + 3, :, c] - fields[3, t + 1, :, c]
            px = m * (
                fields[1, t + 2, :, c] - flow - y_grad(1, t, l)
                - (push_factor * fields[0, t + 2, :, c]) * rise
            )
            uc = uc + gc
            cx[l, block(t), :] = uc
            out.append((uc, gc + csx[l, block(t), :] * (uc - px)))
        return tuple(out)

    rest = tuple((zero, zero) for _ in range(TILES))
    ends = lax.fori_loop(0, STEPS, push_x, rest, unroll=4)

    before_x = []
    for l in range(TILES):
        windows = [[win_x[l, 4 * k + e] for e in range(4)] for k in range(3)]
        total, before = scan_vectors(windows, ends[l], sub)
        before_x.append(before)
        f, tau = win_x[l, 12], win_x[l, 13]
        rhs_z[zi, l : l + 1, :] = (total[0] - tau * total[1])[7:8, :]
        rhs_z[zi, 4 + l : 5 + l, :] = (-(f * total[1]))[7:8, :]
    rhs_z_copies = gather(rhs_z, zi, z_mates, half)
    sent += rhs_z_copies

    def depth_and_q(t, carry):
        for l in range(TILES):
            c = cols[l]
            m = wetc[t + 2, :, c].astype(f32)
            os_n[t, :, c] = m * (faces[0, t + 1, :, c] - faces[0, t, :, c] + y_grad(0, t, l))
            flow = faces[2, t + 1, :, c] - faces[2, t, :, c]
            qs[l, block(t), :] = m * (fields[2, t + 2, :, c] - flow - y_grad(2, t, l))
        return carry

    lax.fori_loop(0, STEPS, depth_and_q, 0, unroll=2)

    def store_out(staged, out, base):
        copies = [
            pltpu.make_async_copy(staged.at[:, s, :], out.at[s], out_sem.at[base + s])
            for s in range(8)
        ]
        for copy in copies:
            copy.start()
        return copies

    outs = store_out(os_n, corr_out, 0)

    for l in range(TILES):
        turn(qt.at[l], qs[l].T)

    def rhs_step_y(t, carry):
        out = []
        for l in range(TILES):
            uc, gc = carry[l]
            where = pl.ds(t, 8, stride=PITCH)
            uc = uc + gc
            cy[l, block(t), :] = uc
            out.append((uc, gc + cty[l, where, :] * (uc - qt[l, where, :])))
        return tuple(out)

    ends = lax.fori_loop(0, STEPS, rhs_step_y, rest, unroll=2)
    before_y, totals_y = [], []
    sum_y = None
    for l in range(TILES):
        windows = [[win_y[l, 4 * k + e] for e in range(4)] for k in range(3)]
        total, before = scan_vectors(windows, ends[l], sub)
        before_y.append(before)
        totals_y.append(total)
        if sum_y is None:
            sum_y = total
        else:
            moved = apply2([win_y[l, 12 + e] for e in range(4)], sum_y)
            sum_y = (total[0] + moved[0], total[1] + moved[1])
    rhs_y[gy, 0:1, :] = (sum_y[0] - row_y[1] * sum_y[1])[7:8, :]
    rhs_y[gy, 1:2, :] = (-(row_y[0] * sum_y[1]))[7:8, :]
    rhs_y_copies = gather(rhs_y, gy, y_mates, half + base_y)
    sent += rhs_y_copies

    for copy in coef_z_copies:
        copy.wait_recv()

    def port(buf, k):
        return buf[k, 0:4, :], buf[k, 4:8, :], buf[k, 8:12, :]

    group_steps = []
    f, tau, mu = port(coef_z, 0)
    for k in range(1, nz):
        fk, tk, mk = port(coef_z, k)
        inv = 1.0 / (1.0 + tau * mk)
        a = fk * inv
        d = f * inv
        group_steps.append((a, a * tau, d, d * mk))
        f, tau, mu = f * a, tk + fk * (a * tau), mu + f * (d * mk)
    coef_x[xi, 0:4, :] = f
    coef_x[xi, 4:8, :] = tau
    coef_x[xi, 8:12, :] = mu
    coef_x_copies = gather(coef_x, xi, x_mates, base_x)
    sent += coef_x_copies

    def left_chain(ports, mine, rho):
        steps = []
        for k in range(len(ports)):
            fk, tk, mk = ports[k]
            inv = 1.0 / (1.0 + rho * mk)
            a = fk * inv
            steps.append((a, a * rho))
            rho = jnp.where(k < mine, tk + fk * (a * rho), rho)
        return rho, steps

    def right_chain(ports, mine, back):
        steps = [None] * len(ports)
        for k in reversed(range(len(ports))):
            fk, tk, mk = ports[k]
            inv = 1.0 / (1.0 + tk * back)
            a = fk * inv
            steps[k] = (a, a * back)
            back = jnp.where(k >= mine, mk + fk * (a * back), back)
        return back, steps

    def left_values(steps, rhs, mine, w):
        for k in range(len(steps)):
            a, b = steps[k]
            w1, w2 = rhs[k]
            w = jnp.where(k < mine, w1 + a * w + b * w2, w)
        return w

    def right_values(steps, rhs, mine, w):
        for k in reversed(range(len(steps))):
            a, b = steps[k]
            w1, w2 = rhs[k]
            w = jnp.where(k >= mine, w2 + a * w - b * w1, w)
        return w

    def meet(rho, back, wl, wr):
        inv = 1.0 / (1.0 + rho * back)
        return (rho * wr + wl) * inv, (wr - back * wl) * inv

    for copy in coef_y_copies:
        copy.wait_recv()
    ports_y = [tuple(coef_y[k, e : e + 1, :] for e in range(3)) for k in range(ny)]
    row_zero = jnp.zeros((1, LANES), f32)
    rho_y, left_y = left_chain(ports_y, gy, row_zero)
    back_y, right_y = right_chain(ports_y, gy, row_zero + 1.0)

    for copy in coef_x_copies:
        copy.wait_recv()
    ports_x = [port(coef_x, k) for k in range(nx)]
    ports_z = [port(coef_z, k) for k in range(nz)]
    four_zero = jnp.zeros((4, LANES), f32)
    rho_x, left_x = left_chain(ports_x, xi, four_zero)
    back_x, right_x = right_chain(ports_x, xi + 1, four_zero + 1.0)
    rho_z, left_z = left_chain(ports_z, zi, rho_x)
    back_z, right_z = right_chain(ports_z, zi, back_x)

    for copy in rhs_z_copies:
        copy.wait_recv()
    rhs_in_z = [(rhs_z[k, 0:4, :], rhs_z[k, 4:8, :]) for k in range(nz)]
    w1, w2 = rhs_in_z[0]
    for k in range(1, nz):
        a, at, d, dm = group_steps[k - 1]
        k1, k2 = rhs_in_z[k]
        w1, w2 = k1 + a * w1 + at * k2, w2 + d * k2 - dm * w1
    rhs_x[xi, 0:4, :] = w1
    rhs_x[xi, 4:8, :] = w2
    rhs_x_copies = gather(rhs_x, xi, x_mates, half + base_x)
    sent += rhs_x_copies

    for copy in rhs_y_copies:
        copy.wait_recv()
    rhs_in_y = [(rhs_y[k, 0:1, :], rhs_y[k, 1:2, :]) for k in range(ny)]
    wl = left_values(left_y, rhs_in_y, gy, row_zero)
    wr = right_values(right_y, rhs_in_y, gy, row_zero)
    state = meet(rho_y, back_y, wl, wr)
    starts = []
    for l in range(TILES):
        before = [pre_y[l, e] for e in range(4)]
        wide = tuple(jnp.broadcast_to(s, (8, LANES)) for s in state)
        moved = apply2(before, wide)
        starts.append((moved[0] + before_y[l][0], moved[1] + before_y[l][1]))
        if l < TILES - 1:
            moved = apply2([win_y[l, 12 + e] for e in range(4)], wide)
            state = tuple((moved[e] + totals_y[l][e])[7:8, :] for e in range(2))

    def finish_y(t, carry):
        for l in range(TILES):
            at = block(t)
            vt[l, pl.ds(t, 8, stride=PITCH), :] = (
                ay[l, at, :] * starts[l][0] + by[l, at, :] * starts[l][1] + cy[l, at, :]
            )
        return carry

    lax.fori_loop(0, STEPS, finish_y, 0, unroll=2)
    for l in range(TILES):
        line = [vt[l, PITCH * s : PITCH * s + STEPS, :] for s in range(8)]
        os_v[:, :, cols[l]] = jnp.concatenate(line, axis=0).T.reshape(STEPS, 8, LANES)
    outs += store_out(os_v, v_out, 8)

    for copy in rhs_x_copies:
        copy.wait_recv()
    rhs_in_x = [(rhs_x[k, 0:4, :], rhs_x[k, 4:8, :]) for k in range(nx)]
    wl = left_values(left_x, rhs_in_x, xi, four_zero)
    wr = right_values(right_x, rhs_in_x, xi + 1, four_zero)
    wl = left_values(left_z, rhs_in_z, zi, wl)
    wr = right_values(right_z, rhs_in_z, zi, wr)
    state = meet(rho_z, back_z, wl, wr)
    for l in range(TILES):
        before = [pre_x[l, e] for e in range(4)]
        wide = tuple(jnp.broadcast_to(s[l : l + 1, :], (8, LANES)) for s in state)
        moved = apply2(before, wide)
        u0, g0 = moved[0] + before_x[l][0], moved[1] + before_x[l][1]
        for t in range(STEPS):
            at = pl.ds(8 * t, 8)
            os_u[t, :, cols[l]] = ax[l, at, :] * u0 + bx[l, at, :] * g0 + cx[l, at, :]
    outs += store_out(os_u, u_out, 16)

    for copy in sent:
        copy.wait_send()
    for copy in outs:
        copy.wait()


def predictor(sizes, spring, depth, momentum_x, momentum_y, bed, wet):
    nx, nz, ny = sizes
    rows, cols = depth.shape
    shape = (8, STEPS, cols)
    flat = jax.ShapeDtypeStruct(shape, f32)
    hbm = pl.BlockSpec(memory_space=pl.ANY)
    tile = (TILES, 128, LANES)
    wide = (TILES, 8 * PITCH, LANES)
    far = 2 * (nz + nx + ny - 3)
    results = pl.pallas_call(
        functools.partial(kernel, sizes, spring),
        out_shape=(flat, flat, flat),
        in_specs=[hbm] * 5,
        out_specs=[hbm] * 3,
        scratch_shapes=[
            pltpu.VMEM((4, STEPS + 4, 8, cols), f32),
            pltpu.VMEM((STEPS + 4, 8, cols), jnp.int32),
            pltpu.VMEM(tile, f32),
            pltpu.VMEM(wide, f32),
            pltpu.VMEM(tile, f32),
            pltpu.VMEM(tile, f32),
            pltpu.VMEM(tile, f32),
            pltpu.VMEM(tile, f32),
            pltpu.VMEM(tile, f32),
            pltpu.VMEM(tile, f32),
            pltpu.VMEM((TILES, 16, 8, LANES), f32),
            pltpu.VMEM((TILES, 16, 8, LANES), f32),
            pltpu.VMEM((TILES, 4, 8, LANES), f32),
            pltpu.VMEM((TILES, 4, 8, LANES), f32),
            pltpu.VMEM((3, STEPS + 1, 8, cols), f32),
            pltpu.VMEM(tile, f32),
            pltpu.VMEM(wide, f32),
            pltpu.VMEM(wide, f32),
            pltpu.VMEM((STEPS, 8, cols), f32),
            pltpu.VMEM((STEPS, 8, cols), f32),
            pltpu.VMEM((STEPS, 8, cols), f32),
            pltpu.VMEM((3, STEPS, 8, cols), f32),
            pltpu.VMEM((128, LANES), f32),
            pltpu.VMEM((2, 24, LANES), f32),
            pltpu.VMEM((5, 24, LANES), f32),
            pltpu.VMEM((3, 128, LANES), f32),
            pltpu.VMEM((3, 128, LANES), f32),
            pltpu.VMEM((nz, 16, LANES), f32),
            pltpu.VMEM((nx, 16, LANES), f32),
            pltpu.VMEM((ny, 8, LANES), f32),
            pltpu.VMEM((nz, 8, LANES), f32),
            pltpu.VMEM((nx, 8, LANES), f32),
            pltpu.VMEM((ny, 8, LANES), f32),
            pltpu.VMEM((3, 8, LANES), f32),
            pltpu.SemaphoreType.DMA((40,)),
            pltpu.SemaphoreType.DMA((6,)),
            pltpu.SemaphoreType.DMA((6,)),
            pltpu.SemaphoreType.DMA((far,)),
            pltpu.SemaphoreType.DMA((far,)),
            pltpu.SemaphoreType.DMA((24,)),
        ],
        compiler_params=pltpu.CompilerParams(collective_id=0, has_side_effects=True),
    )(*(a.reshape(shape) for a in (depth, momentum_x, momentum_y, bed, wet)))
    corr, flux_u, flux_v = (a.reshape(rows, cols) for a in results)
    return (depth - corr, flux_u / depth, flux_v / depth)


def solution(mesh):
    ngx, ny = mesh.shape["gx"], mesh.shape["gy"]
    nz = 8 if ngx % 8 == 0 else max(1, ngx // 2)
    sizes = (ngx // nz, nz, ny)
    scale = (4096 / 4.0) ** 2 / 3.0
    place = P("gx", "gy")
    return jax.shard_map(
        functools.partial(predictor, sizes, 1.0 / scale),
        mesh=mesh,
        in_specs=(place,) * 5,
        out_specs=(place,) * 3,
        check_vma=False,
    )
```

```python
import functools

import jax
import jax.numpy as jnp
from jax import lax
from jax.experimental import pallas as pl
from jax.experimental.pallas import tpu as pltpu
from jax.sharding import PartitionSpec as P

MESH = pl.DeviceIdType.MESH
GRAVITY = 9.81
ROOT_G = GRAVITY**0.5
RATIO = 0.05
LANES = 128
TILES = 4
STEPS = 16
PITCH = 20
f32 = jnp.float32


def minmod(a, c):
    return jnp.maximum(jnp.minimum(a, c), 0.0) + jnp.minimum(jnp.maximum(a, c), 0.0)


def face_flux(lefts, rights, opened):
    hl, pl_, ql = lefts
    hr, pr, qr = rights
    sl = jnp.where(opened, hl, 1.0)
    sr = jnp.where(opened, hr, 1.0)
    il = lax.rsqrt(sl)
    ir = lax.rsqrt(sr)
    ul = pl_ * (il * il)
    ur = pr * (ir * ir)
    fast = jnp.maximum(
        jnp.abs(ul) + (ROOT_G * sl) * il, jnp.abs(ur) + (ROOT_G * sr) * ir
    )
    factor = jnp.where(opened, 0.5 * RATIO, 0.0)
    mass = (pl_ + pr) - fast * (hr - hl)
    normal = (pl_ * ul + pr * ur) + (0.5 * GRAVITY) * (sl * sl + sr * sr) - fast * (pr - pl_)
    across = (ql * ul + qr * ur) - fast * (qr - ql)
    return factor * mass, factor * normal, factor * across


def lane_up(tiles, lane):
    n = len(tiles)
    rolled = [pltpu.roll(t, LANES - 1, 1) for t in tiles]
    return [jnp.where(lane == LANES - 1, rolled[(i + 1) % n], rolled[i]) for i in range(n)]


def lane_down(tiles, lane):
    n = len(tiles)
    rolled = [pltpu.roll(t, 1, 1) for t in tiles]
    return [jnp.where(lane == 0, rolled[(i - 1) % n], rolled[i]) for i in range(n)]


def matmul2(m, a):
    m11, m12, m21, m22 = m
    a11, a12, a21, a22 = a
    return (
        m11 * a11 + m12 * a21,
        m11 * a12 + m12 * a22,
        m21 * a11 + m22 * a21,
        m21 * a12 + m22 * a22,
    )


def apply2(m, v):
    return (m[0] * v[0] + m[1] * v[1], m[2] * v[0] + m[3] * v[1])


def shifted(values, k, sub, first):
    return tuple(
        jnp.where(sub >= k, pltpu.roll(v, k, 0), f) for v, f in zip(values, first)
    )


IDENT = (1.0, 0.0, 0.0, 1.0)


def scan_matrices(m, sub):
    windows = []
    for k in (1, 2, 4):
        windows.append(m)
        m = matmul2(m, shifted(m, k, sub, IDENT))
    return windows, m, shifted(m, 1, sub, IDENT)


def scan_vectors(windows, v, sub):
    for k, m in zip((1, 2, 4), windows):
        moved = apply2(m, shifted(v, k, sub, (0.0, 0.0)))
        v = (v[0] + moved[0], v[1] + moved[1])
    return v, shifted(v, 1, sub, (0.0, 0.0))


def kernel(
    sizes, spring,
    h_in, p_in, q_in, b_in, m_in,
    corr_out, u_out, v_out,
    fields, wetc, csx, cty, ax, bx, cx, ay, by, cy, win_x, win_y, pre_x, pre_y,
    faces, qs, qt, vt, os_n, os_u, os_v, ys, edges, got, seq, fix, fixed,
    coef_z, coef_x, coef_y, rhs_z, rhs_x, rhs_y, row_y,
    load_sem, halo_send, halo_recv, far_send, far_recv, out_sem,
):
    nx, nz, ny = sizes
    gx = lax.axis_index("gx")
    gy = lax.axis_index("gy")
    xi = lax.div(gx, nz)
    zi = lax.rem(gx, nz)
    ngx = nx * nz

    x_up = (lax.rem(gx + 1, ngx), gy)
    x_dn = (lax.rem(gx + ngx - 1, ngx), gy)
    y_up = (gx, lax.rem(gy + 1, ny))
    y_dn = (gx, lax.rem(gy + ny - 1, ny))
    z_mates = [(xi * nz + lax.rem(zi + k, nz), gy) for k in range(1, nz)]
    x_mates = [(lax.rem(xi + k, nx) * nz + zi, gy) for k in range(1, nx)]
    y_mates = [(gx, lax.rem(gy + k, ny)) for k in range(1, ny)]

    barrier = pltpu.get_barrier_semaphore()
    peers = [x_up, x_dn] + z_mates + x_mates + y_mates
    for peer in peers:
        pl.semaphore_signal(barrier, inc=1, device_id=peer, device_id_type=MESH)

    loads = []
    for i, src in enumerate((h_in, p_in, q_in, b_in, m_in)):
        for s in range(8):
            rows = pl.ds(2, STEPS)
            dst = fields.at[i, rows, s, :] if i < 4 else wetc.at[rows, s, :]
            copy = pltpu.make_async_copy(src.at[s], dst, load_sem.at[8 * i + s])
            copy.start()
            loads.append(copy)

    sub = lax.broadcasted_iota(jnp.int32, (8, LANES), 0)
    lane = lax.broadcasted_iota(jnp.int32, (8, LANES), 1)
    zero = jnp.where(lane + sub < 0, 1.0, 0.0)
    one = jnp.where(lane + sub < 0, 0.0, 1.0)
    cols = [pl.ds(LANES * l, LANES) for l in range(TILES)]

    def block(t):
        return pl.ds(pl.multiple_of(8 * t, 8), 8)

    for copy in loads[:8]:
        copy.wait()

    def start_pieces():
        return tuple((one, zero, zero, one) for _ in range(TILES))

    def coef_step_x(t, carry):
        out = []
        for l in range(TILES):
            ua, ga, ub, gb = carry[l]
            h = fields[0, t + 2, :, cols[l]]
            c = spring / (h * h)
            csx[l, block(t), :] = c
            ua = ua + ga
            ub = ub + gb
            ax[l, block(t), :] = ua
            bx[l, block(t), :] = ub
            out.append((ua, ga + c * ua, ub, gb + c * ub))
        return tuple(out)

    ends = lax.fori_loop(0, STEPS, coef_step_x, start_pieces(), unroll=2)
    for l in range(TILES):
        ua, ga, ub, gb = ends[l]
        windows, total, before = scan_matrices((ua, ub, ga, gb), sub)
        for k in range(3):
            for e in range(4):
                win_x[l, 4 * k + e] = windows[k][e]
        for e in range(4):
            pre_x[l, e] = before[e]
        f = 1.0 / total[3]
        coef_x_row = (f, total[1] * f, total[2] * f)
        for e in range(3):
            coef_z[zi, 4 * e + l : 4 * e + l + 1, :] = coef_x_row[e][7:8, :]
            win_x[l, 12 + e] = coef_x_row[e]

    def turn(dst, value):
        for s in range(8):
            dst[PITCH * s : PITCH * s + STEPS, :] = value[STEPS * s : STEPS * (s + 1), :]

    for l in range(TILES):
        turn(cty.at[l], csx[l].T)

    def coef_step_y(t, carry):
        out = []
        for l in range(TILES):
            ua, ga, ub, gb = carry[l]
            c = cty[l, pl.ds(t, 8, stride=PITCH), :]
            ua = ua + ga
            ub = ub + gb
            ay[l, block(t), :] = ua
            by[l, block(t), :] = ub
            out.append((ua, ga + c * ua, ub, gb + c * ub))
        return tuple(out)

    ends = lax.fori_loop(0, STEPS, coef_step_y, start_pieces(), unroll=2)
    total_y = None
    for l in range(TILES):
        ua, ga, ub, gb = ends[l]
        windows, total, before = scan_matrices((ua, ub, ga, gb), sub)
        for k in range(3):
            for e in range(4):
                win_y[l, 4 * k + e] = windows[k][e]
        for e in range(4):
            pre_y[l, e] = before[e]
            win_y[l, 12 + e] = total[e]
        total_y = total if total_y is None else matmul2(total, total_y)
    f = 1.0 / total_y[3]
    coef_y_row = (f, total_y[1] * f, total_y[2] * f)
    for e in range(3):
        coef_y[gy, e : e + 1, :] = coef_y_row[e][7:8, :]
        row_y[e] = coef_y_row[e]

    seq[...] = jnp.zeros((5, 24, LANES), f32)
    fix[...] = jnp.zeros((3, 128, LANES), f32)

    for copy in loads[8:]:
        copy.wait()

    full_lane = lax.broadcasted_iota(jnp.int32, (128, LANES), 1)

    def edge(i, l):
        if i < 4:
            return fields[i, 2 : 2 + STEPS, :, cols[l]].reshape(128, LANES)
        return wetc[2 : 2 + STEPS, :, cols[l]].reshape(128, LANES).astype(f32)

    packed = jnp.where(full_lane < 64, edge(0, 0), edge(0, TILES - 1))
    for i in range(1, 5):
        width = 4 * i
        low = pltpu.roll(edge(i, 0), width, 1)
        high = pltpu.roll(edge(i, TILES - 1), LANES - width, 1)
        packed = jnp.where((full_lane >= width) & (full_lane < 64), low, packed)
        packed = jnp.where((full_lane >= 64) & (full_lane < LANES - width), high, packed)
    edges[...] = packed.T

    pl.semaphore_wait(barrier, len(peers))

    def remote(src, dst, send, recv, device):
        copy = pltpu.make_async_remote_copy(
            src_ref=src, dst_ref=dst, send_sem=send, recv_sem=recv,
            device_id=device, device_id_type=MESH,
        )
        copy.start()
        return copy

    first, last = pl.ds(2, 2), pl.ds(STEPS, 2)
    past, ahead = pl.ds(0, 2), pl.ds(STEPS + 2, 2)
    halos_x = [
        remote(fields.at[:, first, 0, :], fields.at[:, ahead, 7, :],
               halo_send.at[0], halo_recv.at[0], x_dn),
        remote(fields.at[:, last, 7, :], fields.at[:, past, 0, :],
               halo_send.at[1], halo_recv.at[1], x_up),
        remote(wetc.at[first, 0, :], wetc.at[ahead, 7, :],
               halo_send.at[2], halo_recv.at[2], x_dn),
        remote(wetc.at[last, 7, :], wetc.at[past, 0, :],
               halo_send.at[3], halo_recv.at[3], x_up),
    ]
    halos_y = [
        remote(edges.at[pl.ds(0, 24), :], got.at[0], halo_send.at[4], halo_recv.at[4], y_dn),
        remote(edges.at[pl.ds(104, 24), :], got.at[1], halo_send.at[5], halo_recv.at[5], y_up),
    ]

    def gather(buf, slot, mates, base):
        return [
            remote(buf.at[slot], buf.at[slot], far_send.at[base + i], far_recv.at[base + i], mate)
            for i, mate in enumerate(mates)
        ]

    sent = list(halos_x) + list(halos_y)
    base_y = nz - 1
    base_x = base_y + ny - 1
    half = base_x + nx - 1

    coef_z_copies = gather(coef_z, zi, z_mates, 0)
    coef_y_copies = gather(coef_y, gy, y_mates, base_y)
    sent += coef_z_copies + coef_y_copies

    def x_faces(col, dst, start, count):
        w = [[fields[i, start + d, :, col] for d in range(4)] for i in range(3)]
        diff = [[0.5 * (w[i][d + 1] - w[i][d]) for d in range(3)] for i in range(3)]
        slope = [minmod(diff[i][0], diff[i][1]) for i in range(3)]
        for k in range(count):
            lefts, rights = [], []
            for i in range(3):
                after = minmod(diff[i][1], diff[i][2])
                lefts.append(w[i][1] + slope[i])
                rights.append(w[i][2] - after)
                slope[i] = after
                if k + 1 < count:
                    new = fields[i, start + k + 4, :, col]
                    w[i] = [None, w[i][2], w[i][3], new]
                    diff[i] = [None, diff[i][2], 0.5 * (new - w[i][2])]
            m0 = wetc[start + k + 1, :, col]
            m1 = wetc[start + k + 2, :, col]
            flux = face_flux(lefts, rights, (m0 * m1) > 0)
            for i in range(3):
                faces[i, start + k, :, col] = flux[i]

    def interior(l, carry):
        x_faces(pl.ds(pl.multiple_of(LANES * l, LANES), LANES), None, 2, STEPS - 3)
        return carry

    lax.fori_loop(0, TILES, interior, 0)

    push_factor = 0.5 * RATIO * GRAVITY

    def y_inner(t, carry):
        values = [[fields[i, t + 2, :, c] for c in cols] for i in range(3)]
        wet = [wetc[t + 2, :, c].astype(f32) for c in cols]
        opened = [(a * b) > 0.5 for a, b in zip(wet, lane_up(wet, lane))]
        lefts, rights = [], []
        for i in (0, 2, 1):
            w = values[i]
            diff = [0.5 * (a - b) for a, b in zip(lane_up(w, lane), w)]
            slope = [minmod(a, b) for a, b in zip(lane_down(diff, lane), diff)]
            lefts.append([a + s for a, s in zip(w, slope)])
            rights.append(lane_up([a - s for a, s in zip(w, slope)], lane))
        flux = [
            face_flux([x[l] for x in lefts], [x[l] for x in rights], opened[l])
            for l in range(TILES)
        ]
        bed = [fields[3, t + 2, :, c] for c in cols]
        bed_next = lane_up(bed, lane)
        bed_past = lane_down(bed, lane)
        for k, i in ((0, 0), (1, 2), (2, 1)):
            line = [flux[l][i] for l in range(TILES)]
            for l, before in enumerate(lane_down(line, lane)):
                grad = line[l] - before
                if k == 2:
                    grad = grad + (push_factor * values[0][l]) * (bed_next[l] - bed_past[l])
                ys[k, t, :, cols[l]] = grad
        return carry

    lax.fori_loop(0, STEPS, y_inner, 0)

    for copy in halos_x:
        copy.wait_recv()

    def fill(ref, kind, both):
        for l in range(TILES):
            for t, source, rim, shift in (
                (0, STEPS, 0, 1), (1, STEPS + 1, 0, 1),
                (STEPS + 2, 2, 7, 7), (STEPS + 3, 3, 7, 7),
            ):
                if not both and t in (0, STEPS + 3):
                    continue
                gone = gx == 0 if rim == 0 else gx == ngx - 1
                border = jnp.where(gone, jnp.zeros((), kind), ref[t, :, cols[l]])
                ref[t, :, cols[l]] = jnp.where(
                    sub == rim, border, pltpu.roll(ref[source, :, cols[l]], shift, 0)
                )

    for i in range(4):
        fill(fields.at[i], f32, i < 3)
    fill(wetc, jnp.int32, False)

    def rim_faces(l, carry):
        col = pl.ds(pl.multiple_of(LANES * l, LANES), LANES)
        x_faces(col, None, 0, 2)
        x_faces(col, None, STEPS - 1, 2)
        return carry

    lax.fori_loop(0, TILES, rim_faces, 0)

    for copy in halos_y:
        copy.wait_recv()
    for i in range(5):
        low, high = 4 * i, LANES - 4 * i
        seq[i, 0:2, :] = jnp.where(gy > 0, got[1, 22 - low : 24 - low, :], 0.0)
        seq[i, 2:6, :] = edges[low : low + 4, :]
        seq[i, 8:12, :] = edges[high - 4 : high, :]
        seq[i, 12:14, :] = jnp.where(gy < ny - 1, got[0, low : low + 2, :], 0.0)

    def rows_of(i, d):
        return seq[i, d : d + 16, :]

    lefts, rights = [], []
    for i in (0, 2, 1):
        w = [rows_of(i, d) for d in range(4)]
        diff = [0.5 * (w[d + 1] - w[d]) for d in range(3)]
        lefts.append(w[1] + minmod(diff[0], diff[1]))
        rights.append(w[2] - minmod(diff[1], diff[2]))
    flux = face_flux(lefts, rights, (rows_of(4, 1) * rows_of(4, 2)) > 0.5)
    for k, i in ((0, 0), (1, 2), (2, 1)):
        grad = pltpu.roll(flux[i], 15, 0) - flux[i]
        if k == 2:
            grad = grad + (push_factor * rows_of(0, 2)) * (rows_of(3, 3) - rows_of(3, 1))
        fix[k, 0:2, :] = grad[0:2, :]
        fix[k, 126:128, :] = grad[8:10, :]
    for k in (1, 0, 2):
        fixed[k] = fix[k].T

    def y_grad(k, t, l):
        grad = ys[k, t, :, cols[l]]
        if l == 0:
            return jnp.where(lane < 2, fixed[k, block(t), :], grad)
        if l == TILES - 1:
            return jnp.where(lane >= LANES - 2, fixed[k, block(t), :], grad)
        return grad

    def push_x(t, carry):
        out = []
        for l in range(TILES):
            uc, gc = carry[l]
            c = cols[l]
            m = wetc[t + 2, :, c].astype(f32)
            flow = faces[1, t + 1, :, c] - faces[1, t, :, c]
            rise = fields[3, t + 3, :, c] - fields[3, t + 1, :, c]
            px = m * (
                fields[1, t + 2, :, c] - flow - y_grad(1, t, l)
                - (push_factor * fields[0, t + 2, :, c]) * rise
            )
            uc = uc + gc
            cx[l, block(t), :] = uc
            out.append((uc, gc + csx[l, block(t), :] * (uc - px)))
        return tuple(out)

    rest = tuple((zero, zero) for _ in range(TILES))
    ends = lax.fori_loop(0, STEPS, push_x, rest, unroll=4)

    before_x = []
    for l in range(TILES):
        windows = [[win_x[l, 4 * k + e] for e in range(4)] for k in range(3)]
        total, before = scan_vectors(windows, ends[l], sub)
        before_x.append(before)
        f, tau = win_x[l, 12], win_x[l, 13]
        rhs_z[zi, l : l + 1, :] = (total[0] - tau * total[1])[7:8, :]
        rhs_z[zi, 4 + l : 5 + l, :] = (-(f * total[1]))[7:8, :]
    rhs_z_copies = gather(rhs_z, zi, z_mates, half)
    sent += rhs_z_copies

    def depth_and_q(t, carry):
        for l in range(TILES):
            c = cols[l]
            m = wetc[t + 2, :, c].astype(f32)
            os_n[t, :, c] = m * (faces[0, t + 1, :, c] - faces[0, t, :, c] + y_grad(0, t, l))
            flow = faces[2, t + 1, :, c] - faces[2, t, :, c]
            qs[l, block(t), :] = m * (fields[2, t + 2, :, c] - flow - y_grad(2, t, l))
        return carry

    lax.fori_loop(0, STEPS, depth_and_q, 0, unroll=2)

    def store_out(staged, out, base):
        copies = [
            pltpu.make_async_copy(staged.at[:, s, :], out.at[s], out_sem.at[base + s])
            for s in range(8)
        ]
        for copy in copies:
            copy.start()
        return copies

    outs = store_out(os_n, corr_out, 0)

    for l in range(TILES):
        turn(qt.at[l], qs[l].T)

    def rhs_step_y(t, carry):
        out = []
        for l in range(TILES):
            uc, gc = carry[l]
            where = pl.ds(t, 8, stride=PITCH)
            uc = uc + gc
            cy[l, block(t), :] = uc
            out.append((uc, gc + cty[l, where, :] * (uc - qt[l, where, :])))
        return tuple(out)

    ends = lax.fori_loop(0, STEPS, rhs_step_y, rest, unroll=2)
    before_y, totals_y = [], []
    sum_y = None
    for l in range(TILES):
        windows = [[win_y[l, 4 * k + e] for e in range(4)] for k in range(3)]
        total, before = scan_vectors(windows, ends[l], sub)
        before_y.append(before)
        totals_y.append(total)
        if sum_y is None:
            sum_y = total
        else:
            moved = apply2([win_y[l, 12 + e] for e in range(4)], sum_y)
            sum_y = (total[0] + moved[0], total[1] + moved[1])
    rhs_y[gy, 0:1, :] = (sum_y[0] - row_y[1] * sum_y[1])[7:8, :]
    rhs_y[gy, 1:2, :] = (-(row_y[0] * sum_y[1]))[7:8, :]
    rhs_y_copies = gather(rhs_y, gy, y_mates, half + base_y)
    sent += rhs_y_copies

    for copy in coef_z_copies:
        copy.wait_recv()

    def port(buf, k):
        return buf[k, 0:4, :], buf[k, 4:8, :], buf[k, 8:12, :]

    group_steps = []
    f, tau, mu = port(coef_z, 0)
    for k in range(1, nz):
        fk, tk, mk = port(coef_z, k)
        inv = 1.0 / (1.0 + tau * mk)
        a = fk * inv
        d = f * inv
        group_steps.append((a, a * tau, d, d * mk))
        f, tau, mu = f * a, tk + fk * (a * tau), mu + f * (d * mk)
    coef_x[xi, 0:4, :] = f
    coef_x[xi, 4:8, :] = tau
    coef_x[xi, 8:12, :] = mu
    coef_x_copies = gather(coef_x, xi, x_mates, base_x)
    sent += coef_x_copies

    def left_chain(ports, mine, rho):
        steps = []
        for k in range(len(ports)):
            fk, tk, mk = ports[k]
            inv = 1.0 / (1.0 + rho * mk)
            a = fk * inv
            steps.append((a, a * rho))
            rho = jnp.where(k < mine, tk + fk * (a * rho), rho)
        return rho, steps

    def right_chain(ports, mine, back):
        steps = [None] * len(ports)
        for k in reversed(range(len(ports))):
            fk, tk, mk = ports[k]
            inv = 1.0 / (1.0 + tk * back)
            a = fk * inv
            steps[k] = (a, a * back)
            back = jnp.where(k >= mine, mk + fk * (a * back), back)
        return back, steps

    def left_values(steps, rhs, mine, w):
        for k in range(len(steps)):
            a, b = steps[k]
            w1, w2 = rhs[k]
            w = jnp.where(k < mine, w1 + a * w + b * w2, w)
        return w

    def right_values(steps, rhs, mine, w):
        for k in reversed(range(len(steps))):
            a, b = steps[k]
            w1, w2 = rhs[k]
            w = jnp.where(k >= mine, w2 + a * w - b * w1, w)
        return w

    def meet(rho, back, wl, wr):
        inv = 1.0 / (1.0 + rho * back)
        return (rho * wr + wl) * inv, (wr - back * wl) * inv

    for copy in coef_y_copies:
        copy.wait_recv()
    ports_y = [tuple(coef_y[k, e : e + 1, :] for e in range(3)) for k in range(ny)]
    row_zero = jnp.zeros((1, LANES), f32)
    rho_y, left_y = left_chain(ports_y, gy, row_zero)
    back_y, right_y = right_chain(ports_y, gy, row_zero + 1.0)

    for copy in coef_x_copies:
        copy.wait_recv()
    ports_x = [port(coef_x, k) for k in range(nx)]
    ports_z = [port(coef_z, k) for k in range(nz)]
    four_zero = jnp.zeros((4, LANES), f32)
    rho_x, left_x = left_chain(ports_x, xi, four_zero)
    back_x, right_x = right_chain(ports_x, xi + 1, four_zero + 1.0)
    rho_z, left_z = left_chain(ports_z, zi, rho_x)
    back_z, right_z = right_chain(ports_z, zi, back_x)

    for copy in rhs_z_copies:
        copy.wait_recv()
    rhs_in_z = [(rhs_z[k, 0:4, :], rhs_z[k, 4:8, :]) for k in range(nz)]
    w1, w2 = rhs_in_z[0]
    for k in range(1, nz):
        a, at, d, dm = group_steps[k - 1]
        k1, k2 = rhs_in_z[k]
        w1, w2 = k1 + a * w1 + at * k2, w2 + d * k2 - dm * w1
    rhs_x[xi, 0:4, :] = w1
    rhs_x[xi, 4:8, :] = w2
    rhs_x_copies = gather(rhs_x, xi, x_mates, half + base_x)
    sent += rhs_x_copies

    for copy in rhs_y_copies:
        copy.wait_recv()
    rhs_in_y = [(rhs_y[k, 0:1, :], rhs_y[k, 1:2, :]) for k in range(ny)]
    wl = left_values(left_y, rhs_in_y, gy, row_zero)
    wr = right_values(right_y, rhs_in_y, gy, row_zero)
    state = meet(rho_y, back_y, wl, wr)
    starts = []
    for l in range(TILES):
        before = [pre_y[l, e] for e in range(4)]
        wide = tuple(jnp.broadcast_to(s, (8, LANES)) for s in state)
        moved = apply2(before, wide)
        starts.append((moved[0] + before_y[l][0], moved[1] + before_y[l][1]))
        if l < TILES - 1:
            moved = apply2([win_y[l, 12 + e] for e in range(4)], wide)
            state = tuple((moved[e] + totals_y[l][e])[7:8, :] for e in range(2))

    def finish_y(t, carry):
        for l in range(TILES):
            at = block(t)
            vt[l, pl.ds(t, 8, stride=PITCH), :] = (
                ay[l, at, :] * starts[l][0] + by[l, at, :] * starts[l][1] + cy[l, at, :]
            )
        return carry

    lax.fori_loop(0, STEPS, finish_y, 0, unroll=2)
    for l in range(TILES):
        line = [vt[l, PITCH * s : PITCH * s + STEPS, :] for s in range(8)]
        os_v[:, :, cols[l]] = jnp.concatenate(line, axis=0).T.reshape(STEPS, 8, LANES)
    outs += store_out(os_v, v_out, 8)

    for copy in rhs_x_copies:
        copy.wait_recv()
    rhs_in_x = [(rhs_x[k, 0:4, :], rhs_x[k, 4:8, :]) for k in range(nx)]
    wl = left_values(left_x, rhs_in_x, xi, four_zero)
    wr = right_values(right_x, rhs_in_x, xi + 1, four_zero)
    wl = left_values(left_z, rhs_in_z, zi, wl)
    wr = right_values(right_z, rhs_in_z, zi, wr)
    state = meet(rho_z, back_z, wl, wr)
    for l in range(TILES):
        before = [pre_x[l, e] for e in range(4)]
        wide = tuple(jnp.broadcast_to(s[l : l + 1, :], (8, LANES)) for s in state)
        moved = apply2(before, wide)
        u0, g0 = moved[0] + before_x[l][0], moved[1] + before_x[l][1]
        for t in range(STEPS):
            at = pl.ds(8 * t, 8)
            os_u[t, :, cols[l]] = ax[l, at, :] * u0 + bx[l, at, :] * g0 + cx[l, at, :]
    outs += store_out(os_u, u_out, 16)

    for copy in sent:
        copy.wait_send()
    for copy in outs:
        copy.wait()


def predictor(sizes, spring, depth, momentum_x, momentum_y, bed, wet):
    nx, nz, ny = sizes
    rows, cols = depth.shape
    shape = (8, STEPS, cols)
    flat = jax.ShapeDtypeStruct(shape, f32)
    hbm = pl.BlockSpec(memory_space=pl.ANY)
    tile = (TILES, 128, LANES)
    wide = (TILES, 8 * PITCH, LANES)
    far = 2 * (nz + nx + ny - 3)
    results = pl.pallas_call(
        functools.partial(kernel, sizes, spring),
        out_shape=(flat, flat, flat),
        in_specs=[hbm] * 5,
        out_specs=[hbm] * 3,
        scratch_shapes=[
            pltpu.VMEM((4, STEPS + 4, 8, cols), f32),
            pltpu.VMEM((STEPS + 4, 8, cols), jnp.int32),
            pltpu.VMEM(tile, f32),
            pltpu.VMEM(wide, f32),
            pltpu.VMEM(tile, f32),
            pltpu.VMEM(tile, f32),
            pltpu.VMEM(tile, f32),
            pltpu.VMEM(tile, f32),
            pltpu.VMEM(tile, f32),
            pltpu.VMEM(tile, f32),
            pltpu.VMEM((TILES, 16, 8, LANES), f32),
            pltpu.VMEM((TILES, 16, 8, LANES), f32),
            pltpu.VMEM((TILES, 4, 8, LANES), f32),
            pltpu.VMEM((TILES, 4, 8, LANES), f32),
            pltpu.VMEM((3, STEPS + 1, 8, cols), f32),
            pltpu.VMEM(tile, f32),
            pltpu.VMEM(wide, f32),
            pltpu.VMEM(wide, f32),
            pltpu.VMEM((STEPS, 8, cols), f32),
            pltpu.VMEM((STEPS, 8, cols), f32),
            pltpu.VMEM((STEPS, 8, cols), f32),
            pltpu.VMEM((3, STEPS, 8, cols), f32),
            pltpu.VMEM((128, LANES), f32),
            pltpu.VMEM((2, 24, LANES), f32),
            pltpu.VMEM((5, 24, LANES), f32),
            pltpu.VMEM((3, 128, LANES), f32),
            pltpu.VMEM((3, 128, LANES), f32),
            pltpu.VMEM((nz, 16, LANES), f32),
            pltpu.VMEM((nx, 16, LANES), f32),
            pltpu.VMEM((ny, 8, LANES), f32),
            pltpu.VMEM((nz, 8, LANES), f32),
            pltpu.VMEM((nx, 8, LANES), f32),
            pltpu.VMEM((ny, 8, LANES), f32),
            pltpu.VMEM((3, 8, LANES), f32),
            pltpu.SemaphoreType.DMA((40,)),
            pltpu.SemaphoreType.DMA((6,)),
            pltpu.SemaphoreType.DMA((6,)),
            pltpu.SemaphoreType.DMA((far,)),
            pltpu.SemaphoreType.DMA((far,)),
            pltpu.SemaphoreType.DMA((24,)),
        ],
        compiler_params=pltpu.CompilerParams(collective_id=0, has_side_effects=True, vmem_limit_bytes=55_700_000),
    )(*(a.reshape(shape) for a in (depth, momentum_x, momentum_y, bed, wet)))
    corr, flux_u, flux_v = (a.reshape(rows, cols) for a in results)
    return (depth - corr, flux_u / depth, flux_v / depth)


def solution(mesh):
    ngx, ny = mesh.shape["gx"], mesh.shape["gy"]
    nz = 8 if ngx % 8 == 0 else max(1, ngx // 2)
    sizes = (ngx // nz, nz, ny)
    scale = (4096 / 4.0) ** 2 / 3.0
    place = P("gx", "gy")
    return jax.shard_map(
        functools.partial(predictor, sizes, 1.0 / scale),
        mesh=mesh,
        in_specs=(place,) * 5,
        out_specs=(place,) * 3,
        check_vma=False,
    )
```

```python
import functools

import jax
import jax.numpy as jnp
from jax import lax
from jax.experimental import pallas as pl
from jax.experimental.pallas import tpu as pltpu
from jax.sharding import PartitionSpec as P

MESH = pl.DeviceIdType.MESH
GRAVITY = 9.81
ROOT_G = GRAVITY**0.5
RATIO = 0.05
LANES = 128
TILES = 4
STEPS = 16
PITCH = 20
f32 = jnp.float32


def minmod(a, c):
    return jnp.maximum(jnp.minimum(a, c), 0.0) + jnp.minimum(jnp.maximum(a, c), 0.0)


def face_flux(lefts, rights, opened):
    hl, pl_, ql = lefts
    hr, pr, qr = rights
    sl = jnp.where(opened, hl, 1.0)
    sr = jnp.where(opened, hr, 1.0)
    il = lax.rsqrt(sl)
    ir = lax.rsqrt(sr)
    ul = pl_ * (il * il)
    ur = pr * (ir * ir)
    fast = jnp.maximum(
        jnp.abs(ul) + (ROOT_G * sl) * il, jnp.abs(ur) + (ROOT_G * sr) * ir
    )
    factor = jnp.where(opened, 0.5 * RATIO, 0.0)
    mass = (pl_ + pr) - fast * (hr - hl)
    normal = (pl_ * ul + pr * ur) + (0.5 * GRAVITY) * (sl * sl + sr * sr) - fast * (pr - pl_)
    across = (ql * ul + qr * ur) - fast * (qr - ql)
    return factor * mass, factor * normal, factor * across


def lane_up(tiles, lane):
    n = len(tiles)
    rolled = [pltpu.roll(t, LANES - 1, 1) for t in tiles]
    return [jnp.where(lane == LANES - 1, rolled[(i + 1) % n], rolled[i]) for i in range(n)]


def lane_down(tiles, lane):
    n = len(tiles)
    rolled = [pltpu.roll(t, 1, 1) for t in tiles]
    return [jnp.where(lane == 0, rolled[(i - 1) % n], rolled[i]) for i in range(n)]


def matmul2(m, a):
    m11, m12, m21, m22 = m
    a11, a12, a21, a22 = a
    return (
        m11 * a11 + m12 * a21,
        m11 * a12 + m12 * a22,
        m21 * a11 + m22 * a21,
        m21 * a12 + m22 * a22,
    )


def apply2(m, v):
    return (m[0] * v[0] + m[1] * v[1], m[2] * v[0] + m[3] * v[1])


def shifted(values, k, sub, first):
    return tuple(
        jnp.where(sub >= k, pltpu.roll(v, k, 0), f) for v, f in zip(values, first)
    )


IDENT = (1.0, 0.0, 0.0, 1.0)


def scan_matrices(m, sub):
    windows = []
    for k in (1, 2, 4):
        windows.append(m)
        m = matmul2(m, shifted(m, k, sub, IDENT))
    return windows, m, shifted(m, 1, sub, IDENT)


def scan_vectors(windows, v, sub):
    for k, m in zip((1, 2, 4), windows):
        moved = apply2(m, shifted(v, k, sub, (0.0, 0.0)))
        v = (v[0] + moved[0], v[1] + moved[1])
    return v, shifted(v, 1, sub, (0.0, 0.0))


def kernel(
    sizes, spring,
    h_in, p_in, q_in, b_in, m_in,
    corr_out, u_out, v_out,
    fields, wetc, csx, cty, ax, bx, cx, ay, by, cy, win_x, win_y, pre_x, pre_y,
    faces, qs, qt, vt, os_n, os_u, os_v, ys, edges, got, seq, fix, fixed,
    coef_z, coef_x, coef_y, rhs_z, rhs_x, rhs_y, row_y,
    load_sem, halo_send, halo_recv, far_send, far_recv,
):
    nx, nz, ny = sizes
    gx = lax.axis_index("gx")
    gy = lax.axis_index("gy")
    xi = lax.div(gx, nz)
    zi = lax.rem(gx, nz)
    ngx = nx * nz

    x_up = (lax.rem(gx + 1, ngx), gy)
    x_dn = (lax.rem(gx + ngx - 1, ngx), gy)
    y_up = (gx, lax.rem(gy + 1, ny))
    y_dn = (gx, lax.rem(gy + ny - 1, ny))
    z_mates = [(xi * nz + lax.rem(zi + k, nz), gy) for k in range(1, nz)]
    x_mates = [(lax.rem(xi + k, nx) * nz + zi, gy) for k in range(1, nx)]
    y_mates = [(gx, lax.rem(gy + k, ny)) for k in range(1, ny)]

    barrier = pltpu.get_barrier_semaphore()
    far_first = sorted(range(nz - 1), key=lambda k: abs(k + 1 - nz // 2))
    peers = [z_mates[k] for k in far_first] + [x_up, x_dn] + x_mates + y_mates
    for peer in peers:
        pl.semaphore_signal(barrier, inc=1, device_id=peer, device_id_type=MESH)

    def load(i, src):
        copies = []
        for s in range(8):
            rows = pl.ds(2, STEPS)
            dst = fields.at[i, rows, s, :] if i < 4 else wetc.at[rows, s, :]
            copy = pltpu.make_async_copy(src.at[s], dst, load_sem.at[8 * i + s])
            copy.start()
            copies.append(copy)
        return copies

    loads = load(0, h_in)
    for i, src in ((1, p_in), (2, q_in), (3, b_in), (4, m_in)):
        loads += load(i, src)

    sub = lax.broadcasted_iota(jnp.int32, (8, LANES), 0)
    lane = lax.broadcasted_iota(jnp.int32, (8, LANES), 1)
    zero = jnp.where(lane + sub < 0, 1.0, 0.0)
    one = jnp.where(lane + sub < 0, 0.0, 1.0)
    cols = [pl.ds(LANES * l, LANES) for l in range(TILES)]

    def block(t):
        return pl.ds(pl.multiple_of(8 * t, 8), 8)

    for copy in loads[:8]:
        copy.wait()

    def start_pieces():
        return tuple((one, zero, zero, one) for _ in range(TILES))

    def coef_step_x(t, carry):
        out = []
        for l in range(TILES):
            ua, ga, ub, gb = carry[l]
            h = fields[0, t + 2, :, cols[l]]
            c = spring / (h * h)
            csx[l, block(t), :] = c
            ua = ua + ga
            ub = ub + gb
            ax[l, block(t), :] = ua
            bx[l, block(t), :] = ub
            out.append((ua, ga + c * ua, ub, gb + c * ub))
        return tuple(out)

    ends = lax.fori_loop(0, STEPS, coef_step_x, start_pieces(), unroll=2)
    for l in range(TILES):
        ua, ga, ub, gb = ends[l]
        windows, total, before = scan_matrices((ua, ub, ga, gb), sub)
        for k in range(3):
            for e in range(4):
                win_x[l, 4 * k + e] = windows[k][e]
        for e in range(4):
            pre_x[l, e] = before[e]
        f = 1.0 / total[3]
        coef_x_row = (f, total[1] * f, total[2] * f)
        for e in range(3):
            coef_z[zi, 4 * e + l : 4 * e + l + 1, :] = coef_x_row[e][7:8, :]
            win_x[l, 12 + e] = coef_x_row[e]

    seq[...] = jnp.zeros((5, 24, LANES), f32)
    fix[...] = jnp.zeros((3, 128, LANES), f32)

    for copy in loads[8:]:
        copy.wait()

    full_lane = lax.broadcasted_iota(jnp.int32, (128, LANES), 1)

    def edge(i, l):
        if i < 4:
            return fields[i, 2 : 2 + STEPS, :, cols[l]].reshape(128, LANES)
        return wetc[2 : 2 + STEPS, :, cols[l]].reshape(128, LANES).astype(f32)

    packed = None
    for i in range(5):
        both = jnp.where(full_lane < 64, edge(i, 0), edge(i, TILES - 1))
        both = pltpu.roll(both, 8 * i + 4, 1)
        packed = jnp.where(full_lane >= 8 * i, both, packed) if i else both
    edges[...] = packed.T

    pl.semaphore_wait(barrier, len(peers))

    def remote(src, dst, send, recv, device):
        copy = pltpu.make_async_remote_copy(
            src_ref=src, dst_ref=dst, send_sem=send, recv_sem=recv,
            device_id=device, device_id_type=MESH,
        )
        copy.start()
        return copy

    first, last = pl.ds(2, 2), pl.ds(STEPS, 2)
    past, ahead = pl.ds(0, 2), pl.ds(STEPS + 2, 2)
    halos_x = [
        remote(fields.at[:, first, 0, :], fields.at[:, ahead, 7, :],
               halo_send.at[0], halo_recv.at[0], x_dn),
        remote(fields.at[:, last, 7, :], fields.at[:, past, 0, :],
               halo_send.at[1], halo_recv.at[1], x_up),
        remote(wetc.at[first, 0, :], wetc.at[ahead, 7, :],
               halo_send.at[2], halo_recv.at[2], x_dn),
        remote(wetc.at[last, 7, :], wetc.at[past, 0, :],
               halo_send.at[3], halo_recv.at[3], x_up),
    ]
    halos_y = [
        remote(edges.at[pl.ds(0, 40), :], got.at[0], halo_send.at[4], halo_recv.at[4], y_dn),
        remote(edges.at[pl.ds(0, 40), :], got.at[1], halo_send.at[5], halo_recv.at[5], y_up),
    ]

    def gather(buf, slot, mates, base):
        return [
            remote(buf.at[slot], buf.at[slot], far_send.at[base + i], far_recv.at[base + i], mate)
            for i, mate in enumerate(mates)
        ]

    sent = list(halos_x) + list(halos_y)
    base_y = nz - 1
    base_x = base_y + ny - 1
    half = base_x + nx - 1

    coef_z_copies = gather(coef_z, zi, z_mates, 0)
    sent += coef_z_copies

    def x_faces(col, dst, start, count):
        w = [[fields[i, start + d, :, col] for d in range(4)] for i in range(3)]
        diff = [[0.5 * (w[i][d + 1] - w[i][d]) for d in range(3)] for i in range(3)]
        slope = [minmod(diff[i][0], diff[i][1]) for i in range(3)]
        for k in range(count):
            lefts, rights = [], []
            for i in range(3):
                after = minmod(diff[i][1], diff[i][2])
                lefts.append(w[i][1] + slope[i])
                rights.append(w[i][2] - after)
                slope[i] = after
                if k + 1 < count:
                    new = fields[i, start + k + 4, :, col]
                    w[i] = [None, w[i][2], w[i][3], new]
                    diff[i] = [None, diff[i][2], 0.5 * (new - w[i][2])]
            m0 = wetc[start + k + 1, :, col]
            m1 = wetc[start + k + 2, :, col]
            flux = face_flux(lefts, rights, (m0 * m1) > 0)
            for i in range(3):
                faces[i, start + k, :, col] = flux[i]

    def interior(l, carry):
        x_faces(pl.ds(pl.multiple_of(LANES * l, LANES), LANES), None, 2, STEPS - 3)
        return carry

    lax.fori_loop(0, TILES, interior, 0)

    push_factor = 0.5 * RATIO * GRAVITY

    def y_inner(t, carry):
        values = [[fields[i, t + 2, :, c] for c in cols] for i in range(3)]
        signed = [jnp.where(wetc[t + 2, :, c] > 0, h, -h) for c, h in zip(cols, values[0])]
        signed_next = lane_up(signed, lane)
        opened = [jnp.minimum(a, b) > 0.0 for a, b in zip(signed, signed_next)]
        lefts, rights = [], []
        for i in (0, 2, 1):
            w = values[i]
            after = lane_up(w, lane) if i else [jnp.abs(a) for a in signed_next]
            diff = [0.5 * (a - b) for a, b in zip(after, w)]
            slope = [minmod(a, b) for a, b in zip(lane_down(diff, lane), diff)]
            lefts.append([a + s for a, s in zip(w, slope)])
            rights.append(lane_up([a - s for a, s in zip(w, slope)], lane))
        flux = [
            face_flux([x[l] for x in lefts], [x[l] for x in rights], opened[l])
            for l in range(TILES)
        ]
        across = [flux[l][2] for l in range(TILES)]
        for l, before in enumerate(lane_down(across, lane)):
            ys[0, t, :, cols[l]] = flux[l][0]
            ys[1, t, :, cols[l]] = across[l] - before
            ys[2, t, :, cols[l]] = flux[l][1]
        return carry

    lax.fori_loop(0, STEPS, y_inner, 0)

    for copy in halos_y:
        copy.wait_recv()
    for i in range(5):
        high, low = 8 * i, 8 * i + 4
        seq[i, 0:2, :] = jnp.where(gy > 0, got[1, high + 2 : high + 4, :], 0.0)
        seq[i, 2:6, :] = edges[low : low + 4, :]
        seq[i, 8:12, :] = edges[high : high + 4, :]
        seq[i, 12:14, :] = jnp.where(gy < ny - 1, got[0, low : low + 2, :], 0.0)

    def rows_of(i, d):
        return seq[i, d : d + 16, :]

    lefts, rights = [], []
    for i in (0, 2, 1):
        w = [rows_of(i, d) for d in range(4)]
        diff = [0.5 * (w[d + 1] - w[d]) for d in range(3)]
        lefts.append(w[1] + minmod(diff[0], diff[1]))
        rights.append(w[2] - minmod(diff[1], diff[2]))
    flux = face_flux(lefts, rights, (rows_of(4, 1) * rows_of(4, 2)) > 0.5)
    for k, i in ((0, 0), (1, 2), (2, 1)):
        grad = pltpu.roll(flux[i], 15, 0) - flux[i]
        if k == 2:
            grad = grad + (push_factor * rows_of(0, 2)) * (rows_of(3, 3) - rows_of(3, 1))
        fix[k, 0:2, :] = grad[0:2, :]
        fix[k, 126:128, :] = grad[8:10, :]
    for k in (1, 0, 2):
        fixed[k] = fix[k].T

    for copy in halos_x:
        copy.wait_recv()

    def fill(ref, kind, both):
        for l in range(TILES):
            for t, source, rim, shift in (
                (0, STEPS, 0, 1), (1, STEPS + 1, 0, 1),
                (STEPS + 2, 2, 7, 7), (STEPS + 3, 3, 7, 7),
            ):
                if not both and t in (0, STEPS + 3):
                    continue
                gone = gx == 0 if rim == 0 else gx == ngx - 1
                border = jnp.where(gone, jnp.zeros((), kind), ref[t, :, cols[l]])
                ref[t, :, cols[l]] = jnp.where(
                    sub == rim, border, pltpu.roll(ref[source, :, cols[l]], shift, 0)
                )

    for i in range(4):
        fill(fields.at[i], f32, i < 3)
    fill(wetc, jnp.int32, False)

    def rim_faces(l, carry):
        col = pl.ds(pl.multiple_of(LANES * l, LANES), LANES)
        x_faces(col, None, 0, 2)
        x_faces(col, None, STEPS - 1, 2)
        return carry

    lax.fori_loop(0, TILES, rim_faces, 0)

    def patch(k, t, l, grad):
        if l == 0:
            return jnp.where(lane < 2, fixed[k, block(t), :], grad)
        if l == TILES - 1:
            return jnp.where(lane >= LANES - 2, fixed[k, block(t), :], grad)
        return grad

    def push_x(t, carry):
        out = []
        for l in range(TILES):
            uc, gc = carry[l]
            c = cols[l]
            m = wetc[t + 2, :, c].astype(f32)
            flow = faces[1, t + 1, :, c] - faces[1, t, :, c]
            rise = fields[3, t + 3, :, c] - fields[3, t + 1, :, c]
            px = m * (
                fields[1, t + 2, :, c] - flow - patch(1, t, l, ys[1, t, :, c])
                - (push_factor * fields[0, t + 2, :, c]) * rise
            )
            uc = uc + gc
            cx[l, block(t), :] = uc
            out.append((uc, gc + csx[l, block(t), :] * (uc - px)))
        return tuple(out)

    rest = tuple((zero, zero) for _ in range(TILES))
    ends = lax.fori_loop(0, STEPS, push_x, rest, unroll=4)

    before_x = []
    for l in range(TILES):
        windows = [[win_x[l, 4 * k + e] for e in range(4)] for k in range(3)]
        total, before = scan_vectors(windows, ends[l], sub)
        before_x.append(before)
        f, tau = win_x[l, 12], win_x[l, 13]
        rhs_z[zi, l : l + 1, :] = (total[0] - tau * total[1])[7:8, :]
        rhs_z[zi, 4 + l : 5 + l, :] = (-(f * total[1]))[7:8, :]
    rhs_z_copies = gather(rhs_z, zi, z_mates, half)
    sent += rhs_z_copies

    for copy in coef_z_copies:
        copy.wait_recv()

    def port(buf, k):
        return buf[k, 0:4, :], buf[k, 4:8, :], buf[k, 8:12, :]

    group_steps = []
    f, tau, mu = port(coef_z, 0)
    for k in range(1, nz):
        fk, tk, mk = port(coef_z, k)
        inv = 1.0 / (1.0 + tau * mk)
        a = fk * inv
        d = f * inv
        group_steps.append((a, a * tau, d, d * mk))
        f, tau, mu = f * a, tk + fk * (a * tau), mu + f * (d * mk)
    coef_x[xi, 0:4, :] = f
    coef_x[xi, 4:8, :] = tau
    coef_x[xi, 8:12, :] = mu
    coef_x_copies = gather(coef_x, xi, x_mates, base_x)
    sent += coef_x_copies

    def turn(dst, value):
        for s in range(8):
            dst[PITCH * s : PITCH * s + STEPS, :] = value[STEPS * s : STEPS * (s + 1), :]

    for l in range(TILES):
        turn(cty.at[l], csx[l].T)

    def coef_step_y(t, carry):
        out = []
        for l in range(TILES):
            ua, ga, ub, gb = carry[l]
            c = cty[l, pl.ds(t, 8, stride=PITCH), :]
            ua = ua + ga
            ub = ub + gb
            ay[l, block(t), :] = ua
            by[l, block(t), :] = ub
            out.append((ua, ga + c * ua, ub, gb + c * ub))
        return tuple(out)

    ends = lax.fori_loop(0, STEPS, coef_step_y, start_pieces(), unroll=2)
    total_y = None
    for l in range(TILES):
        ua, ga, ub, gb = ends[l]
        windows, total, before = scan_matrices((ua, ub, ga, gb), sub)
        for k in range(3):
            for e in range(4):
                win_y[l, 4 * k + e] = windows[k][e]
        for e in range(4):
            pre_y[l, e] = before[e]
            win_y[l, 12 + e] = total[e]
        total_y = total if total_y is None else matmul2(total, total_y)
    f = 1.0 / total_y[3]
    coef_y_row = (f, total_y[1] * f, total_y[2] * f)
    for e in range(3):
        coef_y[gy, e : e + 1, :] = coef_y_row[e][7:8, :]
        row_y[e] = coef_y_row[e]
    coef_y_copies = gather(coef_y, gy, y_mates, base_y)
    sent += coef_y_copies

    def depth_and_q(t, carry):
        mass, normal, bed = (
            [ref[t + d, :, c] for c in cols] for ref, d in ((ys.at[0], 0), (ys.at[2], 0), (fields.at[3], 2))
        )
        mass_past, normal_past, bed_past = (lane_down(x, lane) for x in (mass, normal, bed))
        bed_next = lane_up(bed, lane)
        for l in range(TILES):
            c = cols[l]
            m = wetc[t + 2, :, c].astype(f32)
            grad = patch(0, t, l, mass[l] - mass_past[l])
            os_n[t, :, c] = m * (faces[0, t + 1, :, c] - faces[0, t, :, c] + grad)
            slope = (push_factor * fields[0, t + 2, :, c]) * (bed_next[l] - bed_past[l])
            grad = patch(2, t, l, normal[l] - normal_past[l] + slope)
            flow = faces[2, t + 1, :, c] - faces[2, t, :, c]
            qs[l, block(t), :] = m * (fields[2, t + 2, :, c] - flow - grad)
        return carry

    lax.fori_loop(0, STEPS, depth_and_q, 0, unroll=2)

    for l in range(TILES):
        turn(qt.at[l], qs[l].T)

    def rhs_step_y(t, carry):
        out = []
        for l in range(TILES):
            uc, gc = carry[l]
            where = pl.ds(t, 8, stride=PITCH)
            uc = uc + gc
            cy[l, block(t), :] = uc
            out.append((uc, gc + cty[l, where, :] * (uc - qt[l, where, :])))
        return tuple(out)

    ends = lax.fori_loop(0, STEPS, rhs_step_y, rest, unroll=2)
    before_y, totals_y = [], []
    sum_y = None
    for l in range(TILES):
        windows = [[win_y[l, 4 * k + e] for e in range(4)] for k in range(3)]
        total, before = scan_vectors(windows, ends[l], sub)
        before_y.append(before)
        totals_y.append(total)
        if sum_y is None:
            sum_y = total
        else:
            moved = apply2([win_y[l, 12 + e] for e in range(4)], sum_y)
            sum_y = (total[0] + moved[0], total[1] + moved[1])
    rhs_y[gy, 0:1, :] = (sum_y[0] - row_y[1] * sum_y[1])[7:8, :]
    rhs_y[gy, 1:2, :] = (-(row_y[0] * sum_y[1]))[7:8, :]
    rhs_y_copies = gather(rhs_y, gy, y_mates, half + base_y)
    sent += rhs_y_copies

    for copy in rhs_z_copies:
        copy.wait_recv()
    rhs_in_z = [(rhs_z[k, 0:4, :], rhs_z[k, 4:8, :]) for k in range(nz)]
    w1, w2 = rhs_in_z[0]
    for k in range(1, nz):
        a, at, d, dm = group_steps[k - 1]
        k1, k2 = rhs_in_z[k]
        w1, w2 = k1 + a * w1 + at * k2, w2 + d * k2 - dm * w1
    rhs_x[xi, 0:4, :] = w1
    rhs_x[xi, 4:8, :] = w2
    rhs_x_copies = gather(rhs_x, xi, x_mates, half + base_x)
    sent += rhs_x_copies

    def left_chain(ports, mine, rho):
        steps = []
        for k in range(len(ports)):
            fk, tk, mk = ports[k]
            inv = 1.0 / (1.0 + rho * mk)
            a = fk * inv
            steps.append((a, a * rho))
            rho = jnp.where(k < mine, tk + fk * (a * rho), rho)
        return rho, steps

    def right_chain(ports, mine, back):
        steps = [None] * len(ports)
        for k in reversed(range(len(ports))):
            fk, tk, mk = ports[k]
            inv = 1.0 / (1.0 + tk * back)
            a = fk * inv
            steps[k] = (a, a * back)
            back = jnp.where(k >= mine, mk + fk * (a * back), back)
        return back, steps

    def left_values(steps, rhs, mine, w):
        for k in range(len(steps)):
            a, b = steps[k]
            w1, w2 = rhs[k]
            w = jnp.where(k < mine, w1 + a * w + b * w2, w)
        return w

    def right_values(steps, rhs, mine, w):
        for k in reversed(range(len(steps))):
            a, b = steps[k]
            w1, w2 = rhs[k]
            w = jnp.where(k >= mine, w2 + a * w - b * w1, w)
        return w

    def meet(rho, back, wl, wr):
        inv = 1.0 / (1.0 + rho * back)
        return (rho * wr + wl) * inv, (wr - back * wl) * inv

    for copy in coef_y_copies:
        copy.wait_recv()
    ports_y = [tuple(coef_y[k, e : e + 1, :] for e in range(3)) for k in range(ny)]
    row_zero = jnp.zeros((1, LANES), f32)
    rho_y, left_y = left_chain(ports_y, gy, row_zero)
    back_y, right_y = right_chain(ports_y, gy, row_zero + 1.0)

    for copy in coef_x_copies:
        copy.wait_recv()
    ports_x = [port(coef_x, k) for k in range(nx)]
    ports_z = [port(coef_z, k) for k in range(nz)]
    four_zero = jnp.zeros((4, LANES), f32)
    rho_x, left_x = left_chain(ports_x, xi, four_zero)
    back_x, right_x = right_chain(ports_x, xi + 1, four_zero + 1.0)
    rho_z, left_z = left_chain(ports_z, zi, rho_x)
    back_z, right_z = right_chain(ports_z, zi, back_x)

    for copy in rhs_y_copies:
        copy.wait_recv()
    rhs_in_y = [(rhs_y[k, 0:1, :], rhs_y[k, 1:2, :]) for k in range(ny)]
    wl = left_values(left_y, rhs_in_y, gy, row_zero)
    wr = right_values(right_y, rhs_in_y, gy, row_zero)
    state = meet(rho_y, back_y, wl, wr)
    starts = []
    for l in range(TILES):
        before = [pre_y[l, e] for e in range(4)]
        wide = tuple(jnp.broadcast_to(s, (8, LANES)) for s in state)
        moved = apply2(before, wide)
        starts.append((moved[0] + before_y[l][0], moved[1] + before_y[l][1]))
        if l < TILES - 1:
            moved = apply2([win_y[l, 12 + e] for e in range(4)], wide)
            state = tuple((moved[e] + totals_y[l][e])[7:8, :] for e in range(2))

    def finish_y(t, carry):
        for l in range(TILES):
            at = block(t)
            vt[l, pl.ds(t, 8, stride=PITCH), :] = (
                ay[l, at, :] * starts[l][0] + by[l, at, :] * starts[l][1] + cy[l, at, :]
            )
        return carry

    lax.fori_loop(0, STEPS, finish_y, 0, unroll=2)
    for l in range(TILES):
        line = [vt[l, PITCH * s : PITCH * s + STEPS, :] for s in range(8)]
        natural = jnp.concatenate(line, axis=0).T
        for t in range(STEPS):
            os_u[l, pl.ds(t, 8, stride=STEPS), :] = natural[8 * t : 8 * t + 8, :]
        v_out[:, cols[l]] = os_u[l]

    for l in range(TILES):
        for t in range(STEPS):
            os_v[l, pl.ds(t, 8, stride=STEPS), :] = os_n[t, :, cols[l]]
        corr_out[:, cols[l]] = os_v[l]

    own_l = left_values(left_z, rhs_in_z, zi, four_zero)
    own_r = right_values(right_z, rhs_in_z, zi, four_zero)
    gain_l = gain_r = four_zero + 1.0
    for k in range(nz):
        gain_l = jnp.where(k < zi, gain_l * left_z[k][0], gain_l)
        gain_r = jnp.where(k >= zi, gain_r * right_z[k][0], gain_r)
    for copy in rhs_x_copies:
        copy.wait_recv()
    rhs_in_x = [(rhs_x[k, 0:4, :], rhs_x[k, 4:8, :]) for k in range(nx)]
    wl = left_values(left_x, rhs_in_x, xi, four_zero)
    wr = right_values(right_x, rhs_in_x, xi + 1, four_zero)
    wl = own_l + gain_l * wl
    wr = own_r + gain_r * wr
    state = meet(rho_z, back_z, wl, wr)
    for l in range(TILES):
        before = [pre_x[l, e] for e in range(4)]
        wide = tuple(jnp.broadcast_to(s[l : l + 1, :], (8, LANES)) for s in state)
        moved = apply2(before, wide)
        u0, g0 = moved[0] + before_x[l][0], moved[1] + before_x[l][1]
        for t in range(STEPS):
            at = pl.ds(8 * t, 8)
            os_u[l, pl.ds(t, 8, stride=STEPS), :] = ax[l, at, :] * u0 + bx[l, at, :] * g0 + cx[l, at, :]
        u_out[:, cols[l]] = os_u[l]

    for copy in sent:
        copy.wait_send()


def predictor(sizes, spring, depth, momentum_x, momentum_y, bed, wet):
    nx, nz, ny = sizes
    rows, cols = depth.shape
    shape = (8, STEPS, cols)
    flat = jax.ShapeDtypeStruct((rows, cols), f32)
    hbm = pl.BlockSpec(memory_space=pl.ANY)
    tile = (TILES, 128, LANES)
    wide = (TILES, 8 * PITCH, LANES)
    far = 2 * (nz + nx + ny - 3)
    results = pl.pallas_call(
        functools.partial(kernel, sizes, spring),
        out_shape=(flat, flat, flat),
        in_specs=[hbm] * 5,
        out_specs=[pl.BlockSpec(memory_space=pltpu.VMEM)] * 3,
        scratch_shapes=[
            pltpu.VMEM((4, STEPS + 4, 8, cols), f32),
            pltpu.VMEM((STEPS + 4, 8, cols), jnp.int32),
            pltpu.VMEM(tile, f32),
            pltpu.VMEM(wide, f32),
            pltpu.VMEM(tile, f32),
            pltpu.VMEM(tile, f32),
            pltpu.VMEM(tile, f32),
            pltpu.VMEM(tile, f32),
            pltpu.VMEM(tile, f32),
            pltpu.VMEM(tile, f32),
            pltpu.VMEM((TILES, 16, 8, LANES), f32),
            pltpu.VMEM((TILES, 16, 8, LANES), f32),
            pltpu.VMEM((TILES, 4, 8, LANES), f32),
            pltpu.VMEM((TILES, 4, 8, LANES), f32),
            pltpu.VMEM((3, STEPS + 1, 8, cols), f32),
            pltpu.VMEM(tile, f32),
            pltpu.VMEM(wide, f32),
            pltpu.VMEM(wide, f32),
            pltpu.VMEM((STEPS, 8, cols), f32),
            pltpu.VMEM(tile, f32),
            pltpu.VMEM(tile, f32),
            pltpu.VMEM((3, STEPS, 8, cols), f32),
            pltpu.VMEM((128, LANES), f32),
            pltpu.VMEM((2, 40, LANES), f32),
            pltpu.VMEM((5, 24, LANES), f32),
            pltpu.VMEM((3, 128, LANES), f32),
            pltpu.VMEM((3, 128, LANES), f32),
            pltpu.VMEM((nz, 16, LANES), f32),
            pltpu.VMEM((nx, 16, LANES), f32),
            pltpu.VMEM((ny, 8, LANES), f32),
            pltpu.VMEM((nz, 8, LANES), f32),
            pltpu.VMEM((nx, 8, LANES), f32),
            pltpu.VMEM((ny, 8, LANES), f32),
            pltpu.VMEM((3, 8, LANES), f32),
            pltpu.SemaphoreType.DMA((40,)),
            pltpu.SemaphoreType.DMA((6,)),
            pltpu.SemaphoreType.DMA((6,)),
            pltpu.SemaphoreType.DMA((far,)),
            pltpu.SemaphoreType.DMA((far,)),
        ],
        compiler_params=pltpu.CompilerParams(collective_id=0, has_side_effects=True, vmem_limit_bytes=55_700_000),
    )(*(a.reshape(shape) for a in (depth, momentum_x, momentum_y, bed, wet)))
    corr, flux_u, flux_v = results
    return (depth - corr, flux_u / depth, flux_v / depth)


def solution(mesh):
    ngx, ny = mesh.shape["gx"], mesh.shape["gy"]
    nz = 8 if ngx % 8 == 0 else max(1, ngx // 2)
    sizes = (ngx // nz, nz, ny)
    scale = (4096 / 4.0) ** 2 / 3.0
    place = P("gx", "gy")
    return jax.shard_map(
        functools.partial(predictor, sizes, 1.0 / scale),
        mesh=mesh,
        in_specs=(place,) * 5,
        out_specs=(place,) * 3,
        check_vma=False,
    )
```

```python
import functools

import jax
import jax.numpy as jnp
from jax import lax
from jax.experimental import pallas as pl
from jax.experimental.pallas import tpu as pltpu
from jax.sharding import PartitionSpec as P

MESH = pl.DeviceIdType.MESH
GRAVITY = 9.81
ROOT_G = GRAVITY**0.5
RATIO = 0.05
LANES = 128
TILES = 4
STEPS = 16
PITCH = 20
f32 = jnp.float32


def minmod(a, c):
    return jnp.maximum(jnp.minimum(a, c), 0.0) + jnp.minimum(jnp.maximum(a, c), 0.0)


def face_flux(lefts, rights, opened):
    hl, pl_, ql = lefts
    hr, pr, qr = rights
    sl = jnp.where(opened, hl, 1.0)
    sr = jnp.where(opened, hr, 1.0)
    il = lax.rsqrt(sl)
    ir = lax.rsqrt(sr)
    ul = pl_ * (il * il)
    ur = pr * (ir * ir)
    fast = jnp.maximum(
        jnp.abs(ul) + (ROOT_G * sl) * il, jnp.abs(ur) + (ROOT_G * sr) * ir
    )
    factor = jnp.where(opened, 0.5 * RATIO, 0.0)
    mass = (pl_ + pr) - fast * (hr - hl)
    normal = (pl_ * ul + pr * ur) + (0.5 * GRAVITY) * (sl * sl + sr * sr) - fast * (pr - pl_)
    across = (ql * ul + qr * ur) - fast * (qr - ql)
    return factor * mass, factor * normal, factor * across


def lane_up(tiles, lane):
    n = len(tiles)
    rolled = [pltpu.roll(t, LANES - 1, 1) for t in tiles]
    return [jnp.where(lane == LANES - 1, rolled[(i + 1) % n], rolled[i]) for i in range(n)]


def lane_down(tiles, lane):
    n = len(tiles)
    rolled = [pltpu.roll(t, 1, 1) for t in tiles]
    return [jnp.where(lane == 0, rolled[(i - 1) % n], rolled[i]) for i in range(n)]


def matmul2(m, a):
    m11, m12, m21, m22 = m
    a11, a12, a21, a22 = a
    return (
        m11 * a11 + m12 * a21,
        m11 * a12 + m12 * a22,
        m21 * a11 + m22 * a21,
        m21 * a12 + m22 * a22,
    )


def apply2(m, v):
    return (m[0] * v[0] + m[1] * v[1], m[2] * v[0] + m[3] * v[1])


def shifted(values, k, sub, first):
    return tuple(
        jnp.where(sub >= k, pltpu.roll(v, k, 0), f) for v, f in zip(values, first)
    )


IDENT = (1.0, 0.0, 0.0, 1.0)


def scan_matrices(m, sub):
    windows = []
    for k in (1, 2, 4):
        windows.append(m)
        m = matmul2(m, shifted(m, k, sub, IDENT))
    return windows, m, shifted(m, 1, sub, IDENT)


def scan_vectors(windows, v, sub):
    for k, m in zip((1, 2, 4), windows):
        moved = apply2(m, shifted(v, k, sub, (0.0, 0.0)))
        v = (v[0] + moved[0], v[1] + moved[1])
    return v, shifted(v, 1, sub, (0.0, 0.0))


def kernel(
    sizes, spring,
    h_in, p_in, q_in, b_in, m_in,
    corr_out, u_out, v_out,
    fields, wetc, csx, cty, ax, bx, cx, ay, by, cy, win_x, win_y, pre_x, pre_y,
    faces, qs, qt, vt, os_n, os_u, os_v, ys, edges, got, seq, fix, fixed,
    coef_z, coef_x, coef_y, rhs_z, rhs_x, rhs_y, row_y,
    load_sem, halo_send, halo_recv, far_send, far_recv,
):
    nx, nz, ny = sizes
    gx = lax.axis_index("gx")
    gy = lax.axis_index("gy")
    xi = lax.div(gx, nz)
    zi = lax.rem(gx, nz)
    ngx = nx * nz

    x_up = (lax.rem(gx + 1, ngx), gy)
    x_dn = (lax.rem(gx + ngx - 1, ngx), gy)
    y_up = (gx, lax.rem(gy + 1, ny))
    y_dn = (gx, lax.rem(gy + ny - 1, ny))
    z_mates = [(xi * nz + lax.rem(zi + k, nz), gy) for k in range(1, nz)]
    x_mates = [(lax.rem(xi + k, nx) * nz + zi, gy) for k in range(1, nx)]
    y_mates = [(gx, lax.rem(gy + k, ny)) for k in range(1, ny)]

    barrier = pltpu.get_barrier_semaphore()
    far_first = sorted(range(nz - 1), key=lambda k: abs(k + 1 - nz // 2))
    peers = [z_mates[k] for k in far_first] + [x_up, x_dn] + x_mates + y_mates
    for peer in peers:
        pl.semaphore_signal(barrier, inc=1, device_id=peer, device_id_type=MESH)

    def load(i, src):
        copies = []
        for s in range(8):
            rows = pl.ds(2, STEPS)
            dst = fields.at[i, rows, s, :] if i < 4 else wetc.at[rows, s, :]
            copy = pltpu.make_async_copy(src.at[s], dst, load_sem.at[8 * i + s])
            copy.start()
            copies.append(copy)
        return copies

    loads = load(0, h_in)
    for i, src in ((1, p_in), (2, q_in), (3, b_in), (4, m_in)):
        loads += load(i, src)

    sub = lax.broadcasted_iota(jnp.int32, (8, LANES), 0)
    lane = lax.broadcasted_iota(jnp.int32, (8, LANES), 1)
    zero = jnp.where(lane + sub < 0, 1.0, 0.0)
    one = jnp.where(lane + sub < 0, 0.0, 1.0)
    cols = [pl.ds(LANES * l, LANES) for l in range(TILES)]

    def block(t):
        return pl.ds(pl.multiple_of(8 * t, 8), 8)

    for copy in loads[:8]:
        copy.wait()

    def start_pieces():
        return tuple((one, zero, zero, one) for _ in range(TILES))

    def coef_step_x(t, carry):
        out = []
        for l in range(TILES):
            ua, ga, ub, gb = carry[l]
            h = fields[0, t + 2, :, cols[l]]
            c = spring / (h * h)
            csx[l, block(t), :] = c
            ua = ua + ga
            ub = ub + gb
            ax[l, block(t), :] = ua
            bx[l, block(t), :] = ub
            out.append((ua, ga + c * ua, ub, gb + c * ub))
        return tuple(out)

    ends = lax.fori_loop(0, STEPS, coef_step_x, start_pieces(), unroll=2)
    for l in range(TILES):
        ua, ga, ub, gb = ends[l]
        windows, total, before = scan_matrices((ua, ub, ga, gb), sub)
        for k in range(3):
            for e in range(4):
                win_x[l, 4 * k + e] = windows[k][e]
        for e in range(4):
            pre_x[l, e] = before[e]
        f = 1.0 / total[3]
        coef_x_row = (f, total[1] * f, total[2] * f)
        for e in range(3):
            coef_z[zi, 4 * e + l : 4 * e + l + 1, :] = coef_x_row[e][7:8, :]
            win_x[l, 12 + e] = coef_x_row[e]

    seq[...] = jnp.zeros((5, 24, LANES), f32)
    fix[...] = jnp.zeros((3, 128, LANES), f32)

    for copy in loads[8:]:
        copy.wait()

    full_lane = lax.broadcasted_iota(jnp.int32, (128, LANES), 1)

    def edge(i, l):
        if i < 4:
            return fields[i, 2 : 2 + STEPS, :, cols[l]].reshape(128, LANES)
        return wetc[2 : 2 + STEPS, :, cols[l]].reshape(128, LANES).astype(f32)

    packed = None
    for i in range(5):
        both = jnp.where(full_lane < 64, edge(i, 0), edge(i, TILES - 1))
        both = pltpu.roll(both, 8 * i + 4, 1)
        packed = jnp.where(full_lane >= 8 * i, both, packed) if i else both
    edges[...] = packed.T

    pl.semaphore_wait(barrier, len(peers))

    def remote(src, dst, send, recv, device):
        copy = pltpu.make_async_remote_copy(
            src_ref=src, dst_ref=dst, send_sem=send, recv_sem=recv,
            device_id=device, device_id_type=MESH,
        )
        copy.start()
        return copy

    first, last = pl.ds(2, 2), pl.ds(STEPS, 2)
    past, ahead = pl.ds(0, 2), pl.ds(STEPS + 2, 2)
    halos_x = [
        remote(fields.at[:, first, 0, :], fields.at[:, ahead, 7, :],
               halo_send.at[0], halo_recv.at[0], x_dn),
        remote(fields.at[:, last, 7, :], fields.at[:, past, 0, :],
               halo_send.at[1], halo_recv.at[1], x_up),
        remote(wetc.at[first, 0, :], wetc.at[ahead, 7, :],
               halo_send.at[2], halo_recv.at[2], x_dn),
        remote(wetc.at[last, 7, :], wetc.at[past, 0, :],
               halo_send.at[3], halo_recv.at[3], x_up),
    ]
    halos_y = [
        remote(edges.at[pl.ds(0, 40), :], got.at[0], halo_send.at[4], halo_recv.at[4], y_dn),
        remote(edges.at[pl.ds(0, 40), :], got.at[1], halo_send.at[5], halo_recv.at[5], y_up),
    ]

    def gather(buf, slot, mates, base):
        return [
            remote(buf.at[slot], buf.at[slot], far_send.at[base + i], far_recv.at[base + i], mate)
            for i, mate in enumerate(mates)
        ]

    sent = list(halos_x) + list(halos_y)
    base_y = nz - 1
    base_x = base_y + ny - 1
    half = base_x + nx - 1

    coef_z_copies = gather(coef_z, zi, z_mates, 0)
    sent += coef_z_copies

    def x_faces(col, dst, start, count):
        w = [[fields[i, start + d, :, col] for d in range(4)] for i in range(3)]
        diff = [[0.5 * (w[i][d + 1] - w[i][d]) for d in range(3)] for i in range(3)]
        slope = [minmod(diff[i][0], diff[i][1]) for i in range(3)]
        for k in range(count):
            lefts, rights = [], []
            for i in range(3):
                after = minmod(diff[i][1], diff[i][2])
                lefts.append(w[i][1] + slope[i])
                rights.append(w[i][2] - after)
                slope[i] = after
                if k + 1 < count:
                    new = fields[i, start + k + 4, :, col]
                    w[i] = [None, w[i][2], w[i][3], new]
                    diff[i] = [None, diff[i][2], 0.5 * (new - w[i][2])]
            m0 = wetc[start + k + 1, :, col]
            m1 = wetc[start + k + 2, :, col]
            flux = face_flux(lefts, rights, (m0 * m1) > 0)
            for i in range(3):
                faces[i, start + k, :, col] = flux[i]

    def interior(l, carry):
        x_faces(pl.ds(pl.multiple_of(LANES * l, LANES), LANES), None, 2, STEPS - 3)
        return carry

    lax.fori_loop(0, TILES, interior, 0)

    push_factor = 0.5 * RATIO * GRAVITY

    def y_inner(t, carry):
        values = [[fields[i, t + 2, :, c] for c in cols] for i in range(3)]
        signed = [jnp.where(wetc[t + 2, :, c] > 0, h, -h) for c, h in zip(cols, values[0])]
        signed_next = lane_up(signed, lane)
        opened = [jnp.minimum(a, b) > 0.0 for a, b in zip(signed, signed_next)]
        lefts, rights = [], []
        for i in (0, 2, 1):
            w = values[i]
            after = lane_up(w, lane) if i else [jnp.abs(a) for a in signed_next]
            diff = [0.5 * (a - b) for a, b in zip(after, w)]
            slope = [minmod(a, b) for a, b in zip(lane_down(diff, lane), diff)]
            lefts.append([a + s for a, s in zip(w, slope)])
            rights.append(lane_up([a - s for a, s in zip(w, slope)], lane))
        flux = [
            face_flux([x[l] for x in lefts], [x[l] for x in rights], opened[l])
            for l in range(TILES)
        ]
        across = [flux[l][2] for l in range(TILES)]
        for l, before in enumerate(lane_down(across, lane)):
            ys[0, t, :, cols[l]] = flux[l][0]
            ys[1, t, :, cols[l]] = across[l] - before
            ys[2, t, :, cols[l]] = flux[l][1]
        return carry

    lax.fori_loop(0, STEPS, y_inner, 0, unroll=2)

    for copy in halos_y:
        copy.wait_recv()
    for i in range(5):
        high, low = 8 * i, 8 * i + 4
        seq[i, 0:2, :] = jnp.where(gy > 0, got[1, high + 2 : high + 4, :], 0.0)
        seq[i, 2:6, :] = edges[low : low + 4, :]
        seq[i, 8:12, :] = edges[high : high + 4, :]
        seq[i, 12:14, :] = jnp.where(gy < ny - 1, got[0, low : low + 2, :], 0.0)

    def rows_of(i, d):
        return seq[i, d : d + 16, :]

    lefts, rights = [], []
    for i in (0, 2, 1):
        w = [rows_of(i, d) for d in range(4)]
        diff = [0.5 * (w[d + 1] - w[d]) for d in range(3)]
        lefts.append(w[1] + minmod(diff[0], diff[1]))
        rights.append(w[2] - minmod(diff[1], diff[2]))
    flux = face_flux(lefts, rights, (rows_of(4, 1) * rows_of(4, 2)) > 0.5)
    for k, i in ((0, 0), (1, 2), (2, 1)):
        grad = pltpu.roll(flux[i], 15, 0) - flux[i]
        if k == 2:
            grad = grad + (push_factor * rows_of(0, 2)) * (rows_of(3, 3) - rows_of(3, 1))
        fix[k, 0:2, :] = grad[0:2, :]
        fix[k, 126:128, :] = grad[8:10, :]
    for k in (1, 0, 2):
        fixed[k] = fix[k].T

    for copy in halos_x:
        copy.wait_recv()

    def fill(ref, kind, both):
        for l in range(TILES):
            for t, source, rim, shift in (
                (0, STEPS, 0, 1), (1, STEPS + 1, 0, 1),
                (STEPS + 2, 2, 7, 7), (STEPS + 3, 3, 7, 7),
            ):
                if not both and t in (0, STEPS + 3):
                    continue
                gone = gx == 0 if rim == 0 else gx == ngx - 1
                border = jnp.where(gone, jnp.zeros((), kind), ref[t, :, cols[l]])
                ref[t, :, cols[l]] = jnp.where(
                    sub == rim, border, pltpu.roll(ref[source, :, cols[l]], shift, 0)
                )

    for i in range(4):
        fill(fields.at[i], f32, i < 3)
    fill(wetc, jnp.int32, False)

    def rim_faces(l, carry):
        col = pl.ds(pl.multiple_of(LANES * l, LANES), LANES)
        x_faces(col, None, 0, 2)
        x_faces(col, None, STEPS - 1, 2)
        return carry

    lax.fori_loop(0, TILES, rim_faces, 0)

    def patch(k, t, l, grad):
        if l == 0:
            return jnp.where(lane < 2, fixed[k, block(t), :], grad)
        if l == TILES - 1:
            return jnp.where(lane >= LANES - 2, fixed[k, block(t), :], grad)
        return grad

    def push_x(t, carry):
        out = []
        for l in range(TILES):
            uc, gc = carry[l]
            c = cols[l]
            m = wetc[t + 2, :, c].astype(f32)
            flow = faces[1, t + 1, :, c] - faces[1, t, :, c]
            rise = fields[3, t + 3, :, c] - fields[3, t + 1, :, c]
            px = m * (
                fields[1, t + 2, :, c] - flow - patch(1, t, l, ys[1, t, :, c])
                - (push_factor * fields[0, t + 2, :, c]) * rise
            )
            uc = uc + gc
            cx[l, block(t), :] = uc
            out.append((uc, gc + csx[l, block(t), :] * (uc - px)))
        return tuple(out)

    rest = tuple((zero, zero) for _ in range(TILES))
    ends = lax.fori_loop(0, STEPS, push_x, rest, unroll=4)

    before_x = []
    for l in range(TILES):
        windows = [[win_x[l, 4 * k + e] for e in range(4)] for k in range(3)]
        total, before = scan_vectors(windows, ends[l], sub)
        before_x.append(before)
        f, tau = win_x[l, 12], win_x[l, 13]
        rhs_z[zi, l : l + 1, :] = (total[0] - tau * total[1])[7:8, :]
        rhs_z[zi, 4 + l : 5 + l, :] = (-(f * total[1]))[7:8, :]
    rhs_z_copies = gather(rhs_z, zi, z_mates, half)
    sent += rhs_z_copies

    for copy in coef_z_copies:
        copy.wait_recv()

    def port(buf, k):
        return buf[k, 0:4, :], buf[k, 4:8, :], buf[k, 8:12, :]

    group_steps = []
    f, tau, mu = port(coef_z, 0)
    for k in range(1, nz):
        fk, tk, mk = port(coef_z, k)
        inv = 1.0 / (1.0 + tau * mk)
        a = fk * inv
        d = f * inv
        group_steps.append((a, a * tau, d, d * mk))
        f, tau, mu = f * a, tk + fk * (a * tau), mu + f * (d * mk)
    coef_x[xi, 0:4, :] = f
    coef_x[xi, 4:8, :] = tau
    coef_x[xi, 8:12, :] = mu
    coef_x_copies = gather(coef_x, xi, x_mates, base_x)
    sent += coef_x_copies

    def turn(dst, value):
        for s in range(8):
            dst[PITCH * s : PITCH * s + STEPS, :] = value[STEPS * s : STEPS * (s + 1), :]

    for l in range(TILES):
        turn(cty.at[l], csx[l].T)

    def coef_step_y(t, carry):
        out = []
        for l in range(TILES):
            ua, ga, ub, gb = carry[l]
            c = cty[l, pl.ds(t, 8, stride=PITCH), :]
            ua = ua + ga
            ub = ub + gb
            ay[l, block(t), :] = ua
            by[l, block(t), :] = ub
            out.append((ua, ga + c * ua, ub, gb + c * ub))
        return tuple(out)

    ends = lax.fori_loop(0, STEPS, coef_step_y, start_pieces(), unroll=2)
    total_y = None
    for l in range(TILES):
        ua, ga, ub, gb = ends[l]
        windows, total, before = scan_matrices((ua, ub, ga, gb), sub)
        for k in range(3):
            for e in range(4):
                win_y[l, 4 * k + e] = windows[k][e]
        for e in range(4):
            pre_y[l, e] = before[e]
            win_y[l, 12 + e] = total[e]
        total_y = total if total_y is None else matmul2(total, total_y)
    f = 1.0 / total_y[3]
    coef_y_row = (f, total_y[1] * f, total_y[2] * f)
    for e in range(3):
        coef_y[gy, e : e + 1, :] = coef_y_row[e][7:8, :]
        row_y[e] = coef_y_row[e]
    coef_y_copies = gather(coef_y, gy, y_mates, base_y)
    sent += coef_y_copies

    def depth_and_q(t, carry):
        mass, normal, bed = (
            [ref[t + d, :, c] for c in cols] for ref, d in ((ys.at[0], 0), (ys.at[2], 0), (fields.at[3], 2))
        )
        mass_past, normal_past, bed_past = (lane_down(x, lane) for x in (mass, normal, bed))
        bed_next = lane_up(bed, lane)
        for l in range(TILES):
            c = cols[l]
            m = wetc[t + 2, :, c].astype(f32)
            grad = patch(0, t, l, mass[l] - mass_past[l])
            os_n[t, :, c] = m * (faces[0, t + 1, :, c] - faces[0, t, :, c] + grad)
            slope = (push_factor * fields[0, t + 2, :, c]) * (bed_next[l] - bed_past[l])
            grad = patch(2, t, l, normal[l] - normal_past[l] + slope)
            flow = faces[2, t + 1, :, c] - faces[2, t, :, c]
            qs[l, block(t), :] = m * (fields[2, t + 2, :, c] - flow - grad)
        return carry

    lax.fori_loop(0, STEPS, depth_and_q, 0, unroll=2)

    for l in range(TILES):
        turn(qt.at[l], qs[l].T)

    def rhs_step_y(t, carry):
        out = []
        for l in range(TILES):
            uc, gc = carry[l]
            where = pl.ds(t, 8, stride=PITCH)
            uc = uc + gc
            cy[l, block(t), :] = uc
            out.append((uc, gc + cty[l, where, :] * (uc - qt[l, where, :])))
        return tuple(out)

    ends = lax.fori_loop(0, STEPS, rhs_step_y, rest, unroll=2)
    before_y, totals_y = [], []
    sum_y = None
    for l in range(TILES):
        windows = [[win_y[l, 4 * k + e] for e in range(4)] for k in range(3)]
        total, before = scan_vectors(windows, ends[l], sub)
        before_y.append(before)
        totals_y.append(total)
        if sum_y is None:
            sum_y = total
        else:
            moved = apply2([win_y[l, 12 + e] for e in range(4)], sum_y)
            sum_y = (total[0] + moved[0], total[1] + moved[1])
    rhs_y[gy, 0:1, :] = (sum_y[0] - row_y[1] * sum_y[1])[7:8, :]
    rhs_y[gy, 1:2, :] = (-(row_y[0] * sum_y[1]))[7:8, :]
    rhs_y_copies = gather(rhs_y, gy, y_mates, half + base_y)
    sent += rhs_y_copies

    for copy in rhs_z_copies:
        copy.wait_recv()
    rhs_in_z = [(rhs_z[k, 0:4, :], rhs_z[k, 4:8, :]) for k in range(nz)]
    w1, w2 = rhs_in_z[0]
    for k in range(1, nz):
        a, at, d, dm = group_steps[k - 1]
        k1, k2 = rhs_in_z[k]
        w1, w2 = k1 + a * w1 + at * k2, w2 + d * k2 - dm * w1
    rhs_x[xi, 0:4, :] = w1
    rhs_x[xi, 4:8, :] = w2
    rhs_x_copies = gather(rhs_x, xi, x_mates, half + base_x)
    sent += rhs_x_copies

    def left_chain(ports, mine, rho):
        steps = []
        for k in range(len(ports)):
            fk, tk, mk = ports[k]
            inv = 1.0 / (1.0 + rho * mk)
            a = fk * inv
            steps.append((a, a * rho))
            rho = jnp.where(k < mine, tk + fk * (a * rho), rho)
        return rho, steps

    def right_chain(ports, mine, back):
        steps = [None] * len(ports)
        for k in reversed(range(len(ports))):
            fk, tk, mk = ports[k]
            inv = 1.0 / (1.0 + tk * back)
            a = fk * inv
            steps[k] = (a, a * back)
            back = jnp.where(k >= mine, mk + fk * (a * back), back)
        return back, steps

    def left_values(steps, rhs, mine, w):
        for k in range(len(steps)):
            a, b = steps[k]
            w1, w2 = rhs[k]
            w = jnp.where(k < mine, w1 + a * w + b * w2, w)
        return w

    def right_values(steps, rhs, mine, w):
        for k in reversed(range(len(steps))):
            a, b = steps[k]
            w1, w2 = rhs[k]
            w = jnp.where(k >= mine, w2 + a * w - b * w1, w)
        return w

    def meet(rho, back, wl, wr):
        inv = 1.0 / (1.0 + rho * back)
        return (rho * wr + wl) * inv, (wr - back * wl) * inv

    for copy in coef_y_copies:
        copy.wait_recv()
    ports_y = [tuple(coef_y[k, e : e + 1, :] for e in range(3)) for k in range(ny)]
    row_zero = jnp.zeros((1, LANES), f32)
    rho_y, left_y = left_chain(ports_y, gy, row_zero)
    back_y, right_y = right_chain(ports_y, gy, row_zero + 1.0)

    for copy in coef_x_copies:
        copy.wait_recv()
    ports_x = [port(coef_x, k) for k in range(nx)]
    ports_z = [port(coef_z, k) for k in range(nz)]
    four_zero = jnp.zeros((4, LANES), f32)
    rho_x, left_x = left_chain(ports_x, xi, four_zero)
    back_x, right_x = right_chain(ports_x, xi + 1, four_zero + 1.0)
    rho_z, left_z = left_chain(ports_z, zi, rho_x)
    back_z, right_z = right_chain(ports_z, zi, back_x)

    for copy in rhs_y_copies:
        copy.wait_recv()
    rhs_in_y = [(rhs_y[k, 0:1, :], rhs_y[k, 1:2, :]) for k in range(ny)]
    wl = left_values(left_y, rhs_in_y, gy, row_zero)
    wr = right_values(right_y, rhs_in_y, gy, row_zero)
    state = meet(rho_y, back_y, wl, wr)
    starts = []
    for l in range(TILES):
        before = [pre_y[l, e] for e in range(4)]
        wide = tuple(jnp.broadcast_to(s, (8, LANES)) for s in state)
        moved = apply2(before, wide)
        starts.append((moved[0] + before_y[l][0], moved[1] + before_y[l][1]))
        if l < TILES - 1:
            moved = apply2([win_y[l, 12 + e] for e in range(4)], wide)
            state = tuple((moved[e] + totals_y[l][e])[7:8, :] for e in range(2))

    def finish_y(t, carry):
        for l in range(TILES):
            at = block(t)
            vt[l, pl.ds(t, 8, stride=PITCH), :] = (
                ay[l, at, :] * starts[l][0] + by[l, at, :] * starts[l][1] + cy[l, at, :]
            )
        return carry

    lax.fori_loop(0, STEPS, finish_y, 0, unroll=2)
    for l in range(TILES):
        line = [vt[l, PITCH * s : PITCH * s + STEPS, :] for s in range(8)]
        natural = jnp.concatenate(line, axis=0).T
        for t in range(STEPS):
            os_u[l, pl.ds(t, 8, stride=STEPS), :] = natural[8 * t : 8 * t + 8, :]
        v_out[:, cols[l]] = os_u[l]

    for l in range(TILES):
        for t in range(STEPS):
            os_v[l, pl.ds(t, 8, stride=STEPS), :] = os_n[t, :, cols[l]]
        corr_out[:, cols[l]] = os_v[l]

    own_l = left_values(left_z, rhs_in_z, zi, four_zero)
    own_r = right_values(right_z, rhs_in_z, zi, four_zero)
    gain_l = gain_r = four_zero + 1.0
    for k in range(nz):
        gain_l = jnp.where(k < zi, gain_l * left_z[k][0], gain_l)
        gain_r = jnp.where(k >= zi, gain_r * right_z[k][0], gain_r)
    for copy in rhs_x_copies:
        copy.wait_recv()
    rhs_in_x = [(rhs_x[k, 0:4, :], rhs_x[k, 4:8, :]) for k in range(nx)]
    wl = left_values(left_x, rhs_in_x, xi, four_zero)
    wr = right_values(right_x, rhs_in_x, xi + 1, four_zero)
    wl = own_l + gain_l * wl
    wr = own_r + gain_r * wr
    state = meet(rho_z, back_z, wl, wr)
    for l in range(TILES):
        before = [pre_x[l, e] for e in range(4)]
        wide = tuple(jnp.broadcast_to(s[l : l + 1, :], (8, LANES)) for s in state)
        moved = apply2(before, wide)
        u0, g0 = moved[0] + before_x[l][0], moved[1] + before_x[l][1]
        for t in range(STEPS):
            at = pl.ds(8 * t, 8)
            os_u[l, pl.ds(t, 8, stride=STEPS), :] = ax[l, at, :] * u0 + bx[l, at, :] * g0 + cx[l, at, :]
        u_out[:, cols[l]] = os_u[l]

    for copy in sent:
        copy.wait_send()


def predictor(sizes, spring, depth, momentum_x, momentum_y, bed, wet):
    nx, nz, ny = sizes
    rows, cols = depth.shape
    shape = (8, STEPS, cols)
    flat = jax.ShapeDtypeStruct((rows, cols), f32)
    hbm = pl.BlockSpec(memory_space=pl.ANY)
    tile = (TILES, 128, LANES)
    wide = (TILES, 8 * PITCH, LANES)
    far = 2 * (nz + nx + ny - 3)
    results = pl.pallas_call(
        functools.partial(kernel, sizes, spring),
        out_shape=(flat, flat, flat),
        in_specs=[hbm] * 5,
        out_specs=[pl.BlockSpec(memory_space=pltpu.VMEM)] * 3,
        scratch_shapes=[
            pltpu.VMEM((4, STEPS + 4, 8, cols), f32),
            pltpu.VMEM((STEPS + 4, 8, cols), jnp.int32),
            pltpu.VMEM(tile, f32),
            pltpu.VMEM(wide, f32),
            pltpu.VMEM(tile, f32),
            pltpu.VMEM(tile, f32),
            pltpu.VMEM(tile, f32),
            pltpu.VMEM(tile, f32),
            pltpu.VMEM(tile, f32),
            pltpu.VMEM(tile, f32),
            pltpu.VMEM((TILES, 16, 8, LANES), f32),
            pltpu.VMEM((TILES, 16, 8, LANES), f32),
            pltpu.VMEM((TILES, 4, 8, LANES), f32),
            pltpu.VMEM((TILES, 4, 8, LANES), f32),
            pltpu.VMEM((3, STEPS + 1, 8, cols), f32),
            pltpu.VMEM(tile, f32),
            pltpu.VMEM(wide, f32),
            pltpu.VMEM(wide, f32),
            pltpu.VMEM((STEPS, 8, cols), f32),
            pltpu.VMEM(tile, f32),
            pltpu.VMEM(tile, f32),
            pltpu.VMEM((3, STEPS, 8, cols), f32),
            pltpu.VMEM((128, LANES), f32),
            pltpu.VMEM((2, 40, LANES), f32),
            pltpu.VMEM((5, 24, LANES), f32),
            pltpu.VMEM((3, 128, LANES), f32),
            pltpu.VMEM((3, 128, LANES), f32),
            pltpu.VMEM((nz, 16, LANES), f32),
            pltpu.VMEM((nx, 16, LANES), f32),
            pltpu.VMEM((ny, 8, LANES), f32),
            pltpu.VMEM((nz, 8, LANES), f32),
            pltpu.VMEM((nx, 8, LANES), f32),
            pltpu.VMEM((ny, 8, LANES), f32),
            pltpu.VMEM((3, 8, LANES), f32),
            pltpu.SemaphoreType.DMA((40,)),
            pltpu.SemaphoreType.DMA((6,)),
            pltpu.SemaphoreType.DMA((6,)),
            pltpu.SemaphoreType.DMA((far,)),
            pltpu.SemaphoreType.DMA((far,)),
        ],
        compiler_params=pltpu.CompilerParams(collective_id=0, has_side_effects=True, vmem_limit_bytes=55_700_000),
    )(*(a.reshape(shape) for a in (depth, momentum_x, momentum_y, bed, wet)))
    corr, flux_u, flux_v = results
    return (depth - corr, flux_u / depth, flux_v / depth)


def solution(mesh):
    ngx, ny = mesh.shape["gx"], mesh.shape["gy"]
    nz = 8 if ngx % 8 == 0 else max(1, ngx // 2)
    sizes = (ngx // nz, nz, ny)
    scale = (4096 / 4.0) ** 2 / 3.0
    place = P("gx", "gy")
    return jax.shard_map(
        functools.partial(predictor, sizes, 1.0 / scale),
        mesh=mesh,
        in_specs=(place,) * 5,
        out_specs=(place,) * 3,
        check_vma=False,
    )
```

```python
import functools

import jax
import jax.numpy as jnp
from jax import lax
from jax.experimental import pallas as pl
from jax.experimental.pallas import tpu as pltpu
from jax.sharding import PartitionSpec as P

MESH = pl.DeviceIdType.MESH
GRAVITY = 9.81
ROOT_G = GRAVITY**0.5
RATIO = 0.05
LANES = 128
TILES = 4
STEPS = 16
PITCH = 20
f32 = jnp.float32


def minmod(a, c):
    return jnp.maximum(jnp.minimum(a, c), 0.0) + jnp.minimum(jnp.maximum(a, c), 0.0)


def face_flux(lefts, rights, opened):
    hl, pl_, ql = lefts
    hr, pr, qr = rights
    sl = jnp.where(opened, hl, 1.0)
    sr = jnp.where(opened, hr, 1.0)
    il = lax.rsqrt(sl)
    ir = lax.rsqrt(sr)
    ul = pl_ * (il * il)
    ur = pr * (ir * ir)
    fast = jnp.maximum(
        jnp.abs(ul) + (ROOT_G * sl) * il, jnp.abs(ur) + (ROOT_G * sr) * ir
    )
    factor = jnp.where(opened, 0.5 * RATIO, 0.0)
    mass = (pl_ + pr) - fast * (hr - hl)
    normal = (pl_ * ul + pr * ur) + (0.5 * GRAVITY) * (sl * sl + sr * sr) - fast * (pr - pl_)
    across = (ql * ul + qr * ur) - fast * (qr - ql)
    return factor * mass, factor * normal, factor * across


def lane_up(tiles, lane):
    n = len(tiles)
    rolled = [pltpu.roll(t, LANES - 1, 1) for t in tiles]
    return [jnp.where(lane == LANES - 1, rolled[(i + 1) % n], rolled[i]) for i in range(n)]


def lane_down(tiles, lane):
    n = len(tiles)
    rolled = [pltpu.roll(t, 1, 1) for t in tiles]
    return [jnp.where(lane == 0, rolled[(i - 1) % n], rolled[i]) for i in range(n)]


def matmul2(m, a):
    m11, m12, m21, m22 = m
    a11, a12, a21, a22 = a
    return (
        m11 * a11 + m12 * a21,
        m11 * a12 + m12 * a22,
        m21 * a11 + m22 * a21,
        m21 * a12 + m22 * a22,
    )


def apply2(m, v):
    return (m[0] * v[0] + m[1] * v[1], m[2] * v[0] + m[3] * v[1])


def shifted(values, k, sub, first):
    return tuple(
        jnp.where(sub >= k, pltpu.roll(v, k, 0), f) for v, f in zip(values, first)
    )


IDENT = (1.0, 0.0, 0.0, 1.0)


def scan_matrices(m, sub):
    windows = []
    for k in (1, 2, 4):
        windows.append(m)
        m = matmul2(m, shifted(m, k, sub, IDENT))
    return windows, m, shifted(m, 1, sub, IDENT)


def scan_vectors(windows, v, sub):
    for k, m in zip((1, 2, 4), windows):
        moved = apply2(m, shifted(v, k, sub, (0.0, 0.0)))
        v = (v[0] + moved[0], v[1] + moved[1])
    return v, shifted(v, 1, sub, (0.0, 0.0))


def kernel(
    sizes, spring,
    h_in, p_in, q_in, b_in, m_in,
    corr_out, u_out, v_out,
    fields, wetc, csx, cty, ax, bx, cx, ay, by, cy, win_x, win_y, pre_x, pre_y,
    faces, qs, qt, vt, os_n, os_u, os_v, ys, edges, got, seq, fix, fixed,
    coef_z, coef_x, coef_y, rhs_z, rhs_x, rhs_y, row_y,
    load_sem, halo_send, halo_recv, far_send, far_recv,
):
    nx, nz, ny = sizes
    gx = lax.axis_index("gx")
    gy = lax.axis_index("gy")
    xi = lax.div(gx, nz)
    zi = lax.rem(gx, nz)
    ngx = nx * nz

    x_up = (lax.rem(gx + 1, ngx), gy)
    x_dn = (lax.rem(gx + ngx - 1, ngx), gy)
    y_up = (gx, lax.rem(gy + 1, ny))
    y_dn = (gx, lax.rem(gy + ny - 1, ny))
    z_mates = [(xi * nz + lax.rem(zi + k, nz), gy) for k in range(1, nz)]
    x_mates = [(lax.rem(xi + k, nx) * nz + zi, gy) for k in range(1, nx)]
    y_mates = [(gx, lax.rem(gy + k, ny)) for k in range(1, ny)]

    barrier = pltpu.get_barrier_semaphore()
    far_first = sorted(range(nz - 1), key=lambda k: abs(k + 1 - nz // 2))
    peers = [z_mates[k] for k in far_first] + [x_up, x_dn] + x_mates + y_mates
    for peer in peers:
        pl.semaphore_signal(barrier, inc=1, device_id=peer, device_id_type=MESH)

    def load(i, src):
        copies = []
        for s in range(8):
            rows = pl.ds(2, STEPS)
            dst = fields.at[i, rows, s, :] if i < 4 else wetc.at[rows, s, :]
            copy = pltpu.make_async_copy(src.at[s], dst, load_sem.at[8 * i + s])
            copy.start()
            copies.append(copy)
        return copies

    loads = load(0, h_in)
    for i, src in ((1, p_in), (2, q_in), (3, b_in), (4, m_in)):
        loads += load(i, src)

    sub = lax.broadcasted_iota(jnp.int32, (8, LANES), 0)
    lane = lax.broadcasted_iota(jnp.int32, (8, LANES), 1)
    zero = jnp.where(lane + sub < 0, 1.0, 0.0)
    one = jnp.where(lane + sub < 0, 0.0, 1.0)
    cols = [pl.ds(LANES * l, LANES) for l in range(TILES)]

    def block(t):
        return pl.ds(pl.multiple_of(8 * t, 8), 8)

    for copy in loads[:8]:
        copy.wait()

    def start_pieces():
        return tuple((one, zero, zero, one) for _ in range(TILES))

    def coef_step_x(t, carry):
        out = []
        for l in range(TILES):
            ua, ga, ub, gb = carry[l]
            h = fields[0, t + 2, :, cols[l]]
            c = spring / (h * h)
            csx[l, block(t), :] = c
            ua = ua + ga
            ub = ub + gb
            ax[l, block(t), :] = ua
            bx[l, block(t), :] = ub
            out.append((ua, ga + c * ua, ub, gb + c * ub))
        return tuple(out)

    ends = lax.fori_loop(0, STEPS, coef_step_x, start_pieces(), unroll=8)
    for l in range(TILES):
        ua, ga, ub, gb = ends[l]
        windows, total, before = scan_matrices((ua, ub, ga, gb), sub)
        for k in range(3):
            for e in range(4):
                win_x[l, 4 * k + e] = windows[k][e]
        for e in range(4):
            pre_x[l, e] = before[e]
        f = 1.0 / total[3]
        coef_x_row = (f, total[1] * f, total[2] * f)
        for e in range(3):
            coef_z[zi, 4 * e + l : 4 * e + l + 1, :] = coef_x_row[e][7:8, :]
            win_x[l, 12 + e] = coef_x_row[e]

    seq[...] = jnp.zeros((5, 24, LANES), f32)
    fix[...] = jnp.zeros((3, 128, LANES), f32)

    for copy in loads[8:]:
        copy.wait()

    full_lane = lax.broadcasted_iota(jnp.int32, (128, LANES), 1)

    def edge(i, l):
        if i < 4:
            return fields[i, 2 : 2 + STEPS, :, cols[l]].reshape(128, LANES)
        return wetc[2 : 2 + STEPS, :, cols[l]].reshape(128, LANES).astype(f32)

    packed = None
    for i in range(5):
        both = jnp.where(full_lane < 64, edge(i, 0), edge(i, TILES - 1))
        both = pltpu.roll(both, 8 * i + 4, 1)
        packed = jnp.where(full_lane >= 8 * i, both, packed) if i else both
    edges[...] = packed.T

    pl.semaphore_wait(barrier, len(peers))

    def remote(src, dst, send, recv, device):
        copy = pltpu.make_async_remote_copy(
            src_ref=src, dst_ref=dst, send_sem=send, recv_sem=recv,
            device_id=device, device_id_type=MESH,
        )
        copy.start()
        return copy

    first, last = pl.ds(2, 2), pl.ds(STEPS, 2)
    past, ahead = pl.ds(0, 2), pl.ds(STEPS + 2, 2)
    halos_x = [
        remote(fields.at[:, first, 0, :], fields.at[:, ahead, 7, :],
               halo_send.at[0], halo_recv.at[0], x_dn),
        remote(fields.at[:, last, 7, :], fields.at[:, past, 0, :],
               halo_send.at[1], halo_recv.at[1], x_up),
        remote(wetc.at[first, 0, :], wetc.at[ahead, 7, :],
               halo_send.at[2], halo_recv.at[2], x_dn),
        remote(wetc.at[last, 7, :], wetc.at[past, 0, :],
               halo_send.at[3], halo_recv.at[3], x_up),
    ]
    halos_y = [
        remote(edges.at[pl.ds(0, 40), :], got.at[0], halo_send.at[4], halo_recv.at[4], y_dn),
        remote(edges.at[pl.ds(0, 40), :], got.at[1], halo_send.at[5], halo_recv.at[5], y_up),
    ]

    def gather(buf, slot, mates, base):
        return [
            remote(buf.at[slot], buf.at[slot], far_send.at[base + i], far_recv.at[base + i], mate)
            for i, mate in enumerate(mates)
        ]

    sent = list(halos_x) + list(halos_y)
    base_y = nz - 1
    base_x = base_y + ny - 1
    half = base_x + nx - 1

    coef_z_copies = gather(coef_z, zi, z_mates, 0)
    sent += coef_z_copies

    def x_faces(col, dst, start, count):
        w = [[fields[i, start + d, :, col] for d in range(4)] for i in range(3)]
        diff = [[0.5 * (w[i][d + 1] - w[i][d]) for d in range(3)] for i in range(3)]
        slope = [minmod(diff[i][0], diff[i][1]) for i in range(3)]
        for k in range(count):
            lefts, rights = [], []
            for i in range(3):
                after = minmod(diff[i][1], diff[i][2])
                lefts.append(w[i][1] + slope[i])
                rights.append(w[i][2] - after)
                slope[i] = after
                if k + 1 < count:
                    new = fields[i, start + k + 4, :, col]
                    w[i] = [None, w[i][2], w[i][3], new]
                    diff[i] = [None, diff[i][2], 0.5 * (new - w[i][2])]
            m0 = wetc[start + k + 1, :, col]
            m1 = wetc[start + k + 2, :, col]
            flux = face_flux(lefts, rights, (m0 * m1) > 0)
            for i in range(3):
                faces[i, start + k, :, col] = flux[i]

    def interior(l, carry):
        x_faces(pl.ds(pl.multiple_of(LANES * l, LANES), LANES), None, 2, STEPS - 3)
        return carry

    lax.fori_loop(0, TILES, interior, 0, unroll=2)

    push_factor = 0.5 * RATIO * GRAVITY

    def y_inner(t, carry):
        values = [[fields[i, t + 2, :, c] for c in cols] for i in range(3)]
        signed = [jnp.where(wetc[t + 2, :, c] > 0, h, -h) for c, h in zip(cols, values[0])]
        signed_next = lane_up(signed, lane)
        opened = [jnp.minimum(a, b) > 0.0 for a, b in zip(signed, signed_next)]
        lefts, rights = [], []
        for i in (0, 2, 1):
            w = values[i]
            after = lane_up(w, lane) if i else [jnp.abs(a) for a in signed_next]
            diff = [0.5 * (a - b) for a, b in zip(after, w)]
            slope = [minmod(a, b) for a, b in zip(lane_down(diff, lane), diff)]
            lefts.append([a + s for a, s in zip(w, slope)])
            rights.append(lane_up([a - s for a, s in zip(w, slope)], lane))
        flux = [
            face_flux([x[l] for x in lefts], [x[l] for x in rights], opened[l])
            for l in range(TILES)
        ]
        across = [flux[l][2] for l in range(TILES)]
        for l, before in enumerate(lane_down(across, lane)):
            ys[0, t, :, cols[l]] = flux[l][0]
            ys[1, t, :, cols[l]] = across[l] - before
            ys[2, t, :, cols[l]] = flux[l][1]
        return carry

    lax.fori_loop(0, STEPS, y_inner, 0, unroll=2)

    for copy in halos_y:
        copy.wait_recv()
    for i in range(5):
        high, low = 8 * i, 8 * i + 4
        seq[i, 0:2, :] = jnp.where(gy > 0, got[1, high + 2 : high + 4, :], 0.0)
        seq[i, 2:6, :] = edges[low : low + 4, :]
        seq[i, 8:12, :] = edges[high : high + 4, :]
        seq[i, 12:14, :] = jnp.where(gy < ny - 1, got[0, low : low + 2, :], 0.0)

    def rows_of(i, d):
        return seq[i, d : d + 16, :]

    lefts, rights = [], []
    for i in (0, 2, 1):
        w = [rows_of(i, d) for d in range(4)]
        diff = [0.5 * (w[d + 1] - w[d]) for d in range(3)]
        lefts.append(w[1] + minmod(diff[0], diff[1]))
        rights.append(w[2] - minmod(diff[1], diff[2]))
    flux = face_flux(lefts, rights, (rows_of(4, 1) * rows_of(4, 2)) > 0.5)
    for k, i in ((0, 0), (1, 2), (2, 1)):
        grad = pltpu.roll(flux[i], 15, 0) - flux[i]
        if k == 2:
            grad = grad + (push_factor * rows_of(0, 2)) * (rows_of(3, 3) - rows_of(3, 1))
        fix[k, 0:2, :] = grad[0:2, :]
        fix[k, 126:128, :] = grad[8:10, :]
    for k in (1, 0, 2):
        fixed[k] = fix[k].T

    for copy in halos_x:
        copy.wait_recv()

    def fill(ref, kind, both):
        for l in range(TILES):
            for t, source, rim, shift in (
                (0, STEPS, 0, 1), (1, STEPS + 1, 0, 1),
                (STEPS + 2, 2, 7, 7), (STEPS + 3, 3, 7, 7),
            ):
                if not both and t in (0, STEPS + 3):
                    continue
                gone = gx == 0 if rim == 0 else gx == ngx - 1
                border = jnp.where(gone, jnp.zeros((), kind), ref[t, :, cols[l]])
                ref[t, :, cols[l]] = jnp.where(
                    sub == rim, border, pltpu.roll(ref[source, :, cols[l]], shift, 0)
                )

    for i in range(4):
        fill(fields.at[i], f32, i < 3)
    fill(wetc, jnp.int32, False)

    def rim_faces(l, carry):
        col = pl.ds(pl.multiple_of(LANES * l, LANES), LANES)
        x_faces(col, None, 0, 2)
        x_faces(col, None, STEPS - 1, 2)
        return carry

    lax.fori_loop(0, TILES, rim_faces, 0, unroll=2)

    def patch(k, t, l, grad):
        if l == 0:
            return jnp.where(lane < 2, fixed[k, block(t), :], grad)
        if l == TILES - 1:
            return jnp.where(lane >= LANES - 2, fixed[k, block(t), :], grad)
        return grad

    def push_x(t, carry):
        out = []
        for l in range(TILES):
            uc, gc = carry[l]
            c = cols[l]
            m = wetc[t + 2, :, c].astype(f32)
            flow = faces[1, t + 1, :, c] - faces[1, t, :, c]
            rise = fields[3, t + 3, :, c] - fields[3, t + 1, :, c]
            px = m * (
                fields[1, t + 2, :, c] - flow - patch(1, t, l, ys[1, t, :, c])
                - (push_factor * fields[0, t + 2, :, c]) * rise
            )
            uc = uc + gc
            cx[l, block(t), :] = uc
            out.append((uc, gc + csx[l, block(t), :] * (uc - px)))
        return tuple(out)

    rest = tuple((zero, zero) for _ in range(TILES))
    ends = lax.fori_loop(0, STEPS, push_x, rest, unroll=8)

    before_x = []
    for l in range(TILES):
        windows = [[win_x[l, 4 * k + e] for e in range(4)] for k in range(3)]
        total, before = scan_vectors(windows, ends[l], sub)
        before_x.append(before)
        f, tau = win_x[l, 12], win_x[l, 13]
        rhs_z[zi, l : l + 1, :] = (total[0] - tau * total[1])[7:8, :]
        rhs_z[zi, 4 + l : 5 + l, :] = (-(f * total[1]))[7:8, :]
    rhs_z_copies = gather(rhs_z, zi, z_mates, half)
    sent += rhs_z_copies

    for copy in coef_z_copies:
        copy.wait_recv()

    def port(buf, k):
        return buf[k, 0:4, :], buf[k, 4:8, :], buf[k, 8:12, :]

    group_steps = []
    f, tau, mu = port(coef_z, 0)
    for k in range(1, nz):
        fk, tk, mk = port(coef_z, k)
        inv = 1.0 / (1.0 + tau * mk)
        a = fk * inv
        d = f * inv
        group_steps.append((a, a * tau, d, d * mk))
        f, tau, mu = f * a, tk + fk * (a * tau), mu + f * (d * mk)
    coef_x[xi, 0:4, :] = f
    coef_x[xi, 4:8, :] = tau
    coef_x[xi, 8:12, :] = mu
    coef_x_copies = gather(coef_x, xi, x_mates, base_x)
    sent += coef_x_copies

    def turn(dst, value):
        for s in range(8):
            dst[PITCH * s : PITCH * s + STEPS, :] = value[STEPS * s : STEPS * (s + 1), :]

    for l in range(TILES):
        turn(cty.at[l], csx[l].T)

    def coef_step_y(t, carry):
        out = []
        for l in range(TILES):
            ua, ga, ub, gb = carry[l]
            c = cty[l, pl.ds(t, 8, stride=PITCH), :]
            ua = ua + ga
            ub = ub + gb
            ay[l, block(t), :] = ua
            by[l, block(t), :] = ub
            out.append((ua, ga + c * ua, ub, gb + c * ub))
        return tuple(out)

    ends = lax.fori_loop(0, STEPS, coef_step_y, start_pieces(), unroll=4)
    total_y = None
    for l in range(TILES):
        ua, ga, ub, gb = ends[l]
        windows, total, before = scan_matrices((ua, ub, ga, gb), sub)
        for k in range(3):
            for e in range(4):
                win_y[l, 4 * k + e] = windows[k][e]
        for e in range(4):
            pre_y[l, e] = before[e]
            win_y[l, 12 + e] = total[e]
        total_y = total if total_y is None else matmul2(total, total_y)
    f = 1.0 / total_y[3]
    coef_y_row = (f, total_y[1] * f, total_y[2] * f)
    for e in range(3):
        coef_y[gy, e : e + 1, :] = coef_y_row[e][7:8, :]
        row_y[e] = coef_y_row[e]
    coef_y_copies = gather(coef_y, gy, y_mates, base_y)
    sent += coef_y_copies

    def depth_and_q(t, carry):
        mass, normal, bed = (
            [ref[t + d, :, c] for c in cols] for ref, d in ((ys.at[0], 0), (ys.at[2], 0), (fields.at[3], 2))
        )
        mass_past, normal_past, bed_past = (lane_down(x, lane) for x in (mass, normal, bed))
        bed_next = lane_up(bed, lane)
        for l in range(TILES):
            c = cols[l]
            m = wetc[t + 2, :, c].astype(f32)
            grad = patch(0, t, l, mass[l] - mass_past[l])
            os_n[t, :, c] = m * (faces[0, t + 1, :, c] - faces[0, t, :, c] + grad)
            slope = (push_factor * fields[0, t + 2, :, c]) * (bed_next[l] - bed_past[l])
            grad = patch(2, t, l, normal[l] - normal_past[l] + slope)
            flow = faces[2, t + 1, :, c] - faces[2, t, :, c]
            qs[l, block(t), :] = m * (fields[2, t + 2, :, c] - flow - grad)
        return carry

    lax.fori_loop(0, STEPS, depth_and_q, 0, unroll=2)

    for l in range(TILES):
        turn(qt.at[l], qs[l].T)

    def rhs_step_y(t, carry):
        out = []
        for l in range(TILES):
            uc, gc = carry[l]
            where = pl.ds(t, 8, stride=PITCH)
            uc = uc + gc
            cy[l, block(t), :] = uc
            out.append((uc, gc + cty[l, where, :] * (uc - qt[l, where, :])))
        return tuple(out)

    ends = lax.fori_loop(0, STEPS, rhs_step_y, rest, unroll=4)
    before_y, totals_y = [], []
    sum_y = None
    for l in range(TILES):
        windows = [[win_y[l, 4 * k + e] for e in range(4)] for k in range(3)]
        total, before = scan_vectors(windows, ends[l], sub)
        before_y.append(before)
        totals_y.append(total)
        if sum_y is None:
            sum_y = total
        else:
            moved = apply2([win_y[l, 12 + e] for e in range(4)], sum_y)
            sum_y = (total[0] + moved[0], total[1] + moved[1])
    rhs_y[gy, 0:1, :] = (sum_y[0] - row_y[1] * sum_y[1])[7:8, :]
    rhs_y[gy, 1:2, :] = (-(row_y[0] * sum_y[1]))[7:8, :]
    rhs_y_copies = gather(rhs_y, gy, y_mates, half + base_y)
    sent += rhs_y_copies

    for copy in rhs_z_copies:
        copy.wait_recv()
    rhs_in_z = [(rhs_z[k, 0:4, :], rhs_z[k, 4:8, :]) for k in range(nz)]
    w1, w2 = rhs_in_z[0]
    for k in range(1, nz):
        a, at, d, dm = group_steps[k - 1]
        k1, k2 = rhs_in_z[k]
        w1, w2 = k1 + a * w1 + at * k2, w2 + d * k2 - dm * w1
    rhs_x[xi, 0:4, :] = w1
    rhs_x[xi, 4:8, :] = w2
    rhs_x_copies = gather(rhs_x, xi, x_mates, half + base_x)
    sent += rhs_x_copies

    def left_chain(ports, mine, rho):
        steps = []
        for k in range(len(ports)):
            fk, tk, mk = ports[k]
            inv = 1.0 / (1.0 + rho * mk)
            a = fk * inv
            steps.append((a, a * rho))
            rho = jnp.where(k < mine, tk + fk * (a * rho), rho)
        return rho, steps

    def right_chain(ports, mine, back):
        steps = [None] * len(ports)
        for k in reversed(range(len(ports))):
            fk, tk, mk = ports[k]
            inv = 1.0 / (1.0 + tk * back)
            a = fk * inv
            steps[k] = (a, a * back)
            back = jnp.where(k >= mine, mk + fk * (a * back), back)
        return back, steps

    def left_values(steps, rhs, mine, w):
        for k in range(len(steps)):
            a, b = steps[k]
            w1, w2 = rhs[k]
            w = jnp.where(k < mine, w1 + a * w + b * w2, w)
        return w

    def right_values(steps, rhs, mine, w):
        for k in reversed(range(len(steps))):
            a, b = steps[k]
            w1, w2 = rhs[k]
            w = jnp.where(k >= mine, w2 + a * w - b * w1, w)
        return w

    def meet(rho, back, wl, wr):
        inv = 1.0 / (1.0 + rho * back)
        return (rho * wr + wl) * inv, (wr - back * wl) * inv

    for copy in coef_y_copies:
        copy.wait_recv()
    ports_y = [tuple(coef_y[k, e : e + 1, :] for e in range(3)) for k in range(ny)]
    row_zero = jnp.zeros((1, LANES), f32)
    rho_y, left_y = left_chain(ports_y, gy, row_zero)
    back_y, right_y = right_chain(ports_y, gy, row_zero + 1.0)

    for copy in coef_x_copies:
        copy.wait_recv()
    ports_x = [port(coef_x, k) for k in range(nx)]
    ports_z = [port(coef_z, k) for k in range(nz)]
    four_zero = jnp.zeros((4, LANES), f32)
    rho_x, left_x = left_chain(ports_x, xi, four_zero)
    back_x, right_x = right_chain(ports_x, xi + 1, four_zero + 1.0)
    rho_z, left_z = left_chain(ports_z, zi, rho_x)
    back_z, right_z = right_chain(ports_z, zi, back_x)

    for copy in rhs_y_copies:
        copy.wait_recv()
    rhs_in_y = [(rhs_y[k, 0:1, :], rhs_y[k, 1:2, :]) for k in range(ny)]
    wl = left_values(left_y, rhs_in_y, gy, row_zero)
    wr = right_values(right_y, rhs_in_y, gy, row_zero)
    state = meet(rho_y, back_y, wl, wr)
    starts = []
    for l in range(TILES):
        before = [pre_y[l, e] for e in range(4)]
        wide = tuple(jnp.broadcast_to(s, (8, LANES)) for s in state)
        moved = apply2(before, wide)
        starts.append((moved[0] + before_y[l][0], moved[1] + before_y[l][1]))
        if l < TILES - 1:
            moved = apply2([win_y[l, 12 + e] for e in range(4)], wide)
            state = tuple((moved[e] + totals_y[l][e])[7:8, :] for e in range(2))

    def finish_y(t, carry):
        for l in range(TILES):
            at = block(t)
            vt[l, pl.ds(t, 8, stride=PITCH), :] = (
                ay[l, at, :] * starts[l][0] + by[l, at, :] * starts[l][1] + cy[l, at, :]
            )
        return carry

    lax.fori_loop(0, STEPS, finish_y, 0, unroll=4)
    for l in range(TILES):
        line = [vt[l, PITCH * s : PITCH * s + STEPS, :] for s in range(8)]
        natural = jnp.concatenate(line, axis=0).T
        for t in range(STEPS):
            os_u[l, pl.ds(t, 8, stride=STEPS), :] = natural[8 * t : 8 * t + 8, :]
        v_out[:, cols[l]] = os_u[l]

    for l in range(TILES):
        for t in range(STEPS):
            os_v[l, pl.ds(t, 8, stride=STEPS), :] = os_n[t, :, cols[l]]
        corr_out[:, cols[l]] = os_v[l]

    own_l = left_values(left_z, rhs_in_z, zi, four_zero)
    own_r = right_values(right_z, rhs_in_z, zi, four_zero)
    gain_l = gain_r = four_zero + 1.0
    for k in range(nz):
        gain_l = jnp.where(k < zi, gain_l * left_z[k][0], gain_l)
        gain_r = jnp.where(k >= zi, gain_r * right_z[k][0], gain_r)
    for copy in rhs_x_copies:
        copy.wait_recv()
    rhs_in_x = [(rhs_x[k, 0:4, :], rhs_x[k, 4:8, :]) for k in range(nx)]
    wl = left_values(left_x, rhs_in_x, xi, four_zero)
    wr = right_values(right_x, rhs_in_x, xi + 1, four_zero)
    wl = own_l + gain_l * wl
    wr = own_r + gain_r * wr
    state = meet(rho_z, back_z, wl, wr)
    for l in range(TILES):
        before = [pre_x[l, e] for e in range(4)]
        wide = tuple(jnp.broadcast_to(s[l : l + 1, :], (8, LANES)) for s in state)
        moved = apply2(before, wide)
        u0, g0 = moved[0] + before_x[l][0], moved[1] + before_x[l][1]
        for t in range(STEPS):
            at = pl.ds(8 * t, 8)
            os_u[l, pl.ds(t, 8, stride=STEPS), :] = ax[l, at, :] * u0 + bx[l, at, :] * g0 + cx[l, at, :]
        u_out[:, cols[l]] = os_u[l]

    for copy in sent:
        copy.wait_send()


def predictor(sizes, spring, depth, momentum_x, momentum_y, bed, wet):
    nx, nz, ny = sizes
    rows, cols = depth.shape
    shape = (8, STEPS, cols)
    flat = jax.ShapeDtypeStruct((rows, cols), f32)
    hbm = pl.BlockSpec(memory_space=pl.ANY)
    tile = (TILES, 128, LANES)
    wide = (TILES, 8 * PITCH, LANES)
    far = 2 * (nz + nx + ny - 3)
    results = pl.pallas_call(
        functools.partial(kernel, sizes, spring),
        out_shape=(flat, flat, flat),
        in_specs=[hbm] * 5,
        out_specs=[pl.BlockSpec(memory_space=pltpu.VMEM)] * 3,
        scratch_shapes=[
            pltpu.VMEM((4, STEPS + 4, 8, cols), f32),
            pltpu.VMEM((STEPS + 4, 8, cols), jnp.int32),
            pltpu.VMEM(tile, f32),
            pltpu.VMEM(wide, f32),
            pltpu.VMEM(tile, f32),
            pltpu.VMEM(tile, f32),
            pltpu.VMEM(tile, f32),
            pltpu.VMEM(tile, f32),
            pltpu.VMEM(tile, f32),
            pltpu.VMEM(tile, f32),
            pltpu.VMEM((TILES, 16, 8, LANES), f32),
            pltpu.VMEM((TILES, 16, 8, LANES), f32),
            pltpu.VMEM((TILES, 4, 8, LANES), f32),
            pltpu.VMEM((TILES, 4, 8, LANES), f32),
            pltpu.VMEM((3, STEPS + 1, 8, cols), f32),
            pltpu.VMEM(tile, f32),
            pltpu.VMEM(wide, f32),
            pltpu.VMEM(wide, f32),
            pltpu.VMEM((STEPS, 8, cols), f32),
            pltpu.VMEM(tile, f32),
            pltpu.VMEM(tile, f32),
            pltpu.VMEM((3, STEPS, 8, cols), f32),
            pltpu.VMEM((128, LANES), f32),
            pltpu.VMEM((2, 40, LANES), f32),
            pltpu.VMEM((5, 24, LANES), f32),
            pltpu.VMEM((3, 128, LANES), f32),
            pltpu.VMEM((3, 128, LANES), f32),
            pltpu.VMEM((nz, 16, LANES), f32),
            pltpu.VMEM((nx, 16, LANES), f32),
            pltpu.VMEM((ny, 8, LANES), f32),
            pltpu.VMEM((nz, 8, LANES), f32),
            pltpu.VMEM((nx, 8, LANES), f32),
            pltpu.VMEM((ny, 8, LANES), f32),
            pltpu.VMEM((3, 8, LANES), f32),
            pltpu.SemaphoreType.DMA((40,)),
            pltpu.SemaphoreType.DMA((6,)),
            pltpu.SemaphoreType.DMA((6,)),
            pltpu.SemaphoreType.DMA((far,)),
            pltpu.SemaphoreType.DMA((far,)),
        ],
        compiler_params=pltpu.CompilerParams(collective_id=0, has_side_effects=True, vmem_limit_bytes=55_700_000),
    )(*(a.reshape(shape) for a in (depth, momentum_x, momentum_y, bed, wet)))
    corr, flux_u, flux_v = results
    return (depth - corr, flux_u / depth, flux_v / depth)


def solution(mesh):
    ngx, ny = mesh.shape["gx"], mesh.shape["gy"]
    nz = 8 if ngx % 8 == 0 else max(1, ngx // 2)
    sizes = (ngx // nz, nz, ny)
    scale = (4096 / 4.0) ** 2 / 3.0
    place = P("gx", "gy")
    return jax.shard_map(
        functools.partial(predictor, sizes, 1.0 / scale),
        mesh=mesh,
        in_specs=(place,) * 5,
        out_specs=(place,) * 3,
        check_vma=False,
    )
```
